32 devices in a mesh: slab: 4 (over y, x), brick: 8 (over z, core).
Axes of the slice: x: 2, y: 2, z: 4, core: 2. Of those that a mesh axis runs over, the one named last changes fastest.
Arguments:
- k_coeffs: float32 [8, 16, 16, 128], P('slab', 'brick'), may hold values from -0.3 to 0.4
- v_basis: float32 [32768, 128], P(('slab', 'brick')), may hold values from -4 to 4
Outputs:
- basis_x: float32 [8, 16, 16, 128], P('slab', 'brick')
- coupling: float32 [128, 128], replicated
- basis_v: float32 [32768, 128], P(('slab', 'brick'))
The draws below stay inside these ranges and needn't reach their ends.
All inputs are finite; a program needn't handle non-finite values.
Results may differ from the reference program's by a relative error of at most 0.0001.
Values sent between devices are 32-bit elements; how exact they have to be, the bound alone decides.
A program may use at most 64 MiB of HBM per device.

```python
import math
import jax
import jax.numpy as jnp
from jax import lax

R = 128
NVX = 32
NV = 32768
NZ = 16
NX = 8
NY = 16


VMAX = 6.0


def node_velocities(indices):
    spacing = 2.0 * VMAX / NVX
    first_index = indices // (NVX * NVX)
    second = indices // NVX % NVX
    third_index = indices % NVX
    coords = jnp.stack([first_index, second, third_index]).astype(jnp.float32)
    return -VMAX + (coords + 0.5) * spacing


def draw_v_basis(key, part):
    velocity = node_velocities(jnp.arange(NV, dtype=jnp.int32))
    square = jnp.sum(velocity * velocity, axis=0)
    gaussian = jnp.exp(-0.5 * square)
    smooth = jnp.stack([gaussian, velocity[0] * gaussian, velocity[1] * gaussian, velocity[2] * gaussian, (square - 3.0) * gaussian], axis=1)
    rough_part = jnp.clip(jax.random.normal(key, (NV, R - 5), jnp.float32), -4.0, 4.0) * jnp.exp(-0.25 * square)[:, None]
    columns = jnp.concatenate([smooth, rough_part], axis=1)
    weight_v = (2.0 * VMAX / NVX) ** 3
    identity = jnp.eye(R, dtype=jnp.float32)
    for sweep_index in range(2):
        gram_matrix = lax.dot_general(columns, columns, (((0,), (0,)), ((), ())), precision=lax.Precision.HIGHEST) * weight_v
        factor = jnp.linalg.cholesky(gram_matrix)
        inverse = jax.scipy.linalg.solve_triangular(factor, identity, lower=True)
        columns = jnp.dot(columns, inverse.T, precision=lax.Precision.HIGHEST)
    return columns.astype(jnp.float32)


def draw_k_coeffs(key, part):
    subkeys = jax.random.split(key, 3)
    rough_part = jnp.clip(jax.random.normal(subkeys[0], (NX, NY, NZ, R), jnp.float32), -5.0, 5.0) * 0.05
    density = jnp.exp(jax.random.uniform(subkeys[1], (NX, NY, NZ), jnp.float32, math.log(0.03), math.log(0.3)))
    row_scale = jnp.concatenate([jnp.zeros((1,), jnp.float32), jnp.full((4,), 0.6, jnp.float32), jnp.ones((R - 5,), jnp.float32)])
    return (rough_part * row_scale).at[..., 0].set(density).astype(jnp.float32)


def setup_inputs(seed: int = 0) -> dict:
    arg_keys = jax.random.split(jax.random.key(seed), 3)
    return {
        "k_coeffs": draw_k_coeffs(jax.random.fold_in(arg_keys[2], 71), 0),
        "v_basis": draw_v_basis(jax.random.fold_in(arg_keys[2], 71), 0),
    }


CFL = 0.9
VMAX = 6.0
COLLIDE = 0.3
RHO_MIN = 0.25
TEMP_MIN = 0.25
PRECISE = lax.Precision.HIGHEST

def velocities(indices):
    spacing = 2.0 * VMAX / NVX
    first_index = indices // (NVX * NVX)
    second = indices // NVX % NVX
    third_index = indices % NVX
    coords = jnp.stack([first_index, second, third_index]).astype(jnp.float32)
    return -VMAX + (coords + 0.5) * spacing

def maxwell(cell_params, velocity):
    distance = (velocity[0][None, :] - cell_params[1][:, None]) ** 2
    distance = distance + (velocity[1][None, :] - cell_params[2][:, None]) ** 2
    distance = distance + (velocity[2][None, :] - cell_params[3][:, None]) ** 2
    amplitude = cell_params[0] * (2.0 * math.pi * cell_params[4]) ** (-1.5)
    return amplitude[:, None] * jnp.exp(distance * (-0.5 / cell_params[4])[:, None])

def cell_state(vectors, coeffs):
    moments = lax.dot_general(vectors, coeffs, (((1,), (1,)), ((), ())), precision=PRECISE)
    density = jnp.maximum(moments[0], RHO_MIN)
    drift_speed = moments[1:4] / density[None, :]
    temper = jnp.maximum((moments[4] / density - jnp.sum(drift_speed * drift_speed, axis=0)) / 3.0, TEMP_MIN)
    return jnp.concatenate([density[None], drift_speed, temper[None]], axis=0)

def transport_flux(backward, forward, transport):
    flux = jnp.zeros_like(backward[0])
    for axis_id in range(3):
        flux = flux + jnp.dot(backward[axis_id], transport[axis_id], precision=PRECISE)
        flux = flux + jnp.dot(forward[axis_id], transport[3 + axis_id], precision=PRECISE)
    return flux

def products(left_side, backward, forward, maxwell_proj):
    pieces = [lax.dot_general(left_side, item, (((0,), (0,)), ((), ())), precision=PRECISE) for item in backward + forward + [maxwell_proj]]
    return jnp.stack(pieces)

def coupling_step(coupling_hat, minus_side, plus_side, projected, transport, time_step):
    drift_sum = jnp.zeros_like(coupling_hat)
    for axis_id in range(3):
        drift_sum = drift_sum + jnp.dot(jnp.dot(minus_side[axis_id], coupling_hat, precision=PRECISE), transport[axis_id], precision=PRECISE)
        drift_sum = drift_sum + jnp.dot(jnp.dot(plus_side[axis_id], coupling_hat, precision=PRECISE), transport[3 + axis_id], precision=PRECISE)
    return coupling_hat + time_step * drift_sum - COLLIDE * (projected - coupling_hat)

def velocity_step(velocity_part, minus_side, plus_side, back_proj, positive, negative, time_step):
    drift_sum = jnp.zeros_like(velocity_part)
    for axis_id in range(3):
        drift_sum = drift_sum + positive[axis_id][:, None] * jnp.dot(velocity_part, minus_side[axis_id].T, precision=PRECISE)
        drift_sum = drift_sum + negative[axis_id][:, None] * jnp.dot(velocity_part, plus_side[axis_id].T, precision=PRECISE)
    return velocity_part - time_step * drift_sum + COLLIDE * (back_proj - velocity_part)

def slopes(field):
    rank_size = field.shape[3]
    lengths = (NX, NY, NZ)
    backward = [((field - jnp.roll(field, 1, axis=axis_id)) * lengths[axis_id]).reshape(-1, rank_size) for axis_id in range(3)]
    forward = [((jnp.roll(field, -1, axis=axis_id) - field) * lengths[axis_id]).reshape(-1, rank_size) for axis_id in range(3)]
    return (backward, forward)

def reference(k_coeffs, v_basis):
    rank_size = k_coeffs.shape[3]
    cell_count = NX * NY * NZ
    time_step = CFL / (VMAX * (NX + NY + NZ))
    weight_x = 1.0 / cell_count
    weight_v = (2.0 * VMAX / NVX) ** 3
    velocity = velocities(jnp.arange(NV, dtype=jnp.int32))
    positive = jnp.maximum(velocity, 0.0)
    negative = jnp.minimum(velocity, 0.0)
    weights = jnp.stack([jnp.ones_like(velocity[0]), velocity[0], velocity[1], velocity[2], jnp.sum(velocity * velocity, axis=0)])
    vectors = jnp.dot(weights, v_basis, precision=PRECISE) * weight_v
    transport = jnp.stack([lax.dot_general(v_basis * (side[axis_id] * weight_v)[:, None], v_basis, (((0,), (0,)), ((), ())), precision=PRECISE) for side in (positive, negative) for axis_id in range(3)])
    coeff_flat = k_coeffs.reshape(cell_count, rank_size)
    cell_params = cell_state(vectors, coeff_flat)
    block_rows = math.gcd(NV, 2048)
    block_total = NV // block_rows
    vel_blocks = velocity.reshape(3, block_total, block_rows).transpose(1, 0, 2)
    basis_blocks = v_basis.reshape(block_total, block_rows, rank_size)

    def add_block(accumulated, pair):
        return (accumulated + jnp.dot(maxwell(cell_params, pair[0]), pair[1], precision=PRECISE) * weight_v, None)
    maxwell_proj = lax.scan(add_block, jnp.zeros((cell_count, rank_size), jnp.float32), (vel_blocks, basis_blocks))[0]
    backward, forward = slopes(k_coeffs)
    advanced = coeff_flat - time_step * transport_flux(backward, forward, transport) + COLLIDE * (maxwell_proj - coeff_flat)
    gram_matrix = lax.dot_general(advanced, advanced, (((0,), (0,)), ((), ())), precision=PRECISE) * weight_x
    factor = jnp.linalg.cholesky(gram_matrix)
    identity = jnp.eye(rank_size, dtype=jnp.float32)
    inverse = jax.scipy.linalg.solve_triangular(factor, identity, lower=True)
    basis_new = jnp.dot(advanced, inverse.T, precision=PRECISE)
    backward, forward = slopes(basis_new.reshape(NX, NY, NZ, rank_size))
    reduced = products(basis_new, backward, forward, maxwell_proj) * weight_x
    coupling_mid = coupling_step(factor.T, reduced[0:3], reduced[3:6], reduced[6], transport, time_step)

    def back_block(vblock):
        return lax.dot_general(maxwell(cell_params, vblock), basis_new, (((0,), (0,)), ((), ())), precision=PRECISE) * weight_x
    back_proj = lax.map(back_block, vel_blocks).reshape(NV, rank_size)
    velocity_part = jnp.dot(v_basis, coupling_mid.T, precision=PRECISE)
    velocity_new = velocity_step(velocity_part, reduced[0:3], reduced[3:6], back_proj, positive, negative, time_step)
    gram_v = lax.dot_general(velocity_new, velocity_new, (((0,), (0,)), ((), ())), precision=PRECISE) * weight_v
    coupling = jnp.linalg.cholesky(gram_v)
    inverse_v = jax.scipy.linalg.solve_triangular(coupling, identity, lower=True)
    vbasis_new = jnp.dot(velocity_new, inverse_v.T, precision=PRECISE)
    return (basis_new.reshape(NX, NY, NZ, rank_size), coupling, vbasis_new)
```

```python
import functools
import math

import jax
import jax.numpy as jnp
from jax import lax
from jax.experimental import pallas as pl
from jax.experimental.pallas import tpu as pltpu
from jax.sharding import PartitionSpec as P

NVX = 32

CFL = 0.9
VMAX = 6.0
COLLIDE = 0.3
RHO_MIN = 0.25
TEMP_MIN = 0.25
PRECISE = lax.Precision.HIGHEST
MESH = pl.DeviceIdType.MESH
VM = pl.BlockSpec(memory_space=pltpu.VMEM)
F32 = jnp.float32
BF16 = jnp.bfloat16
BITS = NVX.bit_length() - 1


def halves(values):
    high = values.astype(BF16)
    return high, (values - high.astype(F32)).astype(BF16)


def dot(left, right):
    return jnp.dot(left, right, preferred_element_type=F32)


def dot_split(high, low, right):
    width = right.shape[1]
    right_high, right_low = halves(right)
    both = dot(high, jnp.concatenate([right_high, right_low], axis=1))
    return both[:, :width] + (both[:, width:] + dot(low, right_high))


def dot3(left, right):
    return dot_split(*halves(left), right)


def dot6(left, right):
    return jnp.dot(left, right, precision=PRECISE, preferred_element_type=F32)


def node_velocity(indices):
    spacing = 2.0 * VMAX / NVX
    last = NVX - 1
    parts = (
        lax.shift_right_logical(indices, 2 * BITS),
        lax.shift_right_logical(indices, BITS) & last,
        indices & last,
    )
    return [-VMAX + (part.astype(F32) + 0.5) * spacing for part in parts]


class Sum:
    def __init__(self, send, pos, x, first, second, out, sems):
        self.send, self.pos = send, pos
        self.x, self.first, self.second, self.out = x, first, second, out
        self.sems = sems

    def scatter(self):
        me, members, member = self.pos.me, self.pos.members, self.pos.member
        self.copies = []
        for k in range(1, members):
            to, device = member(k)
            self.copies.append(
                self.send(
                    self.x.at[to], self.first.at[k - 1], self.sems[0].at[k - 1], self.sems[1].at[k - 1], device
                )
            )

    def cross(self):
        me, layer = self.pos.me, self.pos.layer
        total = self.x[me]
        for k, copy in enumerate(self.copies):
            copy.wait_recv()
            total = total + self.first[k]
        self.second[layer] = total
        mine = self.second.at[layer]
        self.copies = [
            self.send(mine, mine, self.sems[2].at[k - 1], self.sems[3].at[k - 1], self.pos.across(k))
            for k in range(1, self.pos.layers)
        ]

    def collect(self):
        me = self.pos.me
        for copy in self.copies:
            copy.wait_recv()
        total = self.second[0]
        for k in range(1, self.pos.layers):
            total = total + self.second[k]
        self.out[me] = total
        mine = self.out.at[me]
        self.copies = [
            self.send(mine, mine, self.sems[4].at[k - 1], self.sems[5].at[k - 1], self.pos.member(k)[1])
            for k in range(1, self.pos.members)
        ]

    def finish(self):
        for copy in self.copies:
            copy.wait_recv()


class Position:
    def __init__(self, slabs, layers):
        self.slabs, self.layers, self.members = slabs, layers, 2 * slabs
        brick = lax.axis_index("brick")
        self.brick = brick
        self.core, self.layer = lax.rem(brick, 2), lax.div(brick, 2)
        self.slab = lax.axis_index("slab")
        self.me = 2 * self.slab + self.core

    def member(self, k):
        to = lax.rem(self.me + k, self.members)
        return to, (lax.div(to, 2), 2 * self.layer + lax.rem(to, 2))

    def across(self, k):
        return (self.slab, 2 * lax.rem(self.layer + k, self.layers) + self.core)

    def partner(self):
        return (self.slab, 2 * self.layer + 1 - self.core)

    def slab_at(self, k):
        to = lax.rem(self.slab + k, self.slabs)
        return to, (to, self.brick)

    def brick_at(self, k):
        bricks = 2 * self.layers
        return (self.slab, lax.rem(self.brick + k + bricks, bricks))


def factor_steps(work, matrix):
    size = matrix.shape[0]
    panel = 8
    row = lax.broadcasted_iota(jnp.int32, (size, size), 0)
    column = lax.broadcasted_iota(jnp.int32, (size, size), 1)
    work[:, :size] = matrix
    work[:, size:] = jnp.where(row == column, 1.0, 0.0)
    sub_one = lax.broadcasted_iota(jnp.int32, (panel, size), 0)
    for start in range(0, size, panel):
        rows = work[start : start + panel, :]
        columns = [
            jnp.broadcast_to(rows[:, start + k : start + k + 1], (panel, size))
            for k in range(panel)
        ]
        for k in range(panel):
            scale = lax.rsqrt(columns[k][k : k + 1, :])
            ratio = columns[k] * (scale * scale)
            ratio = jnp.where(sub_one > k, ratio, jnp.where(sub_one == k, 1.0 - scale, 0.0))
            for m in range(k + 1, panel):
                columns[m] = columns[m] - ratio * columns[m][k : k + 1, :]
            rows = rows - jnp.concatenate([ratio, ratio], axis=1) * rows[k : k + 1, :]
        work[start : start + panel, :] = rows
        if start + panel < size:
            tall = rows[:, :size].T[start + panel :, :]
            work[start + panel :, :] = work[start + panel :, :] - jnp.dot(
                tall, rows, precision=PRECISE, preferred_element_type=F32
            )
    factor = jnp.where(column <= row, work[:, :size].T, 0.0)
    inverse = jnp.where(column <= row, work[:, size:], 0.0)
    return factor, inverse


def step_kernel(names, slabs, layers, *refs):
    ref = dict(zip(names, refs))
    pos = Position(slabs, layers)
    core, slab, layer, brick, me = pos.core, pos.slab, pos.layer, pos.brick, pos.me
    members, bricks = pos.members, 2 * layers
    k_ref, v_ref = ref["k"], ref["v"]
    cells_x, cells_y, cells_z, rank = k_ref.shape
    own = cells_x * cells_y * cells_z
    nodes = v_ref.shape[0]
    lengths = (cells_x * slabs, cells_y * bricks, cells_z)
    cells = lengths[0] * lengths[1] * lengths[2]
    time_step = CFL / (VMAX * (lengths[0] + lengths[1] + lengths[2]))
    weight_x = 1.0 / cells
    weight_v = (2.0 * VMAX / NVX) ** 3
    base = (slab * bricks + brick) * nodes
    started = []

    def send(source, target, send_sem, recv_sem, device):
        copy = pltpu.make_async_remote_copy(
            src_ref=source,
            dst_ref=target,
            send_sem=send_sem,
            recv_sem=recv_sem,
            device_id=device,
            device_id_type=MESH,
        )
        copy.start()
        started.append(copy)
        return copy

    barrier = pltpu.get_barrier_semaphore()
    peers = [pos.member(k)[1] for k in range(1, members)]
    peers += [pos.across(k) for k in range(1, layers)]
    peers += [pos.brick_at(1), pos.brick_at(-1)]
    for peer in peers:
        pl.semaphore_signal(barrier, inc=1, device_id=peer, device_id_type=MESH)

    lane = lax.broadcasted_iota(jnp.int32, (8, nodes), 1)
    sub = lax.broadcasted_iota(jnp.int32, (8, nodes), 0)
    velocity = node_velocity(base + lane)
    square = velocity[0] * velocity[0] + velocity[1] * velocity[1] + velocity[2] * velocity[2]
    weights = jnp.where(sub == 0, 1.0, jnp.where(sub == 4, square, 0.0))
    upward = jnp.zeros_like(weights)
    for d in range(3):
        weights = jnp.where(sub == d + 1, velocity[d], weights)
        upward = jnp.where(sub == d + 5, jnp.maximum(velocity[d], 0.0), upward)
    values = v_ref[...]
    v_high, v_low = halves(values)
    v_rest = (values - v_high.astype(F32) - v_low.astype(F32)).astype(BF16)
    sums = dot(jnp.concatenate(halves(weights), axis=0), jnp.concatenate([v_high, v_low, v_rest], axis=1))
    sums = sums[:8] + sums[8:]
    squares = dot(upward.astype(BF16), jnp.concatenate(halves(values * values), axis=1))
    partial = sums[:, :rank] + (sums[:, rank : 2 * rank] + sums[:, 2 * rank :])
    partial = (partial + (squares[:, :rank] + squares[:, rank:])) * weight_v
    vec_l, vec_m = ref["vec_l"], ref["vec_m"]
    vec_l[layer] = partial

    pl.semaphore_wait(barrier, len(peers))
    mine = vec_l.at[layer]
    copies = [
        send(mine, mine, ref["vls"].at[k - 1], ref["vlr"].at[k - 1], pos.across(k)) for k in range(1, layers)
    ]
    halo_a, halo_b = ref["halo_a"], ref["halo_b"]
    halos = [
        send(k_ref.at[cells_x - 1], halo_a.at[0], ref["hs"].at[0], ref["hr"].at[0], pos.slab_at(1)[1]),
        send(k_ref.at[0], halo_a.at[1], ref["hs"].at[1], ref["hr"].at[1], pos.slab_at(slabs - 1)[1]),
        send(k_ref.at[:, cells_y - 1], halo_b.at[0], ref["hs"].at[2], ref["hr"].at[2], pos.brick_at(1)),
        send(k_ref.at[:, 0], halo_b.at[1], ref["hs"].at[3], ref["hr"].at[3], pos.brick_at(-1)),
    ]

    turned_v = values.T
    vt_high, vt_low = halves(turned_v)
    vt = ref["vt"]
    vt[:rank] = vt_high
    vt[rank:] = vt_low
    v_both = jnp.concatenate([v_high, v_low], axis=1)
    row = lax.broadcasted_iota(jnp.int32, (rank, rank), 0)
    column = lax.broadcasted_iota(jnp.int32, (rank, rank), 1)
    packed = []
    for d in range(3):
        sides = []
        for side in (jnp.maximum(velocity[d][:1], 0.0), jnp.minimum(velocity[d][:1], 0.0)):
            high, low = halves(turned_v * (side * weight_v))
            both = dot(high, v_both)
            sides.append(both[:, :rank] + (both[:, rank:] + dot(low, v_high)))
        packed.append(jnp.where(row > column, sides[0], sides[1]))
    share = 3 * rank // members
    ref["tx"][...] = jnp.concatenate(packed, axis=0).reshape(members, share, rank)
    transport_sum = Sum(send, pos, ref["tx"], ref["t1"], ref["t2"], ref["to"], [ref[f"tsem{i}"] for i in range(6)])

    for copy in copies:
        copy.wait_recv()
    total = vec_l[0]
    for k in range(1, layers):
        total = total + vec_l[k]
    vec_m[me] = total
    mine = vec_m.at[me]
    copies = [
        send(mine, mine, ref["vms"].at[k - 1], ref["vmr"].at[k - 1], pos.member(k)[1]) for k in range(1, members)
    ]
    transport_sum.scatter()
    own_k = k_ref[...].reshape(own, rank)
    kpad = ref["kpad"]
    kpad[...] = jnp.zeros_like(kpad)
    kpad[pl.ds(pl.multiple_of(core * own, 8), own), :] = own_k
    for copy in copies:
        copy.wait_recv()
    vectors = vec_m[0]
    for k in range(1, members):
        vectors = vectors + vec_m[k]

    moments = lax.dot_general(
        vectors, kpad[...], (((1,), (1,)), ((), ())), precision=PRECISE, preferred_element_type=F32
    )
    pair = 2 * own
    density = jnp.maximum(moments[0:1], RHO_MIN)
    drift = [moments[d : d + 1] / density for d in range(1, 4)]
    bulk = drift[0] * drift[0] + drift[1] * drift[1] + drift[2] * drift[2]
    temper = jnp.maximum((moments[4:5] / density - bulk) / 3.0, TEMP_MIN)
    wide = 2.0 * math.pi * temper
    amplitude = density / (wide * jnp.sqrt(wide))
    state = jnp.zeros((8, pair), F32)
    sub_pair = lax.broadcasted_iota(jnp.int32, (8, pair), 0)
    lane_pair = lax.broadcasted_iota(jnp.int32, (8, pair), 1)
    for i, item in enumerate(drift + [-0.5 / temper, amplitude]):
        state = jnp.where(sub_pair == i, item, state)
    inside = (lane_pair >= core * own) & (lane_pair < (core + 1) * own)
    par = ref["par"]
    par[me, layer] = jnp.where(inside, state, 0.0)
    mine = par.at[me, layer]
    copies = [
        send(mine, mine, ref["pls"].at[k - 1], ref["plr"].at[k - 1], pos.across(k)) for k in range(1, layers)
    ]
    transport_sum.cross()
    for copy in copies:
        copy.wait_recv()
    mine = par.at[me]
    copies = [
        send(mine, mine, ref["pms"].at[k - 1], ref["pmr"].at[k - 1], pos.member(k)[1]) for k in range(1, members)
    ]
    transport_sum.collect()
    for copy in copies:
        copy.wait_recv()

    mt_high, mt_low = ref["mt_high"], ref["mt_low"]
    mp, first, half, second, third = ref["mp"], ref["first"], ref["half"], ref["second"], ref["third"]
    group = math.gcd(nodes, NVX)
    groups = nodes // group
    width = 2 * pair
    slots = layers // 2
    fast_v = node_velocity(base + lax.broadcasted_iota(jnp.int32, (group, width), 0))
    slow_v = node_velocity(base + group * lax.broadcasted_iota(jnp.int32, (groups, width), 0))

    def project(to, slot):
        blocks = [par[2 * to, 2 * slot + i] + par[2 * to + 1, 2 * slot + i] for i in range(2)]
        state = jnp.concatenate(blocks, axis=1)
        u = [state[d : d + 1] for d in range(3)]
        rate, scale = state[3:4], state[4:5]
        fast = jnp.exp((fast_v[2] - u[2]) ** 2 * rate)
        slow = jnp.exp(((slow_v[0] - u[0]) ** 2 + (slow_v[1] - u[1]) ** 2) * rate) * scale
        place = pl.ds(pl.multiple_of((to * slots + slot) * width, width), width)
        for t in range(groups):
            high, low = halves(fast * slow[t : t + 1])
            mt_high[t * group : (t + 1) * group, place] = high
            mt_low[t * group : (t + 1) * group, place] = low
        high = dot(vt[...], mt_high[:, place])
        low = dot(vt[:rank], mt_low[:, place])
        result = ((high[:rank] + (high[rank:] + low)) * weight_v).T
        for i in range(2):
            for c in range(2):
                at = (2 * i + c) * own
                mp[to, 2 * slot + i, c] = result[at : at + own]

    def hand_over(k, slot, to):
        at = pl.ds(2 * slot, 2)
        return send(
            mp.at[to, at, 1 - core], first.at[to, at], ref["cs"].at[k, slot], ref["cr"].at[k, slot], pos.partner()
        )

    over = []

    def hand_on(k, slot, to, copy):
        copy.wait_recv()
        at = pl.ds(2 * slot, 2)
        if k == 0:
            second[slab, at] = mp[slab, at, core] + first[slab, at]
            return
        half[to, at] = mp[to, at, core] + first[to, at]
        over.append(
            send(half.at[to, at], second.at[slab, at], ref["ss"].at[k - 1, slot], ref["sr"].at[k - 1, slot], (to, brick))
        )

    waiting = []
    for k in list(range(1, slabs)) + [0]:
        to = lax.rem(slab + k, slabs)
        for slot in range(slots):
            project(to, slot)
            copy = hand_over(k, slot, to)
            if len(waiting) >= 1:
                hand_on(*waiting.pop(0))
            waiting.append((k, slot, to, copy))

    transport_sum.finish()
    packed = ref["to"][...].reshape(3 * rank, rank)
    trans = ref["trans"]
    for d in range(3):
        block = packed[d * rank : (d + 1) * rank]
        flipped = block.T
        diagonal = jnp.where(row == column, vectors[d + 5 : d + 6], 0.0)
        trans[d * rank : (d + 1) * rank] = jnp.where(row <= column, block, flipped)
        trans[(d + 3) * rank : (d + 4) * rank] = jnp.where(
            row > column, block, jnp.where(row < column, flipped, diagonal)
        )
    for copy in waiting:
        hand_on(*copy)
    for copy in halos:
        copy.wait_recv()
    field = k_ref[...]
    after_a = jnp.concatenate([field[1:], halo_a[1:2]], axis=0)
    before_a = jnp.concatenate([halo_a[0:1], field[:-1]], axis=0)
    after_b = jnp.concatenate([field[:, 1:], halo_b[1].reshape(cells_x, 1, cells_z, rank)], axis=1)
    before_b = jnp.concatenate([halo_b[0].reshape(cells_x, 1, cells_z, rank), field[:, :-1]], axis=1)

    def next_third(flat):
        count = flat.shape[0]
        index = lax.broadcasted_iota(jnp.int32, flat.shape, 0)
        return jnp.where(
            lax.rem(index, cells_z) == cells_z - 1,
            pltpu.roll(flat, cells_z - 1, 0),
            pltpu.roll(flat, count - 1, 0),
        )

    def last_third(flat):
        count = flat.shape[0]
        index = lax.broadcasted_iota(jnp.int32, flat.shape, 0)
        return jnp.where(
            lax.rem(index, cells_z) == 0,
            pltpu.roll(flat, count - cells_z + 1, 0),
            pltpu.roll(flat, 1, 0),
        )

    fields = [
        (after_a.reshape(own, rank) - own_k) * lengths[0],
        (after_b.reshape(own, rank) - own_k) * lengths[1],
        (next_third(own_k) - own_k) * lengths[2],
        (own_k - before_a.reshape(own, rank)) * lengths[0],
        (own_k - before_b.reshape(own, rank)) * lengths[1],
        (own_k - last_third(own_k)) * lengths[2],
    ]
    flux = dot3(jnp.concatenate(fields, axis=1), trans[...])
    kept = own_k - time_step * flux - COLLIDE * own_k

    for copy in over:
        copy.wait_recv()
    total = second[0]
    for k in range(1, slabs):
        total = total + second[k]
    quarter = ref["quarter"]
    quarter[...] = total
    copies = []
    for k in range(1, layers):
        to = lax.rem(layer + k, layers)
        copies.append(
            send(quarter.at[to], third.at[layer], ref["zs"].at[k - 1], ref["zr"].at[k - 1], pos.across(k))
        )
    third[layer] = quarter[layer]
    for copy in copies:
        copy.wait_recv()
    mproj = third[0]
    for k in range(1, layers):
        mproj = mproj + third[k]
    advanced = kept + COLLIDE * mproj

    adv = ref["adv"]
    adv[slab, brick] = advanced.reshape(cells_x, cells_y, cells_z, rank)
    here = adv.at[slab, brick]

    def to_slabs(block, j):
        return [
            send(block, block, ref["bs"].at[k - 1, j], ref["br"].at[k - 1, j], pos.slab_at(k)[1])
            for k in range(1, slabs)
        ]

    along = [
        send(here, here, ref["as"].at[k - 1], ref["ar"].at[k - 1], pos.across(k)) for k in range(1, layers)
    ]
    crossing = [to_slabs(here, 0)]
    last = [send(here, here, ref["ds"].at[0, 0], ref["dr"].at[0, 0], pos.partner())]
    raw_sum = Sum(send, pos, ref["rx"], ref["r1"], ref["r2"], ref["ro"], [ref[f"rsem{i}"] for i in range(6)])
    ref["rx"][...] = dot3(advanced.T, mproj).reshape(members, rank // members, rank)
    for j in range(1, layers):
        along[j - 1].wait_recv()
        block = adv.at[slab, 2 * lax.rem(layer + layers - j, layers) + core]
        crossing.append(to_slabs(block, j))
        last.append(send(block, block, ref["ds"].at[0, j], ref["dr"].at[0, j], pos.partner()))
    raw_sum.scatter()
    for j in range(layers):
        for k in range(1, slabs):
            crossing[j][k - 1].wait_recv()
            block = adv.at[lax.rem(slab + slabs - k, slabs), 2 * lax.rem(layer + layers - j, layers) + core]
            last.append(send(block, block, ref["ds"].at[k, j], ref["dr"].at[k, j], pos.partner()))
    raw_sum.cross()
    for copy in last:
        copy.wait_recv()
    raw_sum.collect()

    at, ahl = ref["at"], ref["ahl"]
    d_high, d_low = ref["d_high"], ref["d_low"]
    plane = cells // slabs
    for s in range(slabs):
        block = adv[s]
        flat = block.reshape(plane, rank)
        span = slice(s * plane, (s + 1) * plane)
        high, low = halves(flat)
        ahl[span, :rank] = high
        ahl[span, rank:] = low
        high, low = halves(flat.T)
        at[:rank, span] = high
        at[rank:, span] = low
        following = adv[(s + 1) % slabs]
        up_a = jnp.concatenate([block[:, 1:], following[:, :1]], axis=1)
        wrapped = jnp.concatenate([block[1:, :, :1], block[:1, :, :1]], axis=0)
        up_b = jnp.concatenate([block[:, :, 1:], wrapped], axis=2)
        ups = [up_a.reshape(plane, rank), up_b.reshape(plane, rank), next_third(flat)]
        for d in range(3):
            high, low = halves(ups[d] - flat)
            d_high[span, d * rank : (d + 1) * rank] = high
            d_low[span, d * rank : (d + 1) * rank] = low
    both = dot(at[:rank], ahl[...])
    mixed = both[:, rank:]
    gram = (both[:, :rank] + (mixed + mixed.T)) * weight_x
    factor, inverse = factor_steps(ref["work"], gram)

    both = dot(at[...], d_high[...])
    slopes = both[:rank] + (both[rank:] + dot(at[:rank], d_low[...]))
    slopes = [slopes[:, d * rank : (d + 1) * rank] * (lengths[d] * weight_x) for d in range(3)]
    raw_sum.finish()
    raw = ref["ro"][...].reshape(rank, rank) * weight_x
    source = time_step * dot6(
        jnp.concatenate(slopes + [-item.T for item in slopes], axis=1), trans[...]
    ) - COLLIDE * raw

    place = 2 * own
    scaled = ahl[...]
    top = dot(mt_high[...], scaled)
    low = dot(mt_low[...], ahl[:, :rank])
    back_raw = (top[:, :rank] + (top[:, rank:] + low)) * weight_x

    turned = inverse.T
    middle = (1.0 + COLLIDE) * factor + dot6(source.T, turned)
    moved = dot6(inverse, jnp.concatenate(slopes, axis=1))
    plus = dot6(jnp.concatenate([moved[:, d * rank : (d + 1) * rank] for d in range(3)], axis=0), turned)
    plus = [plus[d * rank : (d + 1) * rank] for d in range(3)]
    sides = jnp.concatenate(plus + [item.T for item in plus], axis=1)
    lnew = ref["lnew"]
    chunk = math.gcd(nodes, 256)
    for at_row in range(0, nodes, chunk):
        span = slice(at_row, at_row + chunk)
        lnow = dot3(v_ref[span, :], middle)
        sliding = dot3(lnow, sides)
        part = node_velocity(base + at_row + lax.broadcasted_iota(jnp.int32, (chunk, rank), 0))
        slide = jnp.zeros((chunk, rank), F32)
        for d in range(3):
            slide = slide + jnp.maximum(part[d], 0.0) * sliding[:, d * rank : (d + 1) * rank]
            slide = slide - jnp.minimum(part[d], 0.0) * sliding[:, (d + 3) * rank : (d + 4) * rank]
        mback = dot3(back_raw[span], turned)
        lnew[span, :] = lnow + time_step * slide + COLLIDE * (mback - lnow)

    new = lnew[...]
    high, low = halves(new)
    rest = (new - high.astype(F32) - low.astype(F32)).astype(BF16)
    new_t = new.T
    high_t, low_t = halves(new_t)
    both = dot(high_t, jnp.concatenate([high, low, rest], axis=1))
    mixed = both[:, rank : 2 * rank] + (both[:, 2 * rank :] + 0.5 * dot(low_t, low))
    gram_v = (both[:, :rank] + (mixed + mixed.T)) * weight_v
    ref["gx"][...] = gram_v.reshape(members, rank // members, rank)
    gram_sum = Sum(send, pos, ref["gx"], ref["g1"], ref["g2"], ref["go"], [ref[f"gsem{i}"] for i in range(6)])
    gram_sum.scatter()
    ref["basis_x"][...] = dot3(advanced, turned).reshape(cells_x, cells_y, cells_z, rank)
    gram_sum.cross()
    gram_sum.collect()
    gram_sum.finish()
    coupling, inverse_v = factor_steps(ref["work"], ref["go"][...].reshape(rank, rank))
    ref["coupling"][...] = coupling
    ref["basis_v"][...] = dot3(lnew[...], inverse_v.T)
    for copy in started:
        copy.wait_send()


def local(k_coeffs, v_basis):
    cells_x, cells_y, cells_z, rank = k_coeffs.shape
    slabs = lax.axis_size("slab")
    layers = lax.axis_size("brick") // 2
    members = 2 * slabs
    own = cells_x * cells_y * cells_z
    nodes = v_basis.shape[0]
    cells = own * members * layers
    share = 3 * rank // members
    part = rank // members
    pair = 2 * own
    names = ["k", "v", "basis_x", "coupling", "basis_v"]
    scratch = []

    def buffer(name, shape, dtype=F32):
        names.append(name)
        scratch.append(pltpu.VMEM(shape, dtype))

    def semaphores(name, *shape):
        names.append(name)
        scratch.append(pltpu.SemaphoreType.DMA(shape))

    def reduction(name, rows):
        buffer(name + "x", (members, rows, rank))
        buffer(name + "1", (members - 1, rows, rank))
        buffer(name + "2", (layers, rows, rank))
        buffer(name + "o", (members, rows, rank))
        for i, count in enumerate([members, members, layers, layers, members, members]):
            semaphores(name + "sem" + str(i), count - 1)

    buffer("vec_l", (layers, 8, rank))
    buffer("vec_m", (members, 8, rank))
    buffer("halo_a", (2, cells_y, cells_z, rank))
    buffer("halo_b", (2, cells_x, cells_z, rank))
    buffer("vt", (2 * rank, nodes), BF16)
    buffer("kpad", (pair, rank))
    buffer("par", (members, layers, 8, pair))
    buffer("mt_high", (nodes, cells), BF16)
    buffer("mt_low", (nodes, cells), BF16)
    buffer("mp", (slabs, layers, 2, own, rank))
    buffer("first", (slabs, layers, own, rank))
    buffer("half", (slabs, layers, own, rank))
    buffer("second", (slabs, layers, own, rank))
    buffer("quarter", (layers, own, rank))
    buffer("third", (layers, own, rank))
    buffer("trans", (6 * rank, rank))
    buffer("adv", (slabs, 2 * layers, cells_x, cells_y, cells_z, rank))
    buffer("at", (2 * rank, cells), BF16)
    buffer("ahl", (cells, 2 * rank), BF16)
    buffer("d_high", (cells, 3 * rank), BF16)
    buffer("d_low", (cells, 3 * rank), BF16)
    buffer("work", (rank, 2 * rank))
    buffer("lnew", (nodes, rank))
    reduction("t", share)
    reduction("r", part)
    reduction("g", part)
    for name in ("vl", "pl", "z", "a"):
        semaphores(name + "s", layers - 1)
        semaphores(name + "r", layers - 1)
    for name in ("vm", "pm"):
        semaphores(name + "s", members - 1)
        semaphores(name + "r", members - 1)
    semaphores("hs", 4)
    semaphores("hr", 4)
    for name, shape in (
        ("c", (slabs, layers // 2)),
        ("s", (slabs - 1, layers // 2)),
        ("b", (slabs - 1, layers)),
        ("d", (slabs, layers)),
    ):
        semaphores(name + "s", *shape)
        semaphores(name + "r", *shape)
    return pl.pallas_call(
        functools.partial(step_kernel, tuple(names), slabs, layers),
        out_shape=(
            jax.ShapeDtypeStruct(k_coeffs.shape, F32),
            jax.ShapeDtypeStruct((rank, rank), F32),
            jax.ShapeDtypeStruct(v_basis.shape, F32),
        ),
        in_specs=[VM, VM],
        out_specs=(VM, VM, VM),
        scratch_shapes=scratch,
        compiler_params=pltpu.CompilerParams(
            collective_id=1, has_side_effects=True, vmem_limit_bytes=60 * 2**20
        ),
    )(k_coeffs, v_basis)


def solution(mesh):
    return jax.shard_map(
        local,
        mesh=mesh,
        in_specs=(P("slab", "brick", None, None), P(("slab", "brick"), None)),
        out_specs=(P("slab", "brick", None, None), P(), P(("slab", "brick"), None)),
        check_vma=False,
    )
```

```python
import functools
import math

import jax
import jax.numpy as jnp
from jax import lax
from jax.experimental import pallas as pl
from jax.experimental.pallas import tpu as pltpu
from jax.sharding import PartitionSpec as P

NVX = 32

CFL = 0.9
VMAX = 6.0
COLLIDE = 0.3
RHO_MIN = 0.25
TEMP_MIN = 0.25
PRECISE = lax.Precision.HIGHEST
MESH = pl.DeviceIdType.MESH
VM = pl.BlockSpec(memory_space=pltpu.VMEM)
ANY = pl.BlockSpec(memory_space=pl.ANY)
F32 = jnp.float32
BF16 = jnp.bfloat16
BITS = NVX.bit_length() - 1


def halves(values):
    high = values.astype(BF16)
    return high, (values - high.astype(F32)).astype(BF16)


def dot(left, right):
    return jnp.dot(left, right, preferred_element_type=F32)


def dot_split(high, low, right):
    width = right.shape[1]
    right_high, right_low = halves(right)
    both = dot(high, jnp.concatenate([right_high, right_low], axis=1))
    return both[:, :width] + (both[:, width:] + dot(low, right_high))


def dot3(left, right):
    return dot_split(*halves(left), right)


def dot6(left, right):
    return jnp.dot(left, right, precision=PRECISE, preferred_element_type=F32)


def node_velocity(indices):
    spacing = 2.0 * VMAX / NVX
    last = NVX - 1
    parts = (
        lax.shift_right_logical(indices, 2 * BITS),
        lax.shift_right_logical(indices, BITS) & last,
        indices & last,
    )
    return [-VMAX + (part.astype(F32) + 0.5) * spacing for part in parts]


class Sum:
    def __init__(self, send, pos, x, first, second, out, sems):
        self.send, self.pos = send, pos
        self.x, self.first, self.second, self.out = x, first, second, out
        self.sems = sems

    def scatter(self):
        me, members, member = self.pos.me, self.pos.members, self.pos.member
        self.copies = []
        for k in range(1, members):
            to, device = member(k)
            self.copies.append(
                self.send(
                    self.x.at[to], self.first.at[k - 1], self.sems[0].at[k - 1], self.sems[1].at[k - 1], device
                )
            )

    def cross(self):
        me, layer = self.pos.me, self.pos.layer
        total = self.x[me]
        for k, copy in enumerate(self.copies):
            copy.wait_recv()
            total = total + self.first[k]
        self.second[layer] = total
        mine = self.second.at[layer]
        self.copies = [
            self.send(mine, mine, self.sems[2].at[k - 1], self.sems[3].at[k - 1], self.pos.across(k))
            for k in range(1, self.pos.layers)
        ]

    def collect(self):
        me = self.pos.me
        for copy in self.copies:
            copy.wait_recv()
        total = self.second[0]
        for k in range(1, self.pos.layers):
            total = total + self.second[k]
        self.out[me] = total
        mine = self.out.at[me]
        self.copies = [
            self.send(mine, mine, self.sems[4].at[k - 1], self.sems[5].at[k - 1], self.pos.member(k)[1])
            for k in range(1, self.pos.members)
        ]

    def finish(self):
        for copy in self.copies:
            copy.wait_recv()


class Position:
    def __init__(self, slabs, layers):
        self.slabs, self.layers, self.members = slabs, layers, 2 * slabs
        brick = lax.axis_index("brick")
        self.brick = brick
        self.core, self.layer = lax.rem(brick, 2), lax.div(brick, 2)
        self.slab = lax.axis_index("slab")
        self.me = 2 * self.slab + self.core

    def member(self, k):
        to = lax.rem(self.me + k, self.members)
        return to, (lax.div(to, 2), 2 * self.layer + lax.rem(to, 2))

    def across(self, k):
        return (self.slab, 2 * lax.rem(self.layer + k, self.layers) + self.core)

    def others(self):
        bricks = 2 * self.layers
        count = self.slabs * bricks
        at = self.slab * bricks + self.brick
        for k in range(1, count):
            to = lax.rem(at + k, count)
            yield k - 1, (lax.div(to, bricks), lax.rem(to, bricks))

    def partner(self):
        return (self.slab, 2 * self.layer + 1 - self.core)

    def slab_at(self, k):
        to = lax.rem(self.slab + k, self.slabs)
        return to, (to, self.brick)

    def brick_at(self, k):
        bricks = 2 * self.layers
        return (self.slab, lax.rem(self.brick + k + bricks, bricks))


def factor_steps(work, matrix):
    size = matrix.shape[0]
    panel = 8
    row = lax.broadcasted_iota(jnp.int32, (size, size), 0)
    column = lax.broadcasted_iota(jnp.int32, (size, size), 1)
    work[:, :size] = matrix
    work[:, size:] = jnp.where(row == column, 1.0, 0.0)
    sub_one = lax.broadcasted_iota(jnp.int32, (panel, size), 0)
    for start in range(0, size, panel):
        rows = work[start : start + panel, :]
        columns = [
            jnp.broadcast_to(rows[:, start + k : start + k + 1], (panel, size))
            for k in range(panel)
        ]
        for k in range(panel):
            scale = lax.rsqrt(columns[k][k : k + 1, :])
            ratio = columns[k] * (scale * scale)
            ratio = jnp.where(sub_one > k, ratio, jnp.where(sub_one == k, 1.0 - scale, 0.0))
            for m in range(k + 1, panel):
                columns[m] = columns[m] - ratio * columns[m][k : k + 1, :]
            rows = rows - jnp.concatenate([ratio, ratio], axis=1) * rows[k : k + 1, :]
        work[start : start + panel, :] = rows
        if start + panel < size:
            tall = rows[:, :size].T[start + panel :, :]
            work[start + panel :, :] = work[start + panel :, :] - jnp.dot(
                tall, rows, precision=PRECISE, preferred_element_type=F32
            )
    factor = jnp.where(column <= row, work[:, :size].T, 0.0)
    inverse = jnp.where(column <= row, work[:, size:], 0.0)
    return factor, inverse


def step_kernel(names, slabs, layers, *refs):
    ref = dict(zip(names, refs))
    pos = Position(slabs, layers)
    core, slab, layer, brick, me = pos.core, pos.slab, pos.layer, pos.brick, pos.me
    members, bricks = pos.members, 2 * layers
    k_ref, v_ref = ref["k"], ref["v"]
    cells_x, cells_y, cells_z, rank = k_ref.shape
    own = cells_x * cells_y * cells_z
    nodes = v_ref.shape[0]
    lengths = (cells_x * slabs, cells_y * bricks, cells_z)
    cells = lengths[0] * lengths[1] * lengths[2]
    time_step = CFL / (VMAX * (lengths[0] + lengths[1] + lengths[2]))
    weight_x = 1.0 / cells
    weight_v = (2.0 * VMAX / NVX) ** 3
    base = (slab * bricks + brick) * nodes
    started = []

    def send(source, target, send_sem, recv_sem, device):
        copy = pltpu.make_async_remote_copy(
            src_ref=source,
            dst_ref=target,
            send_sem=send_sem,
            recv_sem=recv_sem,
            device_id=device,
            device_id_type=MESH,
        )
        copy.start()
        started.append(copy)
        return copy

    barrier = pltpu.get_barrier_semaphore()
    peers = [device for _, device in pos.others()]
    for peer in peers:
        pl.semaphore_signal(barrier, inc=1, device_id=peer, device_id_type=MESH)

    lane = lax.broadcasted_iota(jnp.int32, (8, nodes), 1)
    sub = lax.broadcasted_iota(jnp.int32, (8, nodes), 0)
    velocity = node_velocity(base + lane)
    square = velocity[0] * velocity[0] + velocity[1] * velocity[1] + velocity[2] * velocity[2]
    weights = jnp.where(sub == 0, 1.0, jnp.where(sub == 4, square, 0.0))
    upward = jnp.zeros_like(weights)
    for d in range(3):
        weights = jnp.where(sub == d + 1, velocity[d], weights)
        upward = jnp.where(sub == d + 5, jnp.maximum(velocity[d], 0.0), upward)
    values = v_ref[...]
    v_high, v_low = halves(values)
    v_rest = (values - v_high.astype(F32) - v_low.astype(F32)).astype(BF16)
    sums = dot(jnp.concatenate(halves(weights), axis=0), jnp.concatenate([v_high, v_low, v_rest], axis=1))
    sums = sums[:8] + sums[8:]
    squares = dot(upward.astype(BF16), jnp.concatenate(halves(values * values), axis=1))
    partial = sums[:, :rank] + (sums[:, rank : 2 * rank] + sums[:, 2 * rank :])
    partial = (partial + (squares[:, :rank] + squares[:, rank:])) * weight_v
    vec = ref["vec"]
    vec[slab, brick] = partial

    turned_v = values.T
    vt_high, vt_low = halves(turned_v)
    vt = ref["vt"]
    vt[:rank] = vt_high
    vt[rank:] = vt_low
    v_both = jnp.concatenate([v_high, v_low], axis=1)
    row = lax.broadcasted_iota(jnp.int32, (rank, rank), 0)
    column = lax.broadcasted_iota(jnp.int32, (rank, rank), 1)
    packed = []

    def pack(d):
        sides = []
        for side in (jnp.maximum(velocity[d][:1], 0.0), jnp.minimum(velocity[d][:1], 0.0)):
            high, low = halves(turned_v * (side * weight_v))
            both = dot(high, v_both)
            sides.append(both[:, :rank] + (both[:, rank:] + dot(low, v_high)))
        packed.append(jnp.where(row > column, sides[0], sides[1]))

    pack(0)
    pack(1)
    pl.semaphore_wait(barrier, len(peers))
    mine = vec.at[slab, brick]
    copies = [send(mine, mine, ref["vs"].at[i], ref["vr"].at[i], device) for i, device in pos.others()]
    halo_a, halo_b = ref["halo_a"], ref["halo_b"]
    halos = [
        send(k_ref.at[cells_x - 1], halo_a.at[0], ref["hs"].at[0], ref["hr"].at[0], pos.slab_at(1)[1]),
        send(k_ref.at[0], halo_a.at[1], ref["hs"].at[1], ref["hr"].at[1], pos.slab_at(slabs - 1)[1]),
        send(k_ref.at[:, cells_y - 1], halo_b.at[0], ref["hs"].at[2], ref["hr"].at[2], pos.brick_at(1)),
        send(k_ref.at[:, 0], halo_b.at[1], ref["hs"].at[3], ref["hr"].at[3], pos.brick_at(-1)),
    ]

    pack(2)
    share = 3 * rank // members
    ref["tx"][...] = jnp.concatenate(packed, axis=0).reshape(members, share, rank)
    transport_sum = Sum(send, pos, ref["tx"], ref["t1"], ref["t2"], ref["to"], [ref[f"tsem{i}"] for i in range(6)])
    transport_sum.scatter()

    for copy in copies:
        copy.wait_recv()
    vectors = vec[0, 0]
    for k in range(1, slabs * bricks):
        vectors = vectors + vec[k // bricks, k % bricks]

    own_k = k_ref[...].reshape(own, rank)
    kpad = ref["kpad"]
    kpad[...] = jnp.zeros_like(kpad)
    kpad[pl.ds(pl.multiple_of(core * own, 8), own), :] = own_k
    moments = lax.dot_general(
        vectors, kpad[...], (((1,), (1,)), ((), ())), precision=PRECISE, preferred_element_type=F32
    )
    pair = 2 * own
    density = jnp.maximum(moments[0:1], RHO_MIN)
    drift = [moments[d : d + 1] / density for d in range(1, 4)]
    bulk = drift[0] * drift[0] + drift[1] * drift[1] + drift[2] * drift[2]
    temper = jnp.maximum((moments[4:5] / density - bulk) / 3.0, TEMP_MIN)
    wide = 2.0 * math.pi * temper
    amplitude = density / (wide * jnp.sqrt(wide))
    state = jnp.zeros((8, pair), F32)
    sub_pair = lax.broadcasted_iota(jnp.int32, (8, pair), 0)
    lane_pair = lax.broadcasted_iota(jnp.int32, (8, pair), 1)
    for i, item in enumerate(drift + [-0.5 / temper, amplitude]):
        state = jnp.where(sub_pair == i, item, state)
    inside = (lane_pair >= core * own) & (lane_pair < (core + 1) * own)
    par = ref["par"]
    par[me, layer] = jnp.where(inside, state, 0.0)
    mine = par.at[me, layer]
    copies = [send(mine, mine, ref["ps"].at[i], ref["pr"].at[i], device) for i, device in pos.others()]
    transport_sum.cross()
    for copy in copies:
        copy.wait_recv()
    transport_sum.collect()

    mt_high, mt_low = ref["mt_high"], ref["mt_low"]
    mp, first, half, second, third = ref["mp"], ref["first"], ref["half"], ref["second"], ref["third"]
    group = math.gcd(nodes, NVX)
    groups = nodes // group
    width = 2 * pair
    slots = layers // 2
    fast_v = node_velocity(base + lax.broadcasted_iota(jnp.int32, (group, width), 0))
    slow_v = node_velocity(base + group * lax.broadcasted_iota(jnp.int32, (groups, width), 0))

    def project(to, slot):
        blocks = [par[2 * to, 2 * slot + i] + par[2 * to + 1, 2 * slot + i] for i in range(2)]
        state = jnp.concatenate(blocks, axis=1)
        u = [state[d : d + 1] for d in range(3)]
        rate, scale = state[3:4], state[4:5]
        fast = jnp.exp((fast_v[2] - u[2]) ** 2 * rate)
        slow = jnp.exp(((slow_v[0] - u[0]) ** 2 + (slow_v[1] - u[1]) ** 2) * rate) * scale
        place = pl.ds(pl.multiple_of((to * slots + slot) * width, width), width)
        for t in range(groups):
            high, low = halves(fast * slow[t : t + 1])
            mt_high[t * group : (t + 1) * group, place] = high
            mt_low[t * group : (t + 1) * group, place] = low
        high = dot(vt[...], mt_high[:, place])
        low = dot(vt[:rank], mt_low[:, place])
        result = ((high[:rank] + (high[rank:] + low)) * weight_v).T
        for i in range(2):
            for c in range(2):
                at = (2 * i + c) * own
                mp[to, 2 * slot + i, c] = result[at : at + own]

    def hand_over(k, slot, to):
        at = pl.ds(2 * slot, 2)
        return send(
            mp.at[to, at, 1 - core], first.at[to, at], ref["cs"].at[k, slot], ref["cr"].at[k, slot], pos.partner()
        )

    over = []

    def hand_on(k, slot, to, copy):
        copy.wait_recv()
        at = pl.ds(2 * slot, 2)
        if k == 0:
            second[slab, at] = mp[slab, at, core] + first[slab, at]
            return
        half[to, at] = mp[to, at, core] + first[to, at]
        over.append(
            send(half.at[to, at], second.at[slab, at], ref["ss"].at[k - 1, slot], ref["sr"].at[k - 1, slot], (to, brick))
        )

    waiting = []
    for k in list(range(1, slabs)) + [0]:
        to = lax.rem(slab + k, slabs)
        for slot in range(slots):
            project(to, slot)
            copy = hand_over(k, slot, to)
            if len(waiting) >= 1:
                hand_on(*waiting.pop(0))
            waiting.append((k, slot, to, copy))

    transport_sum.finish()
    packed = ref["to"][...].reshape(3 * rank, rank)
    trans = ref["trans"]
    for d in range(3):
        block = packed[d * rank : (d + 1) * rank]
        flipped = block.T
        diagonal = jnp.where(row == column, vectors[d + 5 : d + 6], 0.0)
        trans[d * rank : (d + 1) * rank] = jnp.where(row <= column, block, flipped)
        trans[(d + 3) * rank : (d + 4) * rank] = jnp.where(
            row > column, block, jnp.where(row < column, flipped, diagonal)
        )
    for copy in waiting:
        hand_on(*copy)
    for copy in halos:
        copy.wait_recv()
    field = k_ref[...]
    after_a = jnp.concatenate([field[1:], halo_a[1:2]], axis=0)
    before_a = jnp.concatenate([halo_a[0:1], field[:-1]], axis=0)
    after_b = jnp.concatenate([field[:, 1:], halo_b[1].reshape(cells_x, 1, cells_z, rank)], axis=1)
    before_b = jnp.concatenate([halo_b[0].reshape(cells_x, 1, cells_z, rank), field[:, :-1]], axis=1)

    def next_third(flat):
        count = flat.shape[0]
        index = lax.broadcasted_iota(jnp.int32, flat.shape, 0)
        return jnp.where(
            lax.rem(index, cells_z) == cells_z - 1,
            pltpu.roll(flat, cells_z - 1, 0),
            pltpu.roll(flat, count - 1, 0),
        )

    def last_third(flat):
        count = flat.shape[0]
        index = lax.broadcasted_iota(jnp.int32, flat.shape, 0)
        return jnp.where(
            lax.rem(index, cells_z) == 0,
            pltpu.roll(flat, count - cells_z + 1, 0),
            pltpu.roll(flat, 1, 0),
        )

    fields = [
        (after_a.reshape(own, rank) - own_k) * lengths[0],
        (after_b.reshape(own, rank) - own_k) * lengths[1],
        (next_third(own_k) - own_k) * lengths[2],
        (own_k - before_a.reshape(own, rank)) * lengths[0],
        (own_k - before_b.reshape(own, rank)) * lengths[1],
        (own_k - last_third(own_k)) * lengths[2],
    ]
    flux = dot3(jnp.concatenate(fields, axis=1), trans[...])
    kept = own_k - time_step * flux - COLLIDE * own_k

    for copy in over:
        copy.wait_recv()
    total = second[0]
    for k in range(1, slabs):
        total = total + second[k]
    quarter = ref["quarter"]
    quarter[...] = total
    copies = []
    for k in range(1, layers):
        to = lax.rem(layer + k, layers)
        copies.append(
            send(quarter.at[to], third.at[layer], ref["zs"].at[k - 1], ref["zr"].at[k - 1], pos.across(k))
        )
    third[layer] = quarter[layer]
    for copy in copies:
        copy.wait_recv()
    mproj = third[0]
    for k in range(1, layers):
        mproj = mproj + third[k]
    advanced = kept + COLLIDE * mproj

    adv = ref["adv"]
    adv[slab, brick] = advanced.reshape(cells_x, cells_y, cells_z, rank)
    here = adv.at[slab, brick]

    def to_slabs(block, j):
        return [
            send(block, block, ref["bs"].at[k - 1, j], ref["br"].at[k - 1, j], pos.slab_at(k)[1])
            for k in range(1, slabs)
        ]

    along = [
        send(here, here, ref["as"].at[k - 1], ref["ar"].at[k - 1], pos.across(k)) for k in range(1, layers)
    ]
    crossing = [to_slabs(here, 0)]
    last = [send(here, here, ref["ds"].at[0, 0], ref["dr"].at[0, 0], pos.partner())]
    raw_sum = Sum(send, pos, ref["rx"], ref["r1"], ref["r2"], ref["ro"], [ref[f"rsem{i}"] for i in range(6)])
    ref["rx"][...] = dot3(advanced.T, mproj).reshape(members, rank // members, rank)
    for j in range(1, layers):
        along[j - 1].wait_recv()
        block = adv.at[slab, 2 * lax.rem(layer + layers - j, layers) + core]
        crossing.append(to_slabs(block, j))
        last.append(send(block, block, ref["ds"].at[0, j], ref["dr"].at[0, j], pos.partner()))
    for j in range(layers):
        for k in range(1, slabs):
            crossing[j][k - 1].wait_recv()
            block = adv.at[lax.rem(slab + slabs - k, slabs), 2 * lax.rem(layer + layers - j, layers) + core]
            last.append(send(block, block, ref["ds"].at[k, j], ref["dr"].at[k, j], pos.partner()))
    raw_sum.scatter()
    for copy in last:
        copy.wait_recv()

    at, ahl = ref["at"], ref["ahl"]
    d_high, d_low = ref["d_high"], ref["d_low"]
    plane = cells // slabs
    for s in range(slabs):
        block = adv[s]
        flat = block.reshape(plane, rank)
        span = slice(s * plane, (s + 1) * plane)
        high, low = halves(flat)
        ahl[span, :rank] = high
        ahl[span, rank:] = low
        high, low = halves(flat.T)
        at[:rank, span] = high
        at[rank:, span] = low
        following = adv[(s + 1) % slabs]
        up_a = jnp.concatenate([block[:, 1:], following[:, :1]], axis=1)
        wrapped = jnp.concatenate([block[1:, :, :1], block[:1, :, :1]], axis=0)
        up_b = jnp.concatenate([block[:, :, 1:], wrapped], axis=2)
        ups = [up_a.reshape(plane, rank), up_b.reshape(plane, rank), next_third(flat)]
        for d in range(3):
            high, low = halves(ups[d] - flat)
            d_high[span, d * rank : (d + 1) * rank] = high
            d_low[span, d * rank : (d + 1) * rank] = low
    raw_sum.cross()
    both = dot(at[:rank], ahl[...])
    mixed = both[:, rank:]
    gram = (both[:, :rank] + (mixed + mixed.T)) * weight_x
    factor, inverse = factor_steps(ref["work"], gram)

    both = dot(at[...], d_high[...])
    slopes = both[:rank] + (both[rank:] + dot(at[:rank], d_low[...]))
    slopes = [slopes[:, d * rank : (d + 1) * rank] * (lengths[d] * weight_x) for d in range(3)]
    raw_sum.collect()
    raw_sum.finish()
    raw = ref["ro"][...].reshape(rank, rank) * weight_x
    source = time_step * dot6(
        jnp.concatenate(slopes + [-item.T for item in slopes], axis=1), trans[...]
    ) - COLLIDE * raw

    place = 2 * own
    scaled = ahl[...]
    top = dot(mt_high[...], scaled)
    low = dot(mt_low[...], ahl[:, :rank])
    back_raw = (top[:, :rank] + (top[:, rank:] + low)) * weight_x

    turned = inverse.T
    middle = (1.0 + COLLIDE) * factor + dot6(source.T, turned)
    moved = dot6(inverse, jnp.concatenate(slopes, axis=1))
    plus = dot6(jnp.concatenate([moved[:, d * rank : (d + 1) * rank] for d in range(3)], axis=0), turned)
    plus = [plus[d * rank : (d + 1) * rank] for d in range(3)]
    sides = jnp.concatenate(plus + [item.T for item in plus], axis=1)
    lnew = ref["lnew"]
    chunk = math.gcd(nodes, 256)
    for at_row in range(0, nodes, chunk):
        span = slice(at_row, at_row + chunk)
        lnow = dot3(v_ref[span, :], middle)
        sliding = dot3(lnow, sides)
        part = node_velocity(base + at_row + lax.broadcasted_iota(jnp.int32, (chunk, rank), 0))
        slide = jnp.zeros((chunk, rank), F32)
        for d in range(3):
            slide = slide + jnp.maximum(part[d], 0.0) * sliding[:, d * rank : (d + 1) * rank]
            slide = slide - jnp.minimum(part[d], 0.0) * sliding[:, (d + 3) * rank : (d + 4) * rank]
        mback = dot3(back_raw[span], turned)
        lnew[span, :] = lnow + time_step * slide + COLLIDE * (mback - lnow)

    new = lnew[...]
    high, low = halves(new)
    rest = (new - high.astype(F32) - low.astype(F32)).astype(BF16)
    new_t = new.T
    high_t, low_t = halves(new_t)
    both = dot(high_t, jnp.concatenate([high, low, rest], axis=1))
    mixed = both[:, rank : 2 * rank] + (both[:, 2 * rank :] + 0.5 * dot(low_t, low))
    gram_v = (both[:, :rank] + (mixed + mixed.T)) * weight_v
    half_rank = rank // 2
    lanes = lax.broadcasted_iota(jnp.int32, (half_rank // 2, rank), 1)
    corner = jnp.where(
        lanes < half_rank,
        pltpu.roll(gram_v[half_rank : half_rank + half_rank // 2], half_rank, 1),
        gram_v[half_rank + half_rank // 2 :],
    )
    gx, g1, g2, g3, go = ref["gx"], ref["g1"], ref["g2"], ref["g3"], ref["go"]
    gx[...] = jnp.concatenate([gram_v[:half_rank], corner], axis=0).reshape(gx.shape)
    copy = send(gx.at[1 - core], g1, ref["gcs"].at[0], ref["gcr"].at[0], pos.partner())
    copy.wait_recv()
    g2[slab] = gx[core] + g1[...]
    mine = g2.at[slab]
    copies = [
        send(mine, mine, ref["gss"].at[k - 1], ref["gsr"].at[k - 1], pos.slab_at(k)[1]) for k in range(1, slabs)
    ]
    ref["basis_x"][...] = dot3(advanced, turned)
    for copy in copies:
        copy.wait_recv()
    total = g2[0]
    for k in range(1, slabs):
        total = total + g2[k]
    g3[layer] = total
    mine = g3.at[layer]
    copies = [
        send(mine, mine, ref["gls"].at[k - 1], ref["glr"].at[k - 1], pos.across(k)) for k in range(1, layers)
    ]
    for copy in copies:
        copy.wait_recv()
    total = g3[0]
    for k in range(1, layers):
        total = total + g3[k]
    go[core] = total
    mine = go.at[core]
    send(mine, mine, ref["gcs"].at[1], ref["gcr"].at[1], pos.partner()).wait_recv()
    whole = go[...].reshape(half_rank + half_rank // 2, rank)
    corner = whole[half_rank:]
    gram_ref = ref["gram"]
    gram_ref[:half_rank] = whole[:half_rank]
    gram_ref[half_rank : half_rank + half_rank // 2] = pltpu.roll(corner, half_rank, 1)
    gram_ref[half_rank + half_rank // 2 :] = corner
    for copy in started:
        copy.wait_send()


def finish_kernel(gram, lnew, field, basis_x, coupling, basis_v, work, factor_buffer, out, sems):
    give = pltpu.make_async_copy(field, basis_x, sems.at[0])
    give.start()
    factor, inverse = factor_steps(work, gram[...])
    factor_buffer[...] = factor
    copies = [give, pltpu.make_async_copy(factor_buffer, coupling, sems.at[1])]
    copies[1].start()
    turned = inverse.T
    nodes = lnew.shape[0]
    count = sems.shape[0] - 2
    chunk = nodes // count
    for i in range(count):
        span = pl.ds(i * chunk, chunk)
        out[span, :] = dot3(lnew[span, :], turned)
        copies.append(pltpu.make_async_copy(out.at[span], basis_v.at[span], sems.at[2 + i]))
        copies[-1].start()
    for copy in copies:
        copy.wait()


def local(k_coeffs, v_basis):
    cells_x, cells_y, cells_z, rank = k_coeffs.shape
    slabs = lax.axis_size("slab")
    layers = lax.axis_size("brick") // 2
    members = 2 * slabs
    own = cells_x * cells_y * cells_z
    nodes = v_basis.shape[0]
    cells = own * members * layers
    share = 3 * rank // members
    part = rank // members
    pair = 2 * own
    devices = members * layers
    names = ["k", "v", "basis_x", "gram", "lnew"]
    scratch = []

    used = [0]

    def buffer(name, shape, dtype=F32):
        names.append(name)
        used[0] += math.prod(shape) * jnp.dtype(dtype).itemsize
        scratch.append(pltpu.VMEM(shape, dtype))

    def semaphores(name, *shape):
        names.append(name)
        scratch.append(pltpu.SemaphoreType.DMA(shape))

    def reduction(name, rows):
        buffer(name + "x", (members, rows, rank))
        buffer(name + "1", (members - 1, rows, rank))
        buffer(name + "2", (layers, rows, rank))
        buffer(name + "o", (members, rows, rank))
        for i, count in enumerate([members, members, layers, layers, members, members]):
            semaphores(name + "sem" + str(i), count - 1)

    buffer("vec", (slabs, 2 * layers, 8, rank))
    buffer("halo_a", (2, cells_y, cells_z, rank))
    buffer("halo_b", (2, cells_x, cells_z, rank))
    buffer("vt", (2 * rank, nodes), BF16)
    buffer("kpad", (pair, rank))
    buffer("par", (members, layers, 8, pair))
    buffer("mt_high", (nodes, cells), BF16)
    buffer("mt_low", (nodes, cells), BF16)
    buffer("mp", (slabs, layers, 2, own, rank))
    buffer("first", (slabs, layers, own, rank))
    buffer("half", (slabs, layers, own, rank))
    buffer("second", (slabs, layers, own, rank))
    buffer("quarter", (layers, own, rank))
    buffer("third", (layers, own, rank))
    buffer("trans", (6 * rank, rank))
    buffer("adv", (slabs, 2 * layers, cells_x, cells_y, cells_z, rank))
    buffer("at", (2 * rank, cells), BF16)
    buffer("ahl", (cells, 2 * rank), BF16)
    buffer("d_high", (cells, 3 * rank), BF16)
    buffer("d_low", (cells, 3 * rank), BF16)
    buffer("work", (rank, 2 * rank))
    reduction("t", share)
    reduction("r", part)
    packed = 3 * rank // 8
    buffer("gx", (2, packed, rank))
    buffer("g1", (packed, rank))
    buffer("g2", (slabs, packed, rank))
    buffer("g3", (layers, packed, rank))
    buffer("go", (2, packed, rank))
    for name, count in (("gc", 2), ("gs", slabs - 1), ("v", devices - 1), ("p", devices - 1)):
        semaphores(name + "s", count)
        semaphores(name + "r", count)
    for name in ("gl", "z", "a"):
        semaphores(name + "s", layers - 1)
        semaphores(name + "r", layers - 1)
    semaphores("hs", 4)
    semaphores("hr", 4)
    for name, shape in (
        ("c", (slabs, layers // 2)),
        ("s", (slabs - 1, layers // 2)),
        ("b", (slabs - 1, layers)),
        ("d", (slabs, layers)),
    ):
        semaphores(name + "s", *shape)
        semaphores(name + "r", *shape)
    basis_x, gram, lnew = pl.pallas_call(
        functools.partial(step_kernel, tuple(names), slabs, layers),
        out_shape=(
            jax.ShapeDtypeStruct((own, rank), F32),
            jax.ShapeDtypeStruct((rank, rank), F32),
            jax.ShapeDtypeStruct(v_basis.shape, F32),
        ),
        in_specs=[VM, VM],
        out_specs=(VM, VM, VM),
        scratch_shapes=scratch,
        compiler_params=pltpu.CompilerParams(
            collective_id=1, has_side_effects=True, vmem_limit_bytes=min(60 * 2**20, used[0] + 10 * 2**20)
        ),
    )(k_coeffs, v_basis)
    chunks = 4
    basis_x, coupling, basis_v = pl.pallas_call(
        finish_kernel,
        out_shape=(
            jax.ShapeDtypeStruct((own, rank), F32),
            jax.ShapeDtypeStruct((rank, rank), F32),
            jax.ShapeDtypeStruct(v_basis.shape, F32),
        ),
        in_specs=[VM, VM, VM],
        out_specs=(ANY, ANY, ANY),
        scratch_shapes=[
            pltpu.VMEM((rank, 2 * rank), F32),
            pltpu.VMEM((rank, rank), F32),
            pltpu.VMEM(v_basis.shape, F32),
            pltpu.SemaphoreType.DMA((2 + chunks,)),
        ],
        compiler_params=pltpu.CompilerParams(vmem_limit_bytes=12 * 2**20),
    )(gram, lnew, basis_x)
    return basis_x.reshape(k_coeffs.shape), coupling, basis_v


def solution(mesh):
    return jax.shard_map(
        local,
        mesh=mesh,
        in_specs=(P("slab", "brick", None, None), P(("slab", "brick"), None)),
        out_specs=(P("slab", "brick", None, None), P(), P(("slab", "brick"), None)),
        check_vma=False,
    )
```

```python
import functools
import math

import jax
import jax.numpy as jnp
from jax import lax
from jax.experimental import pallas as pl
from jax.experimental.pallas import tpu as pltpu
from jax.sharding import PartitionSpec as P

NVX = 32

CFL = 0.9
VMAX = 6.0
COLLIDE = 0.3
RHO_MIN = 0.25
TEMP_MIN = 0.25
PRECISE = lax.Precision.HIGHEST
MESH = pl.DeviceIdType.MESH
VM = pl.BlockSpec(memory_space=pltpu.VMEM)
HBM = pl.BlockSpec(memory_space=pltpu.HBM)
F32 = jnp.float32
BF16 = jnp.bfloat16
BITS = NVX.bit_length() - 1


def halves(values):
    high = values.astype(BF16)
    return high, (values - high.astype(F32)).astype(BF16)


def dot(left, right):
    return jnp.dot(left, right, preferred_element_type=F32)


def dot_split(high, low, right):
    width = right.shape[1]
    right_high, right_low = halves(right)
    both = dot(high, jnp.concatenate([right_high, right_low], axis=1))
    return both[:, :width] + (both[:, width:] + dot(low, right_high))


def dot3(left, right):
    depth, width = right.shape
    high, low = halves(left)
    if depth != 128:
        return dot_split(high, low, right)
    right_high, right_low = halves(right)
    top = jnp.concatenate([right_high, right_low], axis=1)
    under = jnp.concatenate([right_high, jnp.zeros_like(right_low)], axis=1)
    both = dot(jnp.concatenate([high, low], axis=1), jnp.concatenate([top, under], axis=0))
    return both[:, :width] + both[:, width:]


def dot6(left, right):
    return jnp.dot(left, right, precision=PRECISE, preferred_element_type=F32)


def node_velocity(indices):
    spacing = 2.0 * VMAX / NVX
    last = NVX - 1
    parts = (
        lax.shift_right_logical(indices, 2 * BITS),
        lax.shift_right_logical(indices, BITS) & last,
        indices & last,
    )
    return [-VMAX + (part.astype(F32) + 0.5) * spacing for part in parts]


class Sum:
    def __init__(self, send, pos, x, first, second, out, sems):
        self.send, self.pos = send, pos
        self.x, self.first, self.second, self.out = x, first, second, out
        self.sems = sems

    def scatter(self):
        me, members, member = self.pos.me, self.pos.members, self.pos.member
        self.copies = []
        for k in range(1, members):
            to, device = member(k)
            self.copies.append(
                self.send(
                    self.x.at[to], self.first.at[k - 1], self.sems[0].at[k - 1], self.sems[1].at[k - 1], device
                )
            )

    def cross(self):
        me, layer = self.pos.me, self.pos.layer
        total = self.x[me]
        for k, copy in enumerate(self.copies):
            copy.wait_recv()
            total = total + self.first[k]
        self.second[layer] = total
        mine = self.second.at[layer]
        self.copies = [
            self.send(mine, mine, self.sems[2].at[k - 1], self.sems[3].at[k - 1], self.pos.across(k))
            for k in range(1, self.pos.layers)
        ]

    def collect(self):
        me = self.pos.me
        for copy in self.copies:
            copy.wait_recv()
        total = self.second[0]
        for k in range(1, self.pos.layers):
            total = total + self.second[k]
        self.out[me] = total
        mine = self.out.at[me]
        self.copies = [
            self.send(mine, mine, self.sems[4].at[k - 1], self.sems[5].at[k - 1], self.pos.member(k)[1])
            for k in range(1, self.pos.members)
        ]

    def finish(self):
        for copy in self.copies:
            copy.wait_recv()


class Position:
    def __init__(self, slabs, layers):
        self.slabs, self.layers, self.members = slabs, layers, 2 * slabs
        brick = lax.axis_index("brick")
        self.brick = brick
        self.core, self.layer = lax.rem(brick, 2), lax.div(brick, 2)
        self.slab = lax.axis_index("slab")
        self.me = 2 * self.slab + self.core

    def member(self, k):
        to = lax.rem(self.me + k, self.members)
        return to, (lax.div(to, 2), 2 * self.layer + lax.rem(to, 2))

    def mate(self, k):
        if self.layers != 4:
            return lax.rem(self.layer + k, self.layers)
        if k == 1:
            return self.layer + 1 - 2 * lax.rem(self.layer, 2)
        return lax.rem(self.layer + 2, self.layers) if k == 2 else self.layers - 1 - self.layer

    def source(self, k):
        if k == 0:
            return self.layer
        return self.mate(k) if self.layers == 4 else lax.rem(self.layer + self.layers - k, self.layers)

    def across(self, k):
        return (self.slab, 2 * lax.rem(self.layer + k, self.layers) + self.core)

    def others(self):
        bricks = 2 * self.layers
        count = self.slabs * bricks
        at = self.slab * bricks + self.brick
        for k in range(1, count):
            to = lax.rem(at + k, count)
            yield k - 1, (lax.div(to, bricks), lax.rem(to, bricks))

    def partner(self):
        return (self.slab, 2 * self.layer + 1 - self.core)

    def slab_at(self, k):
        to = lax.rem(self.slab + k, self.slabs)
        return to, (to, self.brick)

    def brick_at(self, k):
        bricks = 2 * self.layers
        return (self.slab, lax.rem(self.brick + k + bricks, bricks))


def factor_steps(work, matrix):
    size = matrix.shape[0]
    block, panel = 8, 16
    row = lax.broadcasted_iota(jnp.int32, (size, size), 0)
    column = lax.broadcasted_iota(jnp.int32, (size, size), 1)
    work[:, :size] = matrix
    work[:, size:] = jnp.where(row == column, 1.0, 0.0)
    sub = lax.broadcasted_iota(jnp.int32, (block, size), 0)
    narrow, wide = (block, size), (block, 2 * size)
    for start in range(0, size, panel):
        rows = [work[start : start + block, :], work[start + block : start + panel, :]]
        for b in range(2):
            at = start + b * block
            columns = {
                (r, m): jnp.broadcast_to(rows[r][:, at + m : at + m + 1], narrow)
                for r in range(b, 2)
                for m in range(block)
            }
            entry = {
                (i, m): jnp.broadcast_to(columns[b, m][i : i + 1], narrow) for m in range(block) for i in range(m, block)
            }
            scales = entry[0, 0]
            for k in range(block):
                scale = lax.rsqrt(entry[k, k])
                invert = scale * scale
                scales = scale if k == 0 else jnp.where(sub == k, scale, scales)
                ratios = {r: columns[r, k] * invert for r in range(b, 2)}
                ratios[b] = jnp.where(sub > k, ratios[b], 0.0)
                for m in range(k + 1, block):
                    factor = entry[m, k] * invert
                    for i in range(m, block):
                        entry[i, m] = entry[i, m] - entry[i, k] * factor
                for r in range(b, 2):
                    for m in range(k + 1, block):
                        columns[r, m] = columns[r, m] - ratios[r] * entry[m, k]
                pivot = jnp.broadcast_to(rows[b][k : k + 1], wide)
                for r in range(b, 2):
                    rows[r] = rows[r] - jnp.concatenate([ratios[r], ratios[r]], axis=1) * pivot
            rows[b] = rows[b] * jnp.concatenate([scales, scales], axis=1)
        both = jnp.concatenate(rows, axis=0)
        work[start : start + panel, :] = both
        if start + panel < size:
            tall = both[:, :size].T[start + panel :, :]
            work[start + panel :, :] = work[start + panel :, :] - dot6(tall, both)
    factor = jnp.where(column <= row, work[:, :size].T, 0.0)
    inverse = jnp.where(column <= row, work[:, size:], 0.0)
    return factor, inverse


def step_kernel(names, slabs, layers, *refs):
    ref = dict(zip(names, refs))
    pos = Position(slabs, layers)
    core, slab, layer, brick, me = pos.core, pos.slab, pos.layer, pos.brick, pos.me
    members, bricks = pos.members, 2 * layers
    k_ref, v_ref = ref["k_here"], ref["v_here"]
    inputs = [
        pltpu.make_async_copy(ref["k"], k_ref, ref["insem"].at[0]),
        pltpu.make_async_copy(ref["v"], v_ref, ref["insem"].at[1]),
    ]
    for copy in inputs:
        copy.start()
    cells_x, cells_y, cells_z, rank = k_ref.shape
    own = cells_x * cells_y * cells_z
    nodes = v_ref.shape[0]
    lengths = (cells_x * slabs, cells_y * bricks, cells_z)
    cells = lengths[0] * lengths[1] * lengths[2]
    time_step = CFL / (VMAX * (lengths[0] + lengths[1] + lengths[2]))
    weight_x = 1.0 / cells
    weight_v = (2.0 * VMAX / NVX) ** 3
    base = (slab * bricks + brick) * nodes
    started = []

    def send(source, target, send_sem, recv_sem, device):
        copy = pltpu.make_async_remote_copy(
            src_ref=source,
            dst_ref=target,
            send_sem=send_sem,
            recv_sem=recv_sem,
            device_id=device,
            device_id_type=MESH,
        )
        copy.start()
        started.append(copy)
        return copy

    barrier = pltpu.get_barrier_semaphore()
    peers = [device for _, device in pos.others()]
    for peer in peers:
        pl.semaphore_signal(barrier, inc=1, device_id=peer, device_id_type=MESH)

    lane = lax.broadcasted_iota(jnp.int32, (8, nodes), 1)
    sub = lax.broadcasted_iota(jnp.int32, (8, nodes), 0)
    velocity = node_velocity(base + lane)
    square = velocity[0] * velocity[0] + velocity[1] * velocity[1] + velocity[2] * velocity[2]
    weights = jnp.where(sub == 0, 1.0, jnp.where(sub == 4, square, 0.0))
    upward = jnp.zeros_like(weights)
    for d in range(3):
        weights = jnp.where(sub == d + 1, velocity[d], weights)
        upward = jnp.where(sub == d + 5, jnp.maximum(velocity[d], 0.0), upward)
    for copy in inputs:
        copy.wait()
    values = v_ref[...]
    v_high, v_low = halves(values)
    v_rest = (values - v_high.astype(F32) - v_low.astype(F32)).astype(BF16)
    sums = dot(jnp.concatenate(halves(weights), axis=0), jnp.concatenate([v_high, v_low, v_rest], axis=1))
    sums = sums[:8] + sums[8:]
    squares = dot(upward.astype(BF16), jnp.concatenate(halves(values * values), axis=1))
    partial = sums[:, :rank] + (sums[:, rank : 2 * rank] + sums[:, 2 * rank :])
    partial = (partial + (squares[:, :rank] + squares[:, rank:])) * weight_v
    vec = ref["vec"]
    vec[slab, brick] = partial

    turned_v = values.T
    vt_high, vt_low = halves(turned_v)
    vt = ref["vt"]
    vt[:rank] = vt_high
    vt[rank:] = vt_low
    v_both = jnp.concatenate([v_high, v_low], axis=1)
    row = lax.broadcasted_iota(jnp.int32, (rank, rank), 0)
    column = lax.broadcasted_iota(jnp.int32, (rank, rank), 1)
    packed = []

    def pack(d):
        sides = []
        for side in (jnp.maximum(velocity[d][:1], 0.0), jnp.minimum(velocity[d][:1], 0.0)):
            high, low = halves(turned_v * (side * weight_v))
            both = dot(high, v_both)
            sides.append(both[:, :rank] + (both[:, rank:] + dot(low, v_high)))
        packed.append(jnp.where(row > column, sides[0], sides[1]))

    pack(0)
    pl.semaphore_wait(barrier, len(peers))
    mine = vec.at[slab, brick]
    copies = [send(mine, mine, ref["vs"].at[i], ref["vr"].at[i], device) for i, device in pos.others()]
    halo_a, halo_b = ref["halo_a"], ref["halo_b"]
    halos = [
        send(k_ref.at[cells_x - 1], halo_a.at[0], ref["hs"].at[0], ref["hr"].at[0], pos.slab_at(1)[1]),
        send(k_ref.at[0], halo_a.at[1], ref["hs"].at[1], ref["hr"].at[1], pos.slab_at(slabs - 1)[1]),
        send(k_ref.at[:, cells_y - 1], halo_b.at[0], ref["hs"].at[2], ref["hr"].at[2], pos.brick_at(1)),
        send(k_ref.at[:, 0], halo_b.at[1], ref["hs"].at[3], ref["hr"].at[3], pos.brick_at(-1)),
    ]

    pack(1)
    pack(2)
    share = 3 * rank // members
    ref["tx"][...] = jnp.concatenate(packed, axis=0).reshape(members, share, rank)
    transport_sum = Sum(send, pos, ref["tx"], ref["t1"], ref["t2"], ref["to"], [ref[f"tsem{i}"] for i in range(6)])
    transport_sum.scatter()

    for copy in copies:
        copy.wait_recv()
    vectors = vec[0, 0]
    for k in range(1, slabs * bricks):
        vectors = vectors + vec[k // bricks, k % bricks]

    own_k = k_ref[...].reshape(own, rank)
    kpad = ref["kpad"]
    kpad[...] = jnp.zeros_like(kpad)
    kpad[pl.ds(pl.multiple_of(core * own, 8), own), :] = own_k
    moments = lax.dot_general(
        vectors, kpad[...], (((1,), (1,)), ((), ())), precision=PRECISE, preferred_element_type=F32
    )
    pair = 2 * own
    density = jnp.maximum(moments[0:1], RHO_MIN)
    drift = [moments[d : d + 1] / density for d in range(1, 4)]
    bulk = drift[0] * drift[0] + drift[1] * drift[1] + drift[2] * drift[2]
    temper = jnp.maximum((moments[4:5] / density - bulk) / 3.0, TEMP_MIN)
    wide = 2.0 * math.pi * temper
    amplitude = density / (wide * jnp.sqrt(wide))
    state = jnp.zeros((8, pair), F32)
    sub_pair = lax.broadcasted_iota(jnp.int32, (8, pair), 0)
    lane_pair = lax.broadcasted_iota(jnp.int32, (8, pair), 1)
    for i, item in enumerate(drift + [-0.5 / temper, amplitude]):
        state = jnp.where(sub_pair == i, item, state)
    inside = (lane_pair >= core * own) & (lane_pair < (core + 1) * own)
    par = ref["par"]
    par[me, layer] = jnp.where(inside, state, 0.0)
    mine = par.at[me, layer]
    copies = [send(mine, mine, ref["ps"].at[i], ref["pr"].at[i], device) for i, device in pos.others()]
    for copy in copies:
        copy.wait_recv()
    transport_sum.cross()

    mt_high, mt_low = ref["mt_high"], ref["mt_low"]
    mp, first, half, second, third = ref["mp"], ref["first"], ref["half"], ref["second"], ref["third"]
    group = math.gcd(nodes, NVX)
    groups = nodes // group
    width = 2 * pair
    slots = layers // 2
    fast_v = node_velocity(base + lax.broadcasted_iota(jnp.int32, (group, width), 0))
    slow_v = node_velocity(base + group * lax.broadcasted_iota(jnp.int32, (groups, width), 0))

    def project(to, slot):
        blocks = [par[2 * to, 2 * slot + i] + par[2 * to + 1, 2 * slot + i] for i in range(2)]
        state = jnp.concatenate(blocks, axis=1)
        u = [state[d : d + 1] for d in range(3)]
        rate, scale = state[3:4], state[4:5]
        fast = jnp.exp((fast_v[2] - u[2]) ** 2 * rate)
        slow = jnp.exp(((slow_v[0] - u[0]) ** 2 + (slow_v[1] - u[1]) ** 2) * rate) * scale
        place = pl.ds(pl.multiple_of((to * slots + slot) * width, width), width)
        for t in range(groups):
            high, low = halves(fast * slow[t : t + 1])
            mt_high[t * group : (t + 1) * group, place] = high
            mt_low[t * group : (t + 1) * group, place] = low
        high = dot(vt[...], mt_high[:, place])
        low = dot(vt[:rank], mt_low[:, place])
        result = ((high[:rank] + (high[rank:] + low)) * weight_v).T
        for i in range(2):
            for c in range(2):
                at = (2 * i + c) * own
                mp[to, 2 * slot + i, c] = result[at : at + own]

    def hand_over(k, slot, to):
        at = pl.ds(2 * slot, 2)
        return send(
            mp.at[to, at, 1 - core], first.at[to, at], ref["cs"].at[k, slot], ref["cr"].at[k, slot], pos.partner()
        )

    over = []

    def hand_on(k, slot, to, copy):
        copy.wait_recv()
        at = pl.ds(2 * slot, 2)
        if k == 0:
            second[slab, at] = mp[slab, at, core] + first[slab, at]
            return
        half[to, at] = mp[to, at, core] + first[to, at]
        over.append(
            send(half.at[to, at], second.at[slab, at], ref["ss"].at[k - 1, slot], ref["sr"].at[k - 1, slot], (to, brick))
        )

    waiting = []
    for k in list(range(1, slabs)) + [0]:
        to = lax.rem(slab + k, slabs)
        for slot in range(slots):
            project(to, slot)
            copy = hand_over(k, slot, to)
            if len(waiting) >= 1:
                hand_on(*waiting.pop(0))
            waiting.append((k, slot, to, copy))

    transport_sum.collect()
    for copy in waiting:
        hand_on(*copy)

    transport_sum.finish()
    packed = ref["to"][...].reshape(3 * rank, rank)
    trans = ref["trans"]
    for d in range(3):
        block = packed[d * rank : (d + 1) * rank]
        flipped = block.T
        diagonal = jnp.where(row == column, vectors[d + 5 : d + 6], 0.0)
        trans[d * rank : (d + 1) * rank] = jnp.where(row <= column, block, flipped)
        trans[(d + 3) * rank : (d + 4) * rank] = jnp.where(
            row > column, block, jnp.where(row < column, flipped, diagonal)
        )
    for copy in halos:
        copy.wait_recv()
    field = k_ref[...]
    after_a = jnp.concatenate([field[1:], halo_a[1:2]], axis=0)
    before_a = jnp.concatenate([halo_a[0:1], field[:-1]], axis=0)
    after_b = jnp.concatenate([field[:, 1:], halo_b[1].reshape(cells_x, 1, cells_z, rank)], axis=1)
    before_b = jnp.concatenate([halo_b[0].reshape(cells_x, 1, cells_z, rank), field[:, :-1]], axis=1)

    def next_third(flat):
        count = flat.shape[0]
        index = lax.broadcasted_iota(jnp.int32, flat.shape, 0)
        return jnp.where(
            lax.rem(index, cells_z) == cells_z - 1,
            pltpu.roll(flat, cells_z - 1, 0),
            pltpu.roll(flat, count - 1, 0),
        )

    def last_third(flat):
        count = flat.shape[0]
        index = lax.broadcasted_iota(jnp.int32, flat.shape, 0)
        return jnp.where(
            lax.rem(index, cells_z) == 0,
            pltpu.roll(flat, count - cells_z + 1, 0),
            pltpu.roll(flat, 1, 0),
        )

    fields = [
        (after_a.reshape(own, rank) - own_k) * lengths[0],
        (after_b.reshape(own, rank) - own_k) * lengths[1],
        (next_third(own_k) - own_k) * lengths[2],
        (own_k - before_a.reshape(own, rank)) * lengths[0],
        (own_k - before_b.reshape(own, rank)) * lengths[1],
        (own_k - last_third(own_k)) * lengths[2],
    ]
    flux = dot3(jnp.concatenate(fields, axis=1), trans[...])
    kept = own_k - time_step * flux - COLLIDE * own_k

    for copy in over:
        copy.wait_recv()
    total = second[0]
    for k in range(1, slabs):
        total = total + second[k]
    quarter = ref["quarter"]
    quarter[...] = total
    copies = []
    for k in range(1, layers):
        to = lax.rem(layer + k, layers)
        copies.append(
            send(quarter.at[to], third.at[layer], ref["zs"].at[k - 1], ref["zr"].at[k - 1], pos.across(k))
        )
    third[layer] = quarter[layer]
    for copy in copies:
        copy.wait_recv()
    mproj = third[0]
    for k in range(1, layers):
        mproj = mproj + third[k]
    advanced = kept + COLLIDE * mproj

    adv = ref["adv"]
    adv[slab, brick] = advanced.reshape(cells_x, cells_y, cells_z, rank)
    here = adv.at[slab, brick]

    def to_slabs(block, j):
        return [
            send(block, block, ref["bs"].at[k - 1, j], ref["br"].at[k - 1, j], pos.slab_at(k)[1])
            for k in range(1, slabs)
        ]

    along = [
        send(here, here, ref["as"].at[k - 1], ref["ar"].at[k - 1], (slab, 2 * pos.mate(k) + core))
        for k in range(1, layers)
    ]
    crossing = [to_slabs(here, 0)]
    last = [send(here, here, ref["ds"].at[0, 0], ref["dr"].at[0, 0], pos.partner())]
    raw_sum = Sum(send, pos, ref["rx"], ref["r1"], ref["r2"], ref["ro"], [ref[f"rsem{i}"] for i in range(6)])
    ref["rx"][...] = dot3(advanced.T, mproj).reshape(members, rank // members, rank)
    raw_sum.scatter()
    for j in range(1, layers):
        along[j - 1].wait_recv()
        block = adv.at[slab, 2 * pos.source(j) + core]
        crossing.append(to_slabs(block, j))
        last.append(send(block, block, ref["ds"].at[0, j], ref["dr"].at[0, j], pos.partner()))
    raw_sum.cross()
    for j in range(layers):
        for k in range(1, slabs):
            crossing[j][k - 1].wait_recv()
            block = adv.at[lax.rem(slab + slabs - k, slabs), 2 * pos.source(j) + core]
            last.append(send(block, block, ref["ds"].at[k, j], ref["dr"].at[k, j], pos.partner()))
    raw_sum.collect()
    for copy in last:
        copy.wait_recv()

    at, ahl = ref["at"], ref["ahl"]
    d_high, d_low = ref["d_high"], ref["d_low"]
    plane = cells // slabs
    for s in range(slabs):
        block = adv[s]
        flat = block.reshape(plane, rank)
        span = slice(s * plane, (s + 1) * plane)
        high, low = halves(flat)
        ahl[span, :rank] = high
        ahl[span, rank:] = low
        high, low = halves(flat.T)
        at[:rank, span] = high
        at[rank:, span] = low
        following = adv[(s + 1) % slabs]
        up_a = jnp.concatenate([block[:, 1:], following[:, :1]], axis=1)
        wrapped = jnp.concatenate([block[1:, :, :1], block[:1, :, :1]], axis=0)
        up_b = jnp.concatenate([block[:, :, 1:], wrapped], axis=2)
        ups = [up_a.reshape(plane, rank), up_b.reshape(plane, rank), next_third(flat)]
        for d in range(3):
            high, low = halves(ups[d] - flat)
            d_high[span, d * rank : (d + 1) * rank] = high
            d_low[span, d * rank : (d + 1) * rank] = low
    both = dot(at[:rank], ahl[...])
    mixed = both[:, rank:]
    gram = (both[:, :rank] + (mixed + mixed.T)) * weight_x
    factor, inverse = factor_steps(ref["work"], gram)

    both = dot(at[...], d_high[...])
    slopes = both[:rank] + (both[rank:] + dot(at[:rank], d_low[...]))
    slopes = [slopes[:, d * rank : (d + 1) * rank] * (lengths[d] * weight_x) for d in range(3)]
    raw_sum.finish()
    raw = ref["ro"][...].reshape(rank, rank) * weight_x
    source = time_step * dot6(
        jnp.concatenate(slopes + [-item.T for item in slopes], axis=1), trans[...]
    ) - COLLIDE * raw

    place = 2 * own
    scaled = ahl[...]
    top = dot(mt_high[...], scaled)
    low = dot(mt_low[...], ahl[:, :rank])
    back_raw = (top[:, :rank] + (top[:, rank:] + low)) * weight_x

    turned = inverse.T
    middle = (1.0 + COLLIDE) * factor + dot6(source.T, turned)
    moved = dot6(inverse, jnp.concatenate(slopes, axis=1))
    plus = dot6(jnp.concatenate([moved[:, d * rank : (d + 1) * rank] for d in range(3)], axis=0), turned)
    plus = [plus[d * rank : (d + 1) * rank] for d in range(3)]
    lnew = ref["lnew"]
    chunk = math.gcd(nodes, NVX * NVX // 4)
    gram_v = jnp.zeros((rank, rank), F32)
    mixed_v = jnp.zeros((rank, rank), F32)
    back = [-item.T for item in plus]
    for at_row in range(0, nodes, chunk):
        span = slice(at_row, at_row + chunk)
        node = base + at_row
        lnow = dot3(v_ref[span, :], middle)
        ahead = [node // (NVX * NVX) >= NVX // 2, node // NVX % NVX >= NVX // 2]
        sides = [jnp.where(ahead[d], plus[d], back[d]) for d in range(2)] + [plus[2], back[2]]
        sliding = dot3(lnow, jnp.concatenate(sides, axis=1))
        part = node_velocity(node + lax.broadcasted_iota(jnp.int32, (chunk, rank), 0))
        slide = part[0] * sliding[:, :rank] + part[1] * sliding[:, rank : 2 * rank]
        slide = slide + part[2] * jnp.where(part[2] > 0, sliding[:, 2 * rank : 3 * rank], sliding[:, 3 * rank :])
        mback = dot3(back_raw[span], turned)
        new = lnow + time_step * slide + COLLIDE * (mback - lnow)
        lnew[span, :] = new
        high, low = halves(new)
        rest = (new - high.astype(F32) - low.astype(F32)).astype(BF16)
        high_t, low_t = halves(new.T)
        both = dot(high_t, jnp.concatenate([high, low, rest], axis=1))
        gram_v = gram_v + both[:, :rank]
        mixed_v = mixed_v + (both[:, rank : 2 * rank] + (both[:, 2 * rank :] + 0.5 * dot(low_t, low)))
    gram_v = (gram_v + (mixed_v + mixed_v.T)) * weight_v

    half_rank = rank // 2
    lanes = lax.broadcasted_iota(jnp.int32, (half_rank // 2, rank), 1)
    corner = jnp.where(
        lanes < half_rank,
        pltpu.roll(gram_v[half_rank : half_rank + half_rank // 2], half_rank, 1),
        gram_v[half_rank + half_rank // 2 :],
    )
    gx, g1, g2, g3, go = ref["gx"], ref["g1"], ref["g2"], ref["g3"], ref["go"]
    gx[...] = jnp.concatenate([gram_v[:half_rank], corner], axis=0).reshape(gx.shape)
    copy = send(gx.at[1 - core], g1, ref["gcs"].at[0], ref["gcr"].at[0], pos.partner())
    copy.wait_recv()
    g2[slab] = gx[core] + g1[...]
    mine = g2.at[slab]
    copies = [
        send(mine, mine, ref["gss"].at[k - 1], ref["gsr"].at[k - 1], pos.slab_at(k)[1]) for k in range(1, slabs)
    ]
    ref["basis_x"][...] = dot3(advanced, turned)
    for copy in copies:
        copy.wait_recv()
    total = g2[0]
    for k in range(1, slabs):
        total = total + g2[k]
    g3[layer] = total
    mine = g3.at[layer]
    copies = [
        send(mine, mine, ref["gls"].at[k - 1], ref["glr"].at[k - 1], pos.across(k)) for k in range(1, layers)
    ]
    for copy in copies:
        copy.wait_recv()
    total = g3[0]
    for k in range(1, layers):
        total = total + g3[k]
    go[core] = total
    mine = go.at[core]
    send(mine, mine, ref["gcs"].at[1], ref["gcr"].at[1], pos.partner()).wait_recv()
    whole = go[...].reshape(half_rank + half_rank // 2, rank)
    corner = whole[half_rank:]
    gram_ref = ref["gram"]
    gram_ref[:half_rank] = whole[:half_rank]
    gram_ref[half_rank : half_rank + half_rank // 2] = pltpu.roll(corner, half_rank, 1)
    gram_ref[half_rank + half_rank // 2 :] = corner
    for copy in started:
        copy.wait_send()


def finish_kernel(gram, lnew, field, basis_x, coupling, basis_v, work, factor_buffer, out, sems):
    give = pltpu.make_async_copy(field, basis_x, sems.at[0])
    give.start()
    factor, inverse = factor_steps(work, gram[...])
    factor_buffer[...] = factor
    copies = [give, pltpu.make_async_copy(factor_buffer, coupling, sems.at[1])]
    copies[1].start()
    turned = inverse.T
    nodes = lnew.shape[0]
    count = sems.shape[0] - 2
    chunk = nodes // count
    for i in range(count):
        span = pl.ds(i * chunk, chunk)
        out[span, :] = dot3(lnew[span, :], turned)
        copies.append(pltpu.make_async_copy(out.at[span], basis_v.at[span], sems.at[2 + i]))
        copies[-1].start()
    for copy in copies:
        copy.wait()


def local(k_coeffs, v_basis):
    cells_x, cells_y, cells_z, rank = k_coeffs.shape
    slabs = lax.axis_size("slab")
    layers = lax.axis_size("brick") // 2
    members = 2 * slabs
    own = cells_x * cells_y * cells_z
    nodes = v_basis.shape[0]
    cells = own * members * layers
    share = 3 * rank // members
    part = rank // members
    pair = 2 * own
    devices = members * layers
    names = ["k", "v", "basis_x", "gram", "lnew"]
    scratch = []

    used = [0]

    def buffer(name, shape, dtype=F32):
        names.append(name)
        used[0] += math.prod(shape) * jnp.dtype(dtype).itemsize
        scratch.append(pltpu.VMEM(shape, dtype))

    def semaphores(name, *shape):
        names.append(name)
        scratch.append(pltpu.SemaphoreType.DMA(shape))

    def reduction(name, rows):
        buffer(name + "x", (members, rows, rank))
        buffer(name + "1", (members - 1, rows, rank))
        buffer(name + "2", (layers, rows, rank))
        buffer(name + "o", (members, rows, rank))
        for i, count in enumerate([members, members, layers, layers, members, members]):
            semaphores(name + "sem" + str(i), count - 1)

    buffer("k_here", k_coeffs.shape)
    buffer("v_here", v_basis.shape)
    semaphores("insem", 2)
    buffer("vec", (slabs, 2 * layers, 8, rank))
    buffer("halo_a", (2, cells_y, cells_z, rank))
    buffer("halo_b", (2, cells_x, cells_z, rank))
    buffer("vt", (2 * rank, nodes), BF16)
    buffer("kpad", (pair, rank))
    buffer("par", (members, layers, 8, pair))
    buffer("mt_high", (nodes, cells), BF16)
    buffer("mt_low", (nodes, cells), BF16)
    buffer("mp", (slabs, layers, 2, own, rank))
    buffer("first", (slabs, layers, own, rank))
    buffer("half", (slabs, layers, own, rank))
    buffer("second", (slabs, layers, own, rank))
    buffer("quarter", (layers, own, rank))
    buffer("third", (layers, own, rank))
    buffer("trans", (6 * rank, rank))
    buffer("adv", (slabs, 2 * layers, cells_x, cells_y, cells_z, rank))
    buffer("at", (2 * rank, cells), BF16)
    buffer("ahl", (cells, 2 * rank), BF16)
    buffer("d_high", (cells, 3 * rank), BF16)
    buffer("d_low", (cells, 3 * rank), BF16)
    buffer("work", (rank, 2 * rank))
    reduction("t", share)
    reduction("r", part)
    packed = 3 * rank // 8
    buffer("gx", (2, packed, rank))
    buffer("g1", (packed, rank))
    buffer("g2", (slabs, packed, rank))
    buffer("g3", (layers, packed, rank))
    buffer("go", (2, packed, rank))
    for name, count in (("gc", 2), ("gs", slabs - 1), ("v", devices - 1), ("p", devices - 1)):
        semaphores(name + "s", count)
        semaphores(name + "r", count)
    for name in ("gl", "z", "a"):
        semaphores(name + "s", layers - 1)
        semaphores(name + "r", layers - 1)
    semaphores("hs", 4)
    semaphores("hr", 4)
    for name, shape in (
        ("c", (slabs, layers // 2)),
        ("s", (slabs - 1, layers // 2)),
        ("b", (slabs - 1, layers)),
        ("d", (slabs, layers)),
    ):
        semaphores(name + "s", *shape)
        semaphores(name + "r", *shape)
    basis_x, gram, lnew = pl.pallas_call(
        functools.partial(step_kernel, tuple(names), slabs, layers),
        out_shape=(
            jax.ShapeDtypeStruct((own, rank), F32),
            jax.ShapeDtypeStruct((rank, rank), F32),
            jax.ShapeDtypeStruct(v_basis.shape, F32),
        ),
        in_specs=[HBM, HBM],
        out_specs=(VM, VM, VM),
        scratch_shapes=scratch,
        compiler_params=pltpu.CompilerParams(
            collective_id=1, has_side_effects=True, vmem_limit_bytes=min(62 * 2**20, used[0] + 14 * 2**20)
        ),
    )(pltpu.with_memory_space_constraint(k_coeffs, pltpu.HBM), pltpu.with_memory_space_constraint(v_basis, pltpu.HBM))
    chunks = 4
    basis_x, coupling, basis_v = pl.pallas_call(
        finish_kernel,
        out_shape=(
            jax.ShapeDtypeStruct((own, rank), F32),
            jax.ShapeDtypeStruct((rank, rank), F32),
            jax.ShapeDtypeStruct(v_basis.shape, F32),
        ),
        in_specs=[VM, VM, VM],
        out_specs=(HBM, HBM, HBM),
        scratch_shapes=[
            pltpu.VMEM((rank, 2 * rank), F32),
            pltpu.VMEM((rank, rank), F32),
            pltpu.VMEM(v_basis.shape, F32),
            pltpu.SemaphoreType.DMA((2 + chunks,)),
        ],
        compiler_params=pltpu.CompilerParams(vmem_limit_bytes=12 * 2**20),
    )(gram, lnew, basis_x)
    return basis_x.reshape(k_coeffs.shape), coupling, basis_v


def solution(mesh):
    return jax.shard_map(
        local,
        mesh=mesh,
        in_specs=(P("slab", "brick", None, None), P(("slab", "brick"), None)),
        out_specs=(P("slab", "brick", None, None), P(), P(("slab", "brick"), None)),
        check_vma=False,
    )
```

```python
import functools
import math

import jax
import jax.numpy as jnp
from jax import lax
from jax.experimental import pallas as pl
from jax.experimental.pallas import tpu as pltpu
from jax.sharding import PartitionSpec as P

NVX = 32

CFL = 0.9
VMAX = 6.0
COLLIDE = 0.3
RHO_MIN = 0.25
TEMP_MIN = 0.25
PRECISE = lax.Precision.HIGHEST
MESH = pl.DeviceIdType.MESH
VM = pl.BlockSpec(memory_space=pltpu.VMEM)
HBM = pl.BlockSpec(memory_space=pltpu.HBM)
F32 = jnp.float32
BF16 = jnp.bfloat16
BITS = NVX.bit_length() - 1


def halves(values):
    high = values.astype(BF16)
    return high, (values - high.astype(F32)).astype(BF16)


def dot(left, right):
    return jnp.dot(left, right, preferred_element_type=F32)


def dot_split(high, low, right):
    width = right.shape[1]
    right_high, right_low = halves(right)
    both = dot(high, jnp.concatenate([right_high, right_low], axis=1))
    return both[:, :width] + (both[:, width:] + dot(low, right_high))


def dot3(left, right):
    depth, width = right.shape
    high, low = halves(left)
    if depth != 128:
        return dot_split(high, low, right)
    right_high, right_low = halves(right)
    top = jnp.concatenate([right_high, right_low], axis=1)
    under = jnp.concatenate([right_high, jnp.zeros_like(right_low)], axis=1)
    both = dot(jnp.concatenate([high, low], axis=1), jnp.concatenate([top, under], axis=0))
    return both[:, :width] + both[:, width:]


def dot6(left, right):
    return jnp.dot(left, right, precision=PRECISE, preferred_element_type=F32)


def node_velocity(indices):
    spacing = 2.0 * VMAX / NVX
    last = NVX - 1
    parts = (
        lax.shift_right_logical(indices, 2 * BITS),
        lax.shift_right_logical(indices, BITS) & last,
        indices & last,
    )
    return [-VMAX + (part.astype(F32) + 0.5) * spacing for part in parts]


class Sum:
    def __init__(self, send, pos, ref, name):
        self.send, self.pos = send, pos
        self.x, self.first, self.half, self.second, self.third, self.out = [
            ref[name + part] for part in ("x", "1", "h", "2", "3", "o")
        ]
        self.sems = [(ref[name + part + "s"], ref[name + part + "r"]) for part in ("c", "s", "l", "g")]

    def copy(self, source, target, stage, index, device):
        sent, received = self.sems[stage]
        return self.send(source, target, sent.at[index], received.at[index], device)

    def wait(self):
        for copy in self.copies:
            copy.wait_recv()

    def start(self):
        self.copies = [self.copy(self.x.at[1 - self.pos.core], self.first, 0, 0, self.pos.partner())]

    def scatter(self):
        self.wait()
        slab = self.pos.slab
        self.half[...] = self.x[self.pos.core] + self.first[...]
        self.second[slab] = self.half[slab]
        self.copies = []
        for k in range(1, self.pos.slabs):
            to, device = self.pos.slab_at(k)
            self.copies.append(self.copy(self.half.at[to], self.second.at[slab], 1, k - 1, device))

    def cross(self):
        self.wait()
        total = self.second[0]
        for k in range(1, self.pos.slabs):
            total = total + self.second[k]
        self.third[self.pos.layer] = total
        mine = self.third.at[self.pos.layer]
        self.copies = [self.copy(mine, mine, 2, k - 1, self.pos.across(k)) for k in range(1, self.pos.layers)]

    def collect(self):
        self.wait()
        total = self.third[0]
        for k in range(1, self.pos.layers):
            total = total + self.third[k]
        self.out[self.pos.core, self.pos.slab] = total
        mine = self.out.at[self.pos.core, self.pos.slab]
        self.copies = [self.copy(mine, mine, 3, k - 1, self.pos.slab_at(k)[1]) for k in range(1, self.pos.slabs)]

    def share(self):
        self.wait()
        mine = self.out.at[self.pos.core]
        self.copies = [self.copy(mine, mine, 0, 1, self.pos.partner())]

    def finish(self):
        self.wait()


class Position:
    def __init__(self, slabs, layers):
        self.slabs, self.layers, self.members = slabs, layers, 2 * slabs
        brick = lax.axis_index("brick")
        self.brick = brick
        self.core, self.layer = lax.rem(brick, 2), lax.div(brick, 2)
        self.slab = lax.axis_index("slab")
        self.me = 2 * self.slab + self.core

    def member(self, k):
        to = lax.rem(self.me + k, self.members)
        return to, (lax.div(to, 2), 2 * self.layer + lax.rem(to, 2))

    def mate(self, k):
        if self.layers != 4:
            return lax.rem(self.layer + k, self.layers)
        if k == 1:
            return self.layer + 1 - 2 * lax.rem(self.layer, 2)
        return lax.rem(self.layer + 2, self.layers) if k == 2 else self.layers - 1 - self.layer

    def source(self, k):
        if k == 0:
            return self.layer
        return self.mate(k) if self.layers == 4 else lax.rem(self.layer + self.layers - k, self.layers)

    def across(self, k):
        return (self.slab, 2 * lax.rem(self.layer + k, self.layers) + self.core)

    def others(self):
        bricks = 2 * self.layers
        count = self.slabs * bricks
        at = self.slab * bricks + self.brick
        for k in range(1, count):
            to = lax.rem(at + k, count)
            yield k - 1, (lax.div(to, bricks), lax.rem(to, bricks))

    def partner(self):
        return (self.slab, 2 * self.layer + 1 - self.core)

    def slab_at(self, k):
        to = lax.rem(self.slab + k, self.slabs)
        return to, (to, self.brick)

    def brick_at(self, k):
        bricks = 2 * self.layers
        return (self.slab, lax.rem(self.brick + k + bricks, bricks))


def factor_steps(work, matrix):
    size = matrix.shape[0]
    block, panel = 8, 16
    row = lax.broadcasted_iota(jnp.int32, (size, size), 0)
    column = lax.broadcasted_iota(jnp.int32, (size, size), 1)
    work[:, :size] = matrix
    work[:, size:] = jnp.where(row == column, 1.0, 0.0)
    sub = lax.broadcasted_iota(jnp.int32, (block, size), 0)
    narrow, wide = (block, size), (block, 2 * size)
    for start in range(0, size, panel):
        rows = [work[start : start + block, :], work[start + block : start + panel, :]]
        for b in range(2):
            at = start + b * block
            columns = {
                (r, m): jnp.broadcast_to(rows[r][:, at + m : at + m + 1], narrow)
                for r in range(b, 2)
                for m in range(block)
            }
            entry = {
                (i, m): jnp.broadcast_to(columns[b, m][i : i + 1], narrow) for m in range(block) for i in range(m, block)
            }
            scales = entry[0, 0]
            for k in range(block):
                scale = lax.rsqrt(entry[k, k])
                invert = scale * scale
                scales = scale if k == 0 else jnp.where(sub == k, scale, scales)
                ratios = {r: columns[r, k] * invert for r in range(b, 2)}
                ratios[b] = jnp.where(sub > k, ratios[b], 0.0)
                for m in range(k + 1, block):
                    factor = entry[m, k] * invert
                    for i in range(m, block):
                        entry[i, m] = entry[i, m] - entry[i, k] * factor
                for r in range(b, 2):
                    for m in range(k + 1, block):
                        columns[r, m] = columns[r, m] - ratios[r] * entry[m, k]
                pivot = jnp.broadcast_to(rows[b][k : k + 1], wide)
                for r in range(b, 2):
                    rows[r] = rows[r] - jnp.concatenate([ratios[r], ratios[r]], axis=1) * pivot
            rows[b] = rows[b] * jnp.concatenate([scales, scales], axis=1)
        both = jnp.concatenate(rows, axis=0)
        work[start : start + panel, :] = both
        if start + panel < size:
            high = both.astype(BF16).astype(F32)
            low = (both - high).astype(BF16).astype(F32)
            rest = both - high - low
            left = jnp.concatenate([item[:, :size] for item in (high, high, low, high, rest, low)], axis=0)
            right = jnp.concatenate([item.astype(BF16) for item in (high, low, high, rest, high, low)], axis=0)
            tall = left.T[start + panel :, :].astype(BF16)
            work[start + panel :, :] = work[start + panel :, :] - dot(tall, right)
    factor = jnp.where(column <= row, work[:, :size].T, 0.0)
    inverse = jnp.where(column <= row, work[:, size:], 0.0)
    return factor, inverse


def step_kernel(names, slabs, layers, *refs):
    ref = dict(zip(names, refs))
    pos = Position(slabs, layers)
    core, slab, layer, brick, me = pos.core, pos.slab, pos.layer, pos.brick, pos.me
    members, bricks = pos.members, 2 * layers
    k_ref, v_ref = ref["k_here"], ref["v_here"]
    inputs = [
        pltpu.make_async_copy(ref["k"], k_ref, ref["insem"].at[0]),
        pltpu.make_async_copy(ref["v"], v_ref, ref["insem"].at[1]),
    ]
    for copy in inputs:
        copy.start()
    cells_x, cells_y, cells_z, rank = k_ref.shape
    own = cells_x * cells_y * cells_z
    nodes = v_ref.shape[0]
    lengths = (cells_x * slabs, cells_y * bricks, cells_z)
    cells = lengths[0] * lengths[1] * lengths[2]
    time_step = CFL / (VMAX * (lengths[0] + lengths[1] + lengths[2]))
    weight_x = 1.0 / cells
    weight_v = (2.0 * VMAX / NVX) ** 3
    base = (slab * bricks + brick) * nodes
    started = []

    def send(source, target, send_sem, recv_sem, device):
        copy = pltpu.make_async_remote_copy(
            src_ref=source,
            dst_ref=target,
            send_sem=send_sem,
            recv_sem=recv_sem,
            device_id=device,
            device_id_type=MESH,
        )
        copy.start()
        started.append(copy)
        return copy

    barrier = pltpu.get_barrier_semaphore()
    peers = [pos.member(k)[1] for k in range(1, members)] + [pos.across(k) for k in range(1, layers)]
    for peer in peers:
        pl.semaphore_signal(barrier, inc=1, device_id=peer, device_id_type=MESH)

    lane = lax.broadcasted_iota(jnp.int32, (8, nodes), 1)
    sub = lax.broadcasted_iota(jnp.int32, (8, nodes), 0)
    velocity = node_velocity(base + lane)
    square = velocity[0] * velocity[0] + velocity[1] * velocity[1] + velocity[2] * velocity[2]
    weights = jnp.where(sub == 0, 1.0, jnp.where(sub == 4, square, 0.0))
    upward = jnp.zeros_like(weights)
    for d in range(3):
        weights = jnp.where(sub == d + 1, velocity[d], weights)
        upward = jnp.where(sub == d + 5, jnp.maximum(velocity[d], 0.0), upward)
    for copy in inputs:
        copy.wait()
    values = v_ref[...]
    v_high, v_low = halves(values)
    v_rest = (values - v_high.astype(F32) - v_low.astype(F32)).astype(BF16)
    sums = dot(jnp.concatenate(halves(weights), axis=0), jnp.concatenate([v_high, v_low, v_rest], axis=1))
    sums = sums[:8] + sums[8:]
    squares = dot(upward.astype(BF16), jnp.concatenate(halves(values * values), axis=1))
    partial = sums[:, :rank] + (sums[:, rank : 2 * rank] + sums[:, 2 * rank :])
    partial = (partial + (squares[:, :rank] + squares[:, rank:])) * weight_v
    vec_l, vec_m = ref["vec_l"], ref["vec_m"]
    vec_l[layer] = partial

    turned_v = values.T
    vt_high, vt_low = halves(turned_v)
    vt = ref["vt"]
    vt[:rank] = vt_high
    vt[rank:] = vt_low
    v_both = jnp.concatenate([v_high, v_low], axis=1)
    row = lax.broadcasted_iota(jnp.int32, (rank, rank), 0)
    column = lax.broadcasted_iota(jnp.int32, (rank, rank), 1)
    packed = []

    def pack(d):
        sides = []
        for side in (jnp.maximum(velocity[d][:1], 0.0), jnp.minimum(velocity[d][:1], 0.0)):
            high, low = halves(turned_v * (side * weight_v))
            both = dot(high, v_both)
            sides.append(both[:, :rank] + (both[:, rank:] + dot(low, v_high)))
        packed.append(jnp.where(row > column, sides[0], sides[1]))

    pack(0)
    pl.semaphore_wait(barrier, len(peers))
    mine = vec_l.at[layer]
    copies = [
        send(mine, mine, ref["vls"].at[k - 1], ref["vlr"].at[k - 1], pos.across(k)) for k in range(1, layers)
    ]
    pack(1)
    pack(2)
    ref["tx"][...] = jnp.concatenate(packed, axis=0).reshape(ref["tx"].shape)
    transport_sum = Sum(send, pos, ref, "t")

    for copy in copies:
        copy.wait_recv()
    total = vec_l[0]
    for k in range(1, layers):
        total = total + vec_l[k]
    vec_m[me] = total
    mine = vec_m.at[me]
    copies = [
        send(mine, mine, ref["vms"].at[k - 1], ref["vmr"].at[k - 1], pos.member(k)[1]) for k in range(1, members)
    ]
    transport_sum.start()
    transport_sum.scatter()
    for copy in copies:
        copy.wait_recv()
    vectors = vec_m[0]
    for k in range(1, members):
        vectors = vectors + vec_m[k]

    own_k = k_ref[...].reshape(own, rank)
    kpad = ref["kpad"]
    kpad[...] = jnp.zeros_like(kpad)
    kpad[pl.ds(pl.multiple_of(core * own, 8), own), :] = own_k
    moments = lax.dot_general(
        vectors, kpad[...], (((1,), (1,)), ((), ())), precision=PRECISE, preferred_element_type=F32
    )
    pair = 2 * own
    density = jnp.maximum(moments[0:1], RHO_MIN)
    drift = [moments[d : d + 1] / density for d in range(1, 4)]
    bulk = drift[0] * drift[0] + drift[1] * drift[1] + drift[2] * drift[2]
    temper = jnp.maximum((moments[4:5] / density - bulk) / 3.0, TEMP_MIN)
    wide = 2.0 * math.pi * temper
    amplitude = density / (wide * jnp.sqrt(wide))
    state = jnp.zeros((8, pair), F32)
    sub_pair = lax.broadcasted_iota(jnp.int32, (8, pair), 0)
    lane_pair = lax.broadcasted_iota(jnp.int32, (8, pair), 1)
    for i, item in enumerate(drift + [-0.5 / temper, amplitude]):
        state = jnp.where(sub_pair == i, item, state)
    inside = (lane_pair >= core * own) & (lane_pair < (core + 1) * own)
    par = ref["par"]
    par[me, layer] = jnp.where(inside, state, 0.0)
    mine = par.at[me, layer, pl.ds(0, 5)]
    copies = [send(mine, mine, ref["ps"].at[i], ref["pr"].at[i], device) for i, device in pos.others()]
    halo_a, halo_b = ref["halo_a"], ref["halo_b"]
    halos = [
        send(k_ref.at[cells_x - 1], halo_a.at[0], ref["hs"].at[0], ref["hr"].at[0], pos.slab_at(1)[1]),
        send(k_ref.at[0], halo_a.at[1], ref["hs"].at[1], ref["hr"].at[1], pos.slab_at(slabs - 1)[1]),
        send(k_ref.at[:, cells_y - 1], halo_b.at[0], ref["hs"].at[2], ref["hr"].at[2], pos.brick_at(1)),
        send(k_ref.at[:, 0], halo_b.at[1], ref["hs"].at[3], ref["hr"].at[3], pos.brick_at(-1)),
    ]
    transport_sum.cross()
    for copy in copies:
        copy.wait_recv()

    mt_high, mt_low = ref["mt_high"], ref["mt_low"]
    mp, first, half, second, third = ref["mp"], ref["first"], ref["half"], ref["second"], ref["third"]
    group = math.gcd(nodes, NVX)
    groups = nodes // group
    width = 2 * pair
    slots = layers // 2
    fast_v = node_velocity(base + lax.broadcasted_iota(jnp.int32, (group, width), 0))
    slow_v = node_velocity(base + group * lax.broadcasted_iota(jnp.int32, (groups, width), 0))

    def project(to, slot):
        blocks = [par[2 * to, 2 * slot + i] + par[2 * to + 1, 2 * slot + i] for i in range(2)]
        state = jnp.concatenate(blocks, axis=1)
        u = [state[d : d + 1] for d in range(3)]
        rate, scale = state[3:4], state[4:5]
        fast = jnp.exp((fast_v[2] - u[2]) ** 2 * rate)
        slow = jnp.exp(((slow_v[0] - u[0]) ** 2 + (slow_v[1] - u[1]) ** 2) * rate) * scale
        place = pl.ds(pl.multiple_of((to * slots + slot) * width, width), width)
        for t in range(groups):
            high, low = halves(fast * slow[t : t + 1])
            mt_high[t * group : (t + 1) * group, place] = high
            mt_low[t * group : (t + 1) * group, place] = low
        high = dot(vt[...], mt_high[:, place])
        low = dot(vt[:rank], mt_low[:, place])
        result = ((high[:rank] + (high[rank:] + low)) * weight_v).T
        for i in range(2):
            for c in range(2):
                at = (2 * i + c) * own
                mp[to, 2 * slot + i, c] = result[at : at + own]

    def hand_over(k, slot, to):
        at = pl.ds(2 * slot, 2)
        return send(
            mp.at[to, at, 1 - core], first.at[to, at], ref["cs"].at[k, slot], ref["cr"].at[k, slot], pos.partner()
        )

    over = []

    def hand_on(k, slot, to, copy):
        copy.wait_recv()
        at = pl.ds(2 * slot, 2)
        if k == 0:
            second[slab, at] = mp[slab, at, core] + first[slab, at]
            return
        half[to, at] = mp[to, at, core] + first[to, at]
        over.append(
            send(half.at[to, at], second.at[slab, at], ref["ss"].at[k - 1, slot], ref["sr"].at[k - 1, slot], (to, brick))
        )

    waiting = []
    for k in list(range(1, slabs)) + [0]:
        to = lax.rem(slab + k, slabs)
        for slot in range(slots):
            project(to, slot)
            if k == 1 and slot == 0:
                transport_sum.collect()
            copy = hand_over(k, slot, to)
            if len(waiting) >= 1:
                hand_on(*waiting.pop(0))
            waiting.append((k, slot, to, copy))

    transport_sum.share()
    for copy in waiting:
        hand_on(*copy)

    transport_sum.finish()
    packed = ref["to"][...].reshape(3 * rank, rank)
    trans = ref["trans"]
    for d in range(3):
        block = packed[d * rank : (d + 1) * rank]
        flipped = block.T
        diagonal = jnp.where(row == column, vectors[d + 5 : d + 6], 0.0)
        trans[d * rank : (d + 1) * rank] = jnp.where(row <= column, block, flipped)
        trans[(d + 3) * rank : (d + 4) * rank] = jnp.where(
            row > column, block, jnp.where(row < column, flipped, diagonal)
        )
    for copy in halos:
        copy.wait_recv()
    field = k_ref[...]
    after_a = jnp.concatenate([field[1:], halo_a[1:2]], axis=0)
    before_a = jnp.concatenate([halo_a[0:1], field[:-1]], axis=0)
    after_b = jnp.concatenate([field[:, 1:], halo_b[1].reshape(cells_x, 1, cells_z, rank)], axis=1)
    before_b = jnp.concatenate([halo_b[0].reshape(cells_x, 1, cells_z, rank), field[:, :-1]], axis=1)

    def next_third(flat):
        count = flat.shape[0]
        index = lax.broadcasted_iota(jnp.int32, flat.shape, 0)
        return jnp.where(
            lax.rem(index, cells_z) == cells_z - 1,
            pltpu.roll(flat, cells_z - 1, 0),
            pltpu.roll(flat, count - 1, 0),
        )

    def last_third(flat):
        count = flat.shape[0]
        index = lax.broadcasted_iota(jnp.int32, flat.shape, 0)
        return jnp.where(
            lax.rem(index, cells_z) == 0,
            pltpu.roll(flat, count - cells_z + 1, 0),
            pltpu.roll(flat, 1, 0),
        )

    fields = [
        (after_a.reshape(own, rank) - own_k) * lengths[0],
        (after_b.reshape(own, rank) - own_k) * lengths[1],
        (next_third(own_k) - own_k) * lengths[2],
        (own_k - before_a.reshape(own, rank)) * lengths[0],
        (own_k - before_b.reshape(own, rank)) * lengths[1],
        (own_k - last_third(own_k)) * lengths[2],
    ]
    flux = dot3(jnp.concatenate(fields, axis=1), trans[...])
    kept = own_k - time_step * flux - COLLIDE * own_k

    for copy in over:
        copy.wait_recv()
    total = second[0]
    for k in range(1, slabs):
        total = total + second[k]
    quarter = ref["quarter"]
    quarter[...] = total
    copies = []
    for k in range(1, layers):
        to = lax.rem(layer + k, layers)
        copies.append(
            send(quarter.at[to], third.at[layer], ref["zs"].at[k - 1], ref["zr"].at[k - 1], pos.across(k))
        )
    third[layer] = quarter[layer]
    for copy in copies:
        copy.wait_recv()
    mproj = third[0]
    for k in range(1, layers):
        mproj = mproj + third[k]
    advanced = kept + COLLIDE * mproj

    adv = ref["adv"]
    adv[slab, brick] = advanced.reshape(cells_x, cells_y, cells_z, rank)
    here = adv.at[slab, brick]

    def to_slabs(block, j):
        return [
            send(block, block, ref["bs"].at[k - 1, j], ref["br"].at[k - 1, j], pos.slab_at(k)[1])
            for k in range(1, slabs)
        ]

    along = [
        send(here, here, ref["as"].at[k - 1], ref["ar"].at[k - 1], (slab, 2 * pos.mate(k) + core))
        for k in range(1, layers)
    ]
    crossing = [to_slabs(here, 0)]
    last = [send(here, here, ref["ds"].at[0, 0], ref["dr"].at[0, 0], pos.partner())]
    raw_sum = Sum(send, pos, ref, "r")
    ref["rx"][...] = dot3(advanced.T, mproj).reshape(ref["rx"].shape)
    raw_sum.start()
    raw_sum.scatter()
    for j in range(1, layers):
        along[j - 1].wait_recv()
        block = adv.at[slab, 2 * pos.source(j) + core]
        crossing.append(to_slabs(block, j))
        last.append(send(block, block, ref["ds"].at[0, j], ref["dr"].at[0, j], pos.partner()))
    raw_sum.cross()
    for j in range(layers):
        for k in range(1, slabs):
            crossing[j][k - 1].wait_recv()
            block = adv.at[lax.rem(slab + slabs - k, slabs), 2 * pos.source(j) + core]
            last.append(send(block, block, ref["ds"].at[k, j], ref["dr"].at[k, j], pos.partner()))
    raw_sum.collect()
    for copy in last:
        copy.wait_recv()

    at, ahl = ref["at"], ref["ahl"]
    d_high, d_low = ref["d_high"], ref["d_low"]
    plane = cells // slabs
    for s in range(slabs):
        block = adv[s]
        flat = block.reshape(plane, rank)
        span = slice(s * plane, (s + 1) * plane)
        high, low = halves(flat)
        ahl[span, :rank] = high
        ahl[span, rank:] = low
        high, low = halves(flat.T)
        at[:rank, span] = high
        at[rank:, span] = low
        following = adv[(s + 1) % slabs]
        up_a = jnp.concatenate([block[:, 1:], following[:, :1]], axis=1)
        wrapped = jnp.concatenate([block[1:, :, :1], block[:1, :, :1]], axis=0)
        up_b = jnp.concatenate([block[:, :, 1:], wrapped], axis=2)
        ups = [up_a.reshape(plane, rank), up_b.reshape(plane, rank), next_third(flat)]
        for d in range(3):
            high, low = halves(ups[d] - flat)
            d_high[span, d * rank : (d + 1) * rank] = high
            d_low[span, d * rank : (d + 1) * rank] = low
    both = dot(at[:rank], ahl[...])
    mixed = both[:, rank:]
    gram = (both[:, :rank] + (mixed + mixed.T)) * weight_x
    factor, inverse = factor_steps(ref["work"], gram)

    both = dot(at[...], d_high[...])
    slopes = both[:rank] + (both[rank:] + dot(at[:rank], d_low[...]))
    slopes = [slopes[:, d * rank : (d + 1) * rank] * (lengths[d] * weight_x) for d in range(3)]
    raw_sum.share()
    raw_sum.finish()
    raw = ref["ro"][...].reshape(rank, rank) * weight_x
    source = time_step * dot6(
        jnp.concatenate(slopes + [-item.T for item in slopes], axis=1), trans[...]
    ) - COLLIDE * raw

    place = 2 * own
    scaled = ahl[...]
    top = dot(mt_high[...], scaled)
    low = dot(mt_low[...], ahl[:, :rank])
    back_raw = (top[:, :rank] + (top[:, rank:] + low)) * weight_x

    turned = inverse.T
    middle = (1.0 + COLLIDE) * factor + dot6(source.T, turned)
    moved = dot6(inverse, jnp.concatenate(slopes, axis=1))
    plus = dot6(jnp.concatenate([moved[:, d * rank : (d + 1) * rank] for d in range(3)], axis=0), turned)
    plus = [plus[d * rank : (d + 1) * rank] for d in range(3)]
    lnew = ref["lnew"]
    chunk = math.gcd(nodes, NVX * NVX // 4)
    gram_v = jnp.zeros((rank, rank), F32)
    mixed_v = jnp.zeros((rank, rank), F32)
    back = [-item.T for item in plus]
    for at_row in range(0, nodes, chunk):
        span = slice(at_row, at_row + chunk)
        node = base + at_row
        lnow = dot3(v_ref[span, :], middle)
        ahead = [node // (NVX * NVX) >= NVX // 2, node // NVX % NVX >= NVX // 2]
        sides = [jnp.where(ahead[d], plus[d], back[d]) for d in range(2)] + [plus[2], back[2]]
        sliding = dot3(lnow, jnp.concatenate(sides, axis=1))
        part = node_velocity(node + lax.broadcasted_iota(jnp.int32, (chunk, rank), 0))
        slide = part[0] * sliding[:, :rank] + part[1] * sliding[:, rank : 2 * rank]
        slide = slide + part[2] * jnp.where(part[2] > 0, sliding[:, 2 * rank : 3 * rank], sliding[:, 3 * rank :])
        mback = dot3(back_raw[span], turned)
        new = lnow + time_step * slide + COLLIDE * (mback - lnow)
        lnew[span, :] = new
        high, low = halves(new)
        rest = (new - high.astype(F32) - low.astype(F32)).astype(BF16)
        high_t, low_t = halves(new.T)
        both = dot(high_t, jnp.concatenate([high, low, rest], axis=1))
        gram_v = gram_v + both[:, :rank]
        mixed_v = mixed_v + (both[:, rank : 2 * rank] + (both[:, 2 * rank :] + 0.5 * dot(low_t, low)))
    gram_v = (gram_v + (mixed_v + mixed_v.T)) * weight_v

    half_rank = rank // 2
    lanes = lax.broadcasted_iota(jnp.int32, (half_rank // 2, rank), 1)
    corner = jnp.where(
        lanes < half_rank,
        pltpu.roll(gram_v[half_rank : half_rank + half_rank // 2], half_rank, 1),
        gram_v[half_rank + half_rank // 2 :],
    )
    gx, g1, g2, g3, go = ref["gx"], ref["g1"], ref["g2"], ref["g3"], ref["go"]
    gx[...] = jnp.concatenate([gram_v[:half_rank], corner], axis=0).reshape(gx.shape)
    copy = send(gx.at[1 - core], g1, ref["gcs"].at[0], ref["gcr"].at[0], pos.partner())
    copy.wait_recv()
    g2[slab] = gx[core] + g1[...]
    mine = g2.at[slab]
    copies = [
        send(mine, mine, ref["gss"].at[k - 1], ref["gsr"].at[k - 1], pos.slab_at(k)[1]) for k in range(1, slabs)
    ]
    ref["basis_x"][...] = dot3(advanced, turned)
    for copy in copies:
        copy.wait_recv()
    total = g2[0]
    for k in range(1, slabs):
        total = total + g2[k]
    g3[layer] = total
    mine = g3.at[layer]
    copies = [
        send(mine, mine, ref["gls"].at[k - 1], ref["glr"].at[k - 1], pos.across(k)) for k in range(1, layers)
    ]
    for copy in copies:
        copy.wait_recv()
    total = g3[0]
    for k in range(1, layers):
        total = total + g3[k]
    go[core] = total
    mine = go.at[core]
    send(mine, mine, ref["gcs"].at[1], ref["gcr"].at[1], pos.partner()).wait_recv()
    whole = go[...].reshape(half_rank + half_rank // 2, rank)
    corner = whole[half_rank:]
    gram_ref = ref["gram"]
    gram_ref[:half_rank] = whole[:half_rank]
    gram_ref[half_rank : half_rank + half_rank // 2] = pltpu.roll(corner, half_rank, 1)
    gram_ref[half_rank + half_rank // 2 :] = corner
    for copy in started:
        copy.wait_send()


def finish_kernel(gram, lnew, field, basis_x, coupling, basis_v, work, factor_buffer, out, sems):
    give = pltpu.make_async_copy(field, basis_x, sems.at[0])
    give.start()
    factor, inverse = factor_steps(work, gram[...])
    factor_buffer[...] = factor
    copies = [give, pltpu.make_async_copy(factor_buffer, coupling, sems.at[1])]
    copies[1].start()
    turned = inverse.T
    nodes = lnew.shape[0]
    count = sems.shape[0] - 2
    chunk = nodes // count
    for i in range(count):
        span = pl.ds(i * chunk, chunk)
        out[span, :] = dot3(lnew[span, :], turned)
        copies.append(pltpu.make_async_copy(out.at[span], basis_v.at[span], sems.at[2 + i]))
        copies[-1].start()
    for copy in copies:
        copy.wait()


def local(k_coeffs, v_basis):
    cells_x, cells_y, cells_z, rank = k_coeffs.shape
    slabs = lax.axis_size("slab")
    layers = lax.axis_size("brick") // 2
    members = 2 * slabs
    own = cells_x * cells_y * cells_z
    nodes = v_basis.shape[0]
    cells = own * members * layers
    share = 3 * rank // members
    part = rank // members
    pair = 2 * own
    devices = members * layers
    names = ["k", "v", "basis_x", "gram", "lnew"]
    scratch = []

    used = [0]

    def buffer(name, shape, dtype=F32):
        names.append(name)
        used[0] += math.prod(shape) * jnp.dtype(dtype).itemsize
        scratch.append(pltpu.VMEM(shape, dtype))

    def semaphores(name, *shape):
        names.append(name)
        scratch.append(pltpu.SemaphoreType.DMA(shape))

    def reduction(name, rows):
        buffer(name + "x", (2, slabs, rows, rank))
        buffer(name + "1", (slabs, rows, rank))
        buffer(name + "h", (slabs, rows, rank))
        buffer(name + "2", (slabs, rows, rank))
        buffer(name + "3", (layers, rows, rank))
        buffer(name + "o", (2, slabs, rows, rank))
        for stage, count in (("c", 2), ("s", slabs - 1), ("l", layers - 1), ("g", slabs - 1)):
            semaphores(name + stage + "s", count)
            semaphores(name + stage + "r", count)

    buffer("k_here", k_coeffs.shape)
    buffer("v_here", v_basis.shape)
    semaphores("insem", 2)
    buffer("vec_l", (layers, 8, rank))
    buffer("vec_m", (members, 8, rank))
    buffer("halo_a", (2, cells_y, cells_z, rank))
    buffer("halo_b", (2, cells_x, cells_z, rank))
    buffer("vt", (2 * rank, nodes), BF16)
    buffer("kpad", (pair, rank))
    buffer("par", (members, layers, 8, pair))
    buffer("mt_high", (nodes, cells), BF16)
    buffer("mt_low", (nodes, cells), BF16)
    buffer("mp", (slabs, layers, 2, own, rank))
    buffer("first", (slabs, layers, own, rank))
    buffer("half", (slabs, layers, own, rank))
    buffer("second", (slabs, layers, own, rank))
    buffer("quarter", (layers, own, rank))
    buffer("third", (layers, own, rank))
    buffer("trans", (6 * rank, rank))
    buffer("adv", (slabs, 2 * layers, cells_x, cells_y, cells_z, rank))
    buffer("at", (2 * rank, cells), BF16)
    buffer("ahl", (cells, 2 * rank), BF16)
    buffer("d_high", (cells, 3 * rank), BF16)
    buffer("d_low", (cells, 3 * rank), BF16)
    buffer("work", (rank, 2 * rank))
    reduction("t", share)
    reduction("r", part)
    packed = 3 * rank // 8
    buffer("gx", (2, packed, rank))
    buffer("g1", (packed, rank))
    buffer("g2", (slabs, packed, rank))
    buffer("g3", (layers, packed, rank))
    buffer("go", (2, packed, rank))
    for name, count in (("gc", 2), ("gs", slabs - 1), ("vl", layers - 1), ("vm", members - 1), ("p", devices - 1)):
        semaphores(name + "s", count)
        semaphores(name + "r", count)
    for name in ("gl", "z", "a"):
        semaphores(name + "s", layers - 1)
        semaphores(name + "r", layers - 1)
    semaphores("hs", 4)
    semaphores("hr", 4)
    for name, shape in (
        ("c", (slabs, layers // 2)),
        ("s", (slabs - 1, layers // 2)),
        ("b", (slabs - 1, layers)),
        ("d", (slabs, layers)),
    ):
        semaphores(name + "s", *shape)
        semaphores(name + "r", *shape)
    basis_x, gram, lnew = pl.pallas_call(
        functools.partial(step_kernel, tuple(names), slabs, layers),
        out_shape=(
            jax.ShapeDtypeStruct((own, rank), F32),
            jax.ShapeDtypeStruct((rank, rank), F32),
            jax.ShapeDtypeStruct(v_basis.shape, F32),
        ),
        in_specs=[HBM, HBM],
        out_specs=(VM, VM, VM),
        scratch_shapes=scratch,
        compiler_params=pltpu.CompilerParams(
            collective_id=1, has_side_effects=True, vmem_limit_bytes=min(62 * 2**20, used[0] + 14 * 2**20)
        ),
    )(pltpu.with_memory_space_constraint(k_coeffs, pltpu.HBM), pltpu.with_memory_space_constraint(v_basis, pltpu.HBM))
    chunks = 4
    basis_x, coupling, basis_v = pl.pallas_call(
        finish_kernel,
        out_shape=(
            jax.ShapeDtypeStruct((own, rank), F32),
            jax.ShapeDtypeStruct((rank, rank), F32),
            jax.ShapeDtypeStruct(v_basis.shape, F32),
        ),
        in_specs=[VM, VM, VM],
        out_specs=(HBM, HBM, HBM),
        scratch_shapes=[
            pltpu.VMEM((rank, 2 * rank), F32),
            pltpu.VMEM((rank, rank), F32),
            pltpu.VMEM(v_basis.shape, F32),
            pltpu.SemaphoreType.DMA((2 + chunks,)),
        ],
        compiler_params=pltpu.CompilerParams(vmem_limit_bytes=12 * 2**20),
    )(gram, lnew, basis_x)
    return basis_x.reshape(k_coeffs.shape), coupling, basis_v


def solution(mesh):
    return jax.shard_map(
        local,
        mesh=mesh,
        in_specs=(P("slab", "brick", None, None), P(("slab", "brick"), None)),
        out_specs=(P("slab", "brick", None, None), P(), P(("slab", "brick"), None)),
        check_vma=False,
    )
```

```python
import functools
import math

import jax
import jax.numpy as jnp
from jax import lax
from jax.experimental import pallas as pl
from jax.experimental.pallas import tpu as pltpu
from jax.sharding import PartitionSpec as P

NVX = 32

CFL = 0.9
VMAX = 6.0
COLLIDE = 0.3
RHO_MIN = 0.25
TEMP_MIN = 0.25
PRECISE = lax.Precision.HIGHEST
MESH = pl.DeviceIdType.MESH
VM = pl.BlockSpec(memory_space=pltpu.VMEM)
HBM = pl.BlockSpec(memory_space=pltpu.HBM)
F32 = jnp.float32
BF16 = jnp.bfloat16
BITS = NVX.bit_length() - 1


def halves(values):
    high = values.astype(BF16)
    return high, (values - high.astype(F32)).astype(BF16)


def dot(left, right):
    return jnp.dot(left, right, preferred_element_type=F32)


def dot_split(high, low, right):
    width = right.shape[1]
    right_high, right_low = halves(right)
    both = dot(high, jnp.concatenate([right_high, right_low], axis=1))
    return both[:, :width] + (both[:, width:] + dot(low, right_high))


def dot3(left, right):
    depth, width = right.shape
    high, low = halves(left)
    if depth != 128:
        return dot_split(high, low, right)
    right_high, right_low = halves(right)
    top = jnp.concatenate([right_high, right_low], axis=1)
    under = jnp.concatenate([right_high, jnp.zeros_like(right_low)], axis=1)
    both = dot(jnp.concatenate([high, low], axis=1), jnp.concatenate([top, under], axis=0))
    return both[:, :width] + both[:, width:]


def thirds(values):
    high = values.astype(BF16)
    rest = values - high.astype(F32)
    middle = rest.astype(BF16)
    return high, middle, (rest - middle.astype(F32)).astype(BF16)


def dot6(left, right):
    width = right.shape[1]
    high, middle, low = thirds(left)
    right_high, right_middle, right_low = thirds(right)
    top = jnp.concatenate([right_high, right_low], axis=1)
    under = jnp.concatenate([right_high, right_middle], axis=1)
    both = dot(jnp.concatenate([high, middle], axis=1), jnp.concatenate([top, under], axis=0))
    cross = dot(jnp.concatenate([high, low], axis=1), jnp.concatenate([right_middle, right_high], axis=0))
    return both[:, :width] + (cross + both[:, width:])


def node_velocity(indices):
    spacing = 2.0 * VMAX / NVX
    last = NVX - 1
    parts = (
        lax.shift_right_logical(indices, 2 * BITS),
        lax.shift_right_logical(indices, BITS) & last,
        indices & last,
    )
    return [-VMAX + (part.astype(F32) + 0.5) * spacing for part in parts]


class Sum:
    def __init__(self, send, pos, ref, name):
        self.send, self.pos = send, pos
        self.x, self.first, self.half, self.second, self.third, self.out = [
            ref[name + part] for part in ("x", "1", "h", "2", "3", "o")
        ]
        self.sems = [(ref[name + part + "s"], ref[name + part + "r"]) for part in ("c", "s", "l", "g")]

    def copy(self, source, target, stage, index, device):
        sent, received = self.sems[stage]
        return self.send(source, target, sent.at[index], received.at[index], device)

    def wait(self):
        for copy in self.copies:
            copy.wait_recv()

    def start(self):
        self.copies = [self.copy(self.x.at[1 - self.pos.core], self.first, 0, 0, self.pos.partner())]

    def scatter(self):
        self.wait()
        slab = self.pos.slab
        self.half[...] = self.x[self.pos.core] + self.first[...]
        self.second[slab] = self.half[slab]
        self.copies = []
        for k in range(1, self.pos.slabs):
            to, device = self.pos.slab_at(k)
            self.copies.append(self.copy(self.half.at[to], self.second.at[slab], 1, k - 1, device))

    def cross(self):
        self.wait()
        total = self.second[0]
        for k in range(1, self.pos.slabs):
            total = total + self.second[k]
        self.third[self.pos.layer] = total
        mine = self.third.at[self.pos.layer]
        self.copies = [self.copy(mine, mine, 2, k - 1, self.pos.across(k)) for k in range(1, self.pos.layers)]

    def collect(self):
        self.wait()
        total = self.third[0]
        for k in range(1, self.pos.layers):
            total = total + self.third[k]
        self.out[self.pos.core, self.pos.slab] = total
        mine = self.out.at[self.pos.core, self.pos.slab]
        self.copies = [self.copy(mine, mine, 3, k - 1, self.pos.slab_at(k)[1]) for k in range(1, self.pos.slabs)]

    def share(self):
        self.wait()
        mine = self.out.at[self.pos.core]
        self.copies = [self.copy(mine, mine, 0, 1, self.pos.partner())]

    def finish(self):
        self.wait()


class Position:
    def __init__(self, slabs, layers):
        self.slabs, self.layers, self.members = slabs, layers, 2 * slabs
        brick = lax.axis_index("brick")
        self.brick = brick
        self.core, self.layer = lax.rem(brick, 2), lax.div(brick, 2)
        self.slab = lax.axis_index("slab")
        self.me = 2 * self.slab + self.core

    def member(self, k):
        to = lax.rem(self.me + k, self.members)
        return to, (lax.div(to, 2), 2 * self.layer + lax.rem(to, 2))

    def mate(self, k):
        if self.layers != 4:
            return lax.rem(self.layer + k, self.layers)
        if k == 1:
            return self.layer + 1 - 2 * lax.rem(self.layer, 2)
        return lax.rem(self.layer + 2, self.layers) if k == 2 else self.layers - 1 - self.layer

    def source(self, k):
        if k == 0:
            return self.layer
        return self.mate(k) if self.layers == 4 else lax.rem(self.layer + self.layers - k, self.layers)

    def across(self, k):
        return (self.slab, 2 * lax.rem(self.layer + k, self.layers) + self.core)

    def others(self):
        bricks = 2 * self.layers
        count = self.slabs * bricks
        at = self.slab * bricks + self.brick
        for k in range(1, count):
            to = lax.rem(at + k, count)
            yield k - 1, (lax.div(to, bricks), lax.rem(to, bricks))

    def partner(self):
        return (self.slab, 2 * self.layer + 1 - self.core)

    def slab_at(self, k):
        to = lax.rem(self.slab + k, self.slabs)
        return to, (to, self.brick)

    def slab_mate(self, k):
        if self.slabs != 4 or k == 0:
            return lax.rem(self.slab + k, self.slabs)
        if k == 1:
            return self.slabs - 1 - self.slab
        return self.slab + 1 - 2 * lax.rem(self.slab, 2) if k == 2 else lax.rem(self.slab + 2, self.slabs)

    def slab_source(self, k):
        return self.slab_mate(k) if self.slabs == 4 else lax.rem(self.slab + self.slabs - k, self.slabs)

    def brick_at(self, k):
        bricks = 2 * self.layers
        return (self.slab, lax.rem(self.brick + k + bricks, bricks))


def factor_steps(work, matrix, fillers=()):
    size = matrix.shape[0]
    block, panel = 8, 16
    row = lax.broadcasted_iota(jnp.int32, (size, size), 0)
    column = lax.broadcasted_iota(jnp.int32, (size, size), 1)
    work[:, :size] = matrix
    work[:, size:] = jnp.where(row == column, 1.0, 0.0)
    sub = lax.broadcasted_iota(jnp.int32, (block, size), 0)
    narrow, wide = (block, size), (block, 2 * size)
    fillers = list(fillers)
    for start in range(0, size, panel):
        if fillers:
            fillers.pop(0)()
        rows = [work[start : start + block, :], work[start + block : start + panel, :]]
        for b in range(2):
            at = start + b * block
            columns = {
                (r, m): jnp.broadcast_to(rows[r][:, at + m : at + m + 1], narrow)
                for r in range(b, 2)
                for m in range(block)
            }
            entry = {
                (i, m): jnp.broadcast_to(columns[b, m][i : i + 1], narrow) for m in range(block) for i in range(m, block)
            }
            scales = entry[0, 0]
            for k in range(block):
                scale = lax.rsqrt(entry[k, k])
                invert = scale * scale
                scales = scale if k == 0 else jnp.where(sub == k, scale, scales)
                ratios = {r: columns[r, k] * invert for r in range(b, 2)}
                ratios[b] = jnp.where(sub > k, ratios[b], 0.0)
                for m in range(k + 1, block):
                    factor = entry[m, k] * invert
                    for i in range(m, block):
                        entry[i, m] = entry[i, m] - entry[i, k] * factor
                for r in range(b, 2):
                    for m in range(k + 1, block):
                        columns[r, m] = columns[r, m] - ratios[r] * entry[m, k]
                pivot = jnp.broadcast_to(rows[b][k : k + 1], wide)
                for r in range(b, 2):
                    rows[r] = rows[r] - jnp.concatenate([ratios[r], ratios[r]], axis=1) * pivot
            rows[b] = rows[b] * jnp.concatenate([scales, scales], axis=1)
        both = jnp.concatenate(rows, axis=0)
        work[start : start + panel, :] = both
        if start + panel < size:
            high = both.astype(BF16).astype(F32)
            low = (both - high).astype(BF16).astype(F32)
            rest = both - high - low
            left = jnp.concatenate([item[:, :size] for item in (high, high, low, high, rest, low)], axis=0)
            right = jnp.concatenate([item.astype(BF16) for item in (high, low, high, rest, high, low)], axis=0)
            tall = left.T[start + panel :, :].astype(BF16)
            work[start + panel :, :] = work[start + panel :, :] - dot(tall, right)
    for filler in fillers:
        filler()
    factor = jnp.where(column <= row, work[:, :size].T, 0.0)
    inverse = jnp.where(column <= row, work[:, size:], 0.0)
    return factor, inverse


def step_kernel(names, slabs, layers, *refs):
    ref = dict(zip(names, refs))
    pos = Position(slabs, layers)
    core, slab, layer, brick, me = pos.core, pos.slab, pos.layer, pos.brick, pos.me
    members, bricks = pos.members, 2 * layers
    k_ref, v_ref = ref["k_here"], ref["v_here"]
    inputs = [
        pltpu.make_async_copy(ref["k"], k_ref, ref["insem"].at[0]),
        pltpu.make_async_copy(ref["v"], v_ref, ref["insem"].at[1]),
    ]
    for copy in inputs:
        copy.start()
    cells_x, cells_y, cells_z, rank = k_ref.shape
    own = cells_x * cells_y * cells_z
    nodes = v_ref.shape[0]
    lengths = (cells_x * slabs, cells_y * bricks, cells_z)
    cells = lengths[0] * lengths[1] * lengths[2]
    time_step = CFL / (VMAX * (lengths[0] + lengths[1] + lengths[2]))
    weight_x = 1.0 / cells
    weight_v = (2.0 * VMAX / NVX) ** 3
    base = (slab * bricks + brick) * nodes
    started = []

    def send(source, target, send_sem, recv_sem, device):
        copy = pltpu.make_async_remote_copy(
            src_ref=source,
            dst_ref=target,
            send_sem=send_sem,
            recv_sem=recv_sem,
            device_id=device,
            device_id_type=MESH,
        )
        copy.start()
        started.append(copy)
        return copy

    barrier = pltpu.get_barrier_semaphore()
    peers = [pos.member(k)[1] for k in range(1, members)] + [pos.across(k) for k in range(1, layers)]
    for peer in peers:
        pl.semaphore_signal(barrier, inc=1, device_id=peer, device_id_type=MESH)

    lane = lax.broadcasted_iota(jnp.int32, (8, nodes), 1)
    sub = lax.broadcasted_iota(jnp.int32, (8, nodes), 0)
    velocity = node_velocity(base + lane)
    square = velocity[0] * velocity[0] + velocity[1] * velocity[1] + velocity[2] * velocity[2]
    weights = jnp.where(sub == 0, 1.0, jnp.where(sub == 4, square, 0.0))
    upward = jnp.zeros_like(weights)
    for d in range(3):
        weights = jnp.where(sub == d + 1, velocity[d], weights)
        upward = jnp.where(sub == d + 5, jnp.maximum(velocity[d], 0.0), upward)
    for copy in inputs:
        copy.wait()
    values = v_ref[...]
    v_high, v_low = halves(values)
    v_rest = (values - v_high.astype(F32) - v_low.astype(F32)).astype(BF16)
    sums = dot(jnp.concatenate(halves(weights), axis=0), jnp.concatenate([v_high, v_low, v_rest], axis=1))
    sums = sums[:8] + sums[8:]
    squares = dot(upward.astype(BF16), jnp.concatenate(halves(values * values), axis=1))
    partial = sums[:, :rank] + (sums[:, rank : 2 * rank] + sums[:, 2 * rank :])
    partial = (partial + (squares[:, :rank] + squares[:, rank:])) * weight_v
    vec_l, vec_m = ref["vec_l"], ref["vec_m"]
    vec_l[layer] = partial

    turned_v = values.T
    vt_high, vt_low = halves(turned_v)
    vt = ref["vt"]
    vt[:rank] = vt_high
    vt[rank:] = vt_low
    v_both = jnp.concatenate([v_high, v_low], axis=1)
    row = lax.broadcasted_iota(jnp.int32, (rank, rank), 0)
    column = lax.broadcasted_iota(jnp.int32, (rank, rank), 1)
    packed = []

    def pack(d):
        sides = []
        for side in (jnp.maximum(velocity[d][:1], 0.0), jnp.minimum(velocity[d][:1], 0.0)):
            high, low = halves(turned_v * (side * weight_v))
            both = dot(high, v_both)
            sides.append(both[:, :rank] + (both[:, rank:] + dot(low, v_high)))
        packed.append(jnp.where(row > column, sides[0], sides[1]))

    for d in range(3):
        pack(d)
    ref["tx"][...] = jnp.concatenate(packed, axis=0).reshape(ref["tx"].shape)
    transport_sum = Sum(send, pos, ref, "t")
    pl.semaphore_wait(barrier, len(peers))
    mine = vec_l.at[layer]
    copies = [
        send(mine, mine, ref["vls"].at[k - 1], ref["vlr"].at[k - 1], pos.across(k)) for k in range(1, layers)
    ]
    transport_sum.start()
    transport_sum.scatter()
    for copy in copies:
        copy.wait_recv()
    total = vec_l[0]
    for k in range(1, layers):
        total = total + vec_l[k]
    vec_m[me] = total
    mine = vec_m.at[me]
    copies = [
        send(mine, mine, ref["vms"].at[k - 1], ref["vmr"].at[k - 1], pos.member(k)[1]) for k in range(1, members)
    ]
    transport_sum.cross()
    for copy in copies:
        copy.wait_recv()
    vectors = vec_m[0]
    for k in range(1, members):
        vectors = vectors + vec_m[k]

    own_k = k_ref[...].reshape(own, rank)
    kpad = ref["kpad"]
    kpad[...] = jnp.zeros_like(kpad)
    kpad[pl.ds(pl.multiple_of(core * own, 8), own), :] = own_k
    moments = lax.dot_general(
        vectors, kpad[...], (((1,), (1,)), ((), ())), precision=PRECISE, preferred_element_type=F32
    )
    pair = 2 * own
    density = jnp.maximum(moments[0:1], RHO_MIN)
    drift = [moments[d : d + 1] / density for d in range(1, 4)]
    bulk = drift[0] * drift[0] + drift[1] * drift[1] + drift[2] * drift[2]
    temper = jnp.maximum((moments[4:5] / density - bulk) / 3.0, TEMP_MIN)
    wide = 2.0 * math.pi * temper
    amplitude = density / (wide * jnp.sqrt(wide))
    state = jnp.zeros((8, pair), F32)
    sub_pair = lax.broadcasted_iota(jnp.int32, (8, pair), 0)
    lane_pair = lax.broadcasted_iota(jnp.int32, (8, pair), 1)
    for i, item in enumerate(drift + [-0.5 / temper, amplitude]):
        state = jnp.where(sub_pair == i, item, state)
    inside = (lane_pair >= core * own) & (lane_pair < (core + 1) * own)
    par = ref["par"]
    par[me, layer] = jnp.where(inside, state, 0.0)
    mine = par.at[me, layer, pl.ds(0, 5)]
    copies = [send(mine, mine, ref["ps"].at[i], ref["pr"].at[i], device) for i, device in pos.others()]
    halo_a, halo_b = ref["halo_a"], ref["halo_b"]
    halos = [
        send(k_ref.at[cells_x - 1], halo_a.at[0], ref["hs"].at[0], ref["hr"].at[0], pos.slab_at(1)[1]),
        send(k_ref.at[0], halo_a.at[1], ref["hs"].at[1], ref["hr"].at[1], pos.slab_at(slabs - 1)[1]),
        send(k_ref.at[:, cells_y - 1], halo_b.at[0], ref["hs"].at[2], ref["hr"].at[2], pos.brick_at(1)),
        send(k_ref.at[:, 0], halo_b.at[1], ref["hs"].at[3], ref["hr"].at[3], pos.brick_at(-1)),
    ]
    transport_sum.collect()
    for copy in copies:
        copy.wait_recv()

    mt_high, mt_low = ref["mt_high"], ref["mt_low"]
    mp, first, half, second, third = ref["mp"], ref["first"], ref["half"], ref["second"], ref["third"]
    group = math.gcd(nodes, NVX)
    groups = nodes // group
    width = 2 * pair
    slots = layers // 2
    fast_v = node_velocity(base + lax.broadcasted_iota(jnp.int32, (group, width), 0))
    slow_v = node_velocity(base + group * lax.broadcasted_iota(jnp.int32, (groups, width), 0))

    def project(to, slot):
        blocks = [par[2 * to, 2 * slot + i] + par[2 * to + 1, 2 * slot + i] for i in range(2)]
        state = jnp.concatenate(blocks, axis=1)
        u = [state[d : d + 1] for d in range(3)]
        rate, scale = state[3:4], state[4:5]
        fast = jnp.exp((fast_v[2] - u[2]) ** 2 * rate)
        slow = jnp.exp(((slow_v[0] - u[0]) ** 2 + (slow_v[1] - u[1]) ** 2) * rate) * scale
        places = [pl.ds(pl.multiple_of(((2 * slot + i) * slabs + to) * pair, pair), pair) for i in range(2)]
        for t in range(groups):
            high, low = halves(fast * slow[t : t + 1])
            for i, place in enumerate(places):
                mt_high[t * group : (t + 1) * group, place] = high[:, i * pair : (i + 1) * pair]
                mt_low[t * group : (t + 1) * group, place] = low[:, i * pair : (i + 1) * pair]
        high = dot(vt[...], jnp.concatenate([mt_high[:, place] for place in places], axis=1))
        low = dot(vt[:rank], jnp.concatenate([mt_low[:, place] for place in places], axis=1))
        result = ((high[:rank] + (high[rank:] + low)) * weight_v).T
        for i in range(2):
            for c in range(2):
                at = (2 * i + c) * own
                mp[to, 2 * slot + i, c] = result[at : at + own]

    def hand_over(k, slot, to):
        at = pl.ds(2 * slot, 2)
        return send(
            mp.at[to, at, 1 - core], first.at[to, at], ref["cs"].at[k, slot], ref["cr"].at[k, slot], pos.partner()
        )

    over = []

    def hand_on(k, slot, to, copy):
        copy.wait_recv()
        at = pl.ds(2 * slot, 2)
        if k == 0:
            second[slab, at] = mp[slab, at, core] + first[slab, at]
            return
        half[to, at] = mp[to, at, core] + first[to, at]
        over.append(
            send(half.at[to, at], second.at[slab, at], ref["ss"].at[k - 1, slot], ref["sr"].at[k - 1, slot], (to, brick))
        )

    waiting = []
    for k in list(range(1, slabs)) + [0]:
        to = pos.slab_mate(k)
        for slot in range(slots):
            project(to, slot)
            if k == 1 and slot == 0:
                transport_sum.share()
            copy = hand_over(k, slot, to)
            if len(waiting) >= 1:
                hand_on(*waiting.pop(0))
            waiting.append((k, slot, to, copy))

    for copy in waiting:
        hand_on(*copy)

    transport_sum.finish()
    packed = ref["to"][...].reshape(3 * rank, rank)
    trans = ref["trans"]
    for d in range(3):
        block = packed[d * rank : (d + 1) * rank]
        flipped = block.T
        diagonal = jnp.where(row == column, vectors[d + 5 : d + 6], 0.0)
        trans[d * rank : (d + 1) * rank] = jnp.where(row <= column, block, flipped)
        trans[(d + 3) * rank : (d + 4) * rank] = jnp.where(
            row > column, block, jnp.where(row < column, flipped, diagonal)
        )
    for copy in halos:
        copy.wait_recv()
    field = k_ref[...]
    after_a = jnp.concatenate([field[1:], halo_a[1:2]], axis=0)
    before_a = jnp.concatenate([halo_a[0:1], field[:-1]], axis=0)
    after_b = jnp.concatenate([field[:, 1:], halo_b[1].reshape(cells_x, 1, cells_z, rank)], axis=1)
    before_b = jnp.concatenate([halo_b[0].reshape(cells_x, 1, cells_z, rank), field[:, :-1]], axis=1)

    def next_third(flat):
        count = flat.shape[0]
        index = lax.broadcasted_iota(jnp.int32, flat.shape, 0)
        return jnp.where(
            lax.rem(index, cells_z) == cells_z - 1,
            pltpu.roll(flat, cells_z - 1, 0),
            pltpu.roll(flat, count - 1, 0),
        )

    def last_third(flat):
        count = flat.shape[0]
        index = lax.broadcasted_iota(jnp.int32, flat.shape, 0)
        return jnp.where(
            lax.rem(index, cells_z) == 0,
            pltpu.roll(flat, count - cells_z + 1, 0),
            pltpu.roll(flat, 1, 0),
        )

    fields = [
        (after_a.reshape(own, rank) - own_k) * lengths[0],
        (after_b.reshape(own, rank) - own_k) * lengths[1],
        (next_third(own_k) - own_k) * lengths[2],
        (own_k - before_a.reshape(own, rank)) * lengths[0],
        (own_k - before_b.reshape(own, rank)) * lengths[1],
        (own_k - last_third(own_k)) * lengths[2],
    ]
    flux = dot3(jnp.concatenate(fields, axis=1), trans[...])
    kept = own_k - time_step * flux - COLLIDE * own_k

    for copy in over:
        copy.wait_recv()
    total = second[0]
    for k in range(1, slabs):
        total = total + second[k]
    quarter = ref["quarter"]
    quarter[...] = total
    copies = []
    for k in range(1, layers):
        to = lax.rem(layer + k, layers)
        copies.append(
            send(quarter.at[to], third.at[layer], ref["zs"].at[k - 1], ref["zr"].at[k - 1], pos.across(k))
        )
    third[layer] = quarter[layer]
    for copy in copies:
        copy.wait_recv()
    mproj = third[0]
    for k in range(1, layers):
        mproj = mproj + third[k]
    advanced = kept + COLLIDE * mproj

    adv = ref["adv"]
    adv[layer, slab, core] = advanced.reshape(cells_x, cells_y, cells_z, rank)
    here = adv.at[layer, slab, core]

    def to_slabs(block, j):
        return [
            send(block, block, ref["bs"].at[k - 1, j], ref["br"].at[k - 1, j], (pos.slab_mate(k), brick))
            for k in range(1, slabs)
        ]

    along = [
        send(here, here, ref["as"].at[k - 1], ref["ar"].at[k - 1], (slab, 2 * pos.mate(k) + core))
        for k in range(1, layers)
    ]
    crossing = [to_slabs(here, 0)]
    last = [[send(here, here, ref["ds"].at[0, 0], ref["dr"].at[0, 0], pos.partner())]]
    raw_sum = Sum(send, pos, ref, "r")
    ref["rx"][...] = dot3(advanced.T, mproj).reshape(ref["rx"].shape)
    raw_sum.start()
    raw_sum.scatter()
    for j in range(1, layers):
        along[j - 1].wait_recv()
        block = adv.at[pos.source(j), slab, core]
        crossing.append(to_slabs(block, j))
        last.append([send(block, block, ref["ds"].at[0, j], ref["dr"].at[0, j], pos.partner())])

    at, ahl, back = ref["at"], ref["ahl"], ref["back"]
    d_high, d_low, gram_l = ref["d_high"], ref["d_low"], ref["gram_l"]
    plane = cells // layers

    def relay(j):
        for k in range(1, slabs):
            crossing[j][k - 1].wait_recv()
            block = adv.at[pos.source(j), pos.slab_source(k), core]
            last[j].append(send(block, block, ref["ds"].at[k, j], ref["dr"].at[k, j], pos.partner()))

    def store_slopes(span, d, values):
        high, low = halves(values)
        d_high[span, d * rank : (d + 1) * rank] = high
        d_low[span, d * rank : (d + 1) * rank] = low

    def take(j):
        for copy in last[j]:
            copy.wait_recv()
        from_layer = pos.source(j)
        block = adv[from_layer]
        span = pl.ds(pl.multiple_of(from_layer * plane, plane), plane)
        flat = block.reshape(plane, rank)
        high, low = halves(flat)
        ahl[span, :rank] = high
        ahl[span, rank:] = low
        high_t, low_t = halves(flat.T)
        at[:rank, span] = high_t
        at[rank:, span] = low_t
        gram_l[from_layer] = dot(high_t, jnp.concatenate([high, low], axis=1))
        across = jnp.concatenate([block[1:, :, :1], block[:1, :, :1]], axis=0)
        after = jnp.concatenate([block[:, :, 1:], across], axis=2)
        store_slopes(span, 0, after.reshape(plane, rank) - flat)
        store_slopes(span, 2, next_third(flat) - flat)

    def project_back(j, rows):
        span = pl.ds(pl.multiple_of(pos.source(j) * plane, plane), plane)
        top = dot(mt_high[rows, span], ahl[span, :])
        part = top[:, :rank] + (top[:, rank:] + dot(mt_low[rows, span], ahl[span, :rank]))
        back[rows, :] = part if j == 0 else back[rows, :] + part

    quarters = [slice(i * (nodes // 4), (i + 1) * (nodes // 4)) for i in range(4)]
    for j in range(layers):
        relay(j)
        if j == 1:
            raw_sum.cross()
        if j > 0:
            take(j - 1)
            for rows in quarters:
                project_back(j - 1, rows)
    raw_sum.collect()
    take(layers - 1)
    total = gram_l[0]
    for k in range(1, layers):
        total = total + gram_l[k]
    mixed = total[:, rank:]
    gram = (total[:, :rank] + (mixed + mixed.T)) * weight_x
    for k in range(layers):
        block, following = adv[k], adv[(k + 1) % layers]
        ups = [
            jnp.concatenate([block[:, 0, :, 1:], block[:, 1, :, :1]], axis=2),
            jnp.concatenate([block[:, 1, :, 1:], following[:, 0, :, :1]], axis=2),
        ]
        for c in range(2):
            difference = (ups[c] - block[:, c]).reshape(slabs, own, rank)
            for i in range(slabs):
                first_row = k * plane + (2 * i + c) * own
                store_slopes(slice(first_row, first_row + own), 1, difference[i])
    slopes = [None] * 3

    def slope_product(d):
        columns = slice(d * rank, (d + 1) * rank)
        both = dot(at[...], d_high[:, columns])
        both = both[:rank] + (both[rank:] + dot(at[:rank], d_low[:, columns]))
        slopes[d] = both * (lengths[d] * weight_x)

    sources = []

    def drive():
        sources.append(
            time_step * dot6(jnp.concatenate(slopes + [-item.T for item in slopes], axis=1), trans[...])
        )

    back_last = [functools.partial(project_back, layers - 1, rows) for rows in quarters]
    fillers = [functools.partial(slope_product, d) for d in (0, 2, 1)] + [drive]
    fillers += [back_last[0], lambda: (raw_sum.share(), back_last[1]()), back_last[2]]
    fillers += [lambda: (raw_sum.finish(), back_last[3]())]
    factor, inverse = factor_steps(ref["work"], gram, fillers)
    source = sources[0] - COLLIDE * weight_x * ref["ro"][...].reshape(rank, rank)

    turned = inverse.T
    middle = (1.0 + COLLIDE) * factor + dot6(source.T, turned)
    moved = dot6(inverse, jnp.concatenate(slopes, axis=1))
    plus = dot6(jnp.concatenate([moved[:, d * rank : (d + 1) * rank] for d in range(3)], axis=0), turned)
    plus = [plus[d * rank : (d + 1) * rank] for d in range(3)]
    lnew = ref["lnew"]
    chunk = math.gcd(nodes, NVX * NVX // 4)
    gram_v = jnp.zeros((rank, rank), F32)
    mixed_v = jnp.zeros((rank, rank), F32)
    behind = [-item.T for item in plus]
    for at_row in range(0, nodes, chunk):
        span = slice(at_row, at_row + chunk)
        node = base + at_row
        lnow = dot3(v_ref[span, :], middle)
        ahead = [node // (NVX * NVX) >= NVX // 2, node // NVX % NVX >= NVX // 2]
        sides = [jnp.where(ahead[d], plus[d], behind[d]) for d in range(2)] + [plus[2], behind[2]]
        sliding = dot3(lnow, jnp.concatenate(sides, axis=1))
        part = node_velocity(node + lax.broadcasted_iota(jnp.int32, (chunk, rank), 0))
        slide = part[0] * sliding[:, :rank] + part[1] * sliding[:, rank : 2 * rank]
        slide = slide + part[2] * jnp.where(part[2] > 0, sliding[:, 2 * rank : 3 * rank], sliding[:, 3 * rank :])
        mback = dot3(back[span, :] * weight_x, turned)
        new = lnow + time_step * slide + COLLIDE * (mback - lnow)
        lnew[span, :] = new
        high, low = halves(new)
        rest = (new - high.astype(F32) - low.astype(F32)).astype(BF16)
        high_t, low_t = halves(new.T)
        both = dot(high_t, jnp.concatenate([high, low, rest], axis=1))
        gram_v = gram_v + both[:, :rank]
        mixed_v = mixed_v + (both[:, rank : 2 * rank] + (both[:, 2 * rank :] + 0.5 * dot(low_t, low)))
    gram_v = (gram_v + (mixed_v + mixed_v.T)) * weight_v

    half_rank = rank // 2
    lanes = lax.broadcasted_iota(jnp.int32, (half_rank // 2, rank), 1)
    corner = jnp.where(
        lanes < half_rank,
        pltpu.roll(gram_v[half_rank : half_rank + half_rank // 2], half_rank, 1),
        gram_v[half_rank + half_rank // 2 :],
    )
    gx, g1, g2, g3, go = ref["gx"], ref["g1"], ref["g2"], ref["g3"], ref["go"]
    gx[...] = jnp.concatenate([gram_v[:half_rank], corner], axis=0).reshape(gx.shape)
    copy = send(gx.at[1 - core], g1, ref["gcs"].at[0], ref["gcr"].at[0], pos.partner())
    copy.wait_recv()
    g2[slab] = gx[core] + g1[...]
    mine = g2.at[slab]
    copies = [
        send(mine, mine, ref["gss"].at[k - 1], ref["gsr"].at[k - 1], pos.slab_at(k)[1]) for k in range(1, slabs)
    ]
    ref["basis_x"][...] = dot3(advanced, turned)
    for copy in copies:
        copy.wait_recv()
    total = g2[0]
    for k in range(1, slabs):
        total = total + g2[k]
    g3[layer] = total
    mine = g3.at[layer]
    copies = [
        send(mine, mine, ref["gls"].at[k - 1], ref["glr"].at[k - 1], pos.across(k)) for k in range(1, layers)
    ]
    for copy in copies:
        copy.wait_recv()
    total = g3[0]
    for k in range(1, layers):
        total = total + g3[k]
    go[core] = total
    mine = go.at[core]
    send(mine, mine, ref["gcs"].at[1], ref["gcr"].at[1], pos.partner()).wait_recv()
    whole = go[...].reshape(half_rank + half_rank // 2, rank)
    corner = whole[half_rank:]
    gram_ref = ref["gram"]
    gram_ref[:half_rank] = whole[:half_rank]
    gram_ref[half_rank : half_rank + half_rank // 2] = pltpu.roll(corner, half_rank, 1)
    gram_ref[half_rank + half_rank // 2 :] = corner
    for copy in started:
        copy.wait_send()


def finish_kernel(gram, lnew, field, basis_x, coupling, basis_v, work, factor_buffer, out, sems):
    give = pltpu.make_async_copy(field, basis_x, sems.at[0])
    give.start()
    factor, inverse = factor_steps(work, gram[...])
    factor_buffer[...] = factor
    copies = [give, pltpu.make_async_copy(factor_buffer, coupling, sems.at[1])]
    copies[1].start()
    turned = inverse.T
    nodes = lnew.shape[0]
    count = sems.shape[0] - 2
    chunk = nodes // count
    for i in range(count):
        span = pl.ds(i * chunk, chunk)
        out[span, :] = dot3(lnew[span, :], turned)
        copies.append(pltpu.make_async_copy(out.at[span], basis_v.at[span], sems.at[2 + i]))
        copies[-1].start()
    for copy in copies:
        copy.wait()


def local(k_coeffs, v_basis):
    cells_x, cells_y, cells_z, rank = k_coeffs.shape
    slabs = lax.axis_size("slab")
    layers = lax.axis_size("brick") // 2
    members = 2 * slabs
    own = cells_x * cells_y * cells_z
    nodes = v_basis.shape[0]
    cells = own * members * layers
    share = 3 * rank // members
    part = rank // members
    pair = 2 * own
    devices = members * layers
    names = ["k", "v", "basis_x", "gram", "lnew"]
    scratch = []

    used = [0]

    def buffer(name, shape, dtype=F32):
        names.append(name)
        used[0] += math.prod(shape) * jnp.dtype(dtype).itemsize
        scratch.append(pltpu.VMEM(shape, dtype))

    def semaphores(name, *shape):
        names.append(name)
        scratch.append(pltpu.SemaphoreType.DMA(shape))

    def reduction(name, rows):
        buffer(name + "x", (2, slabs, rows, rank))
        buffer(name + "1", (slabs, rows, rank))
        buffer(name + "h", (slabs, rows, rank))
        buffer(name + "2", (slabs, rows, rank))
        buffer(name + "3", (layers, rows, rank))
        buffer(name + "o", (2, slabs, rows, rank))
        for stage, count in (("c", 2), ("s", slabs - 1), ("l", layers - 1), ("g", slabs - 1)):
            semaphores(name + stage + "s", count)
            semaphores(name + stage + "r", count)

    buffer("k_here", k_coeffs.shape)
    buffer("v_here", v_basis.shape)
    semaphores("insem", 2)
    buffer("vec_l", (layers, 8, rank))
    buffer("vec_m", (members, 8, rank))
    buffer("halo_a", (2, cells_y, cells_z, rank))
    buffer("halo_b", (2, cells_x, cells_z, rank))
    buffer("vt", (2 * rank, nodes), BF16)
    buffer("kpad", (pair, rank))
    buffer("par", (members, layers, 8, pair))
    buffer("mt_high", (nodes, cells), BF16)
    buffer("mt_low", (nodes, cells), BF16)
    buffer("mp", (slabs, layers, 2, own, rank))
    buffer("first", (slabs, layers, own, rank))
    buffer("half", (slabs, layers, own, rank))
    buffer("second", (slabs, layers, own, rank))
    buffer("quarter", (layers, own, rank))
    buffer("third", (layers, own, rank))
    buffer("trans", (6 * rank, rank))
    buffer("adv", (layers, slabs, 2, cells_x, cells_y, cells_z, rank))
    buffer("back", (nodes, rank))
    buffer("gram_l", (layers, rank, 2 * rank))
    buffer("at", (2 * rank, cells), BF16)
    buffer("ahl", (cells, 2 * rank), BF16)
    buffer("d_high", (cells, 3 * rank), BF16)
    buffer("d_low", (cells, 3 * rank), BF16)
    buffer("work", (rank, 2 * rank))
    reduction("t", share)
    reduction("r", part)
    packed = 3 * rank // 8
    buffer("gx", (2, packed, rank))
    buffer("g1", (packed, rank))
    buffer("g2", (slabs, packed, rank))
    buffer("g3", (layers, packed, rank))
    buffer("go", (2, packed, rank))
    for name, count in (("gc", 2), ("gs", slabs - 1), ("vl", layers - 1), ("vm", members - 1), ("p", devices - 1)):
        semaphores(name + "s", count)
        semaphores(name + "r", count)
    for name in ("gl", "z", "a"):
        semaphores(name + "s", layers - 1)
        semaphores(name + "r", layers - 1)
    semaphores("hs", 4)
    semaphores("hr", 4)
    for name, shape in (
        ("c", (slabs, layers // 2)),
        ("s", (slabs - 1, layers // 2)),
        ("b", (slabs - 1, layers)),
        ("d", (slabs, layers)),
    ):
        semaphores(name + "s", *shape)
        semaphores(name + "r", *shape)
    basis_x, gram, lnew = pl.pallas_call(
        functools.partial(step_kernel, tuple(names), slabs, layers),
        out_shape=(
            jax.ShapeDtypeStruct((own, rank), F32),
            jax.ShapeDtypeStruct((rank, rank), F32),
            jax.ShapeDtypeStruct(v_basis.shape, F32),
        ),
        in_specs=[HBM, HBM],
        out_specs=(VM, VM, VM),
        scratch_shapes=scratch,
        compiler_params=pltpu.CompilerParams(
            collective_id=1, has_side_effects=True, vmem_limit_bytes=min(62 * 2**20, used[0] + 14 * 2**20)
        ),
    )(pltpu.with_memory_space_constraint(k_coeffs, pltpu.HBM), pltpu.with_memory_space_constraint(v_basis, pltpu.HBM))
    chunks = 4
    basis_x, coupling, basis_v = pl.pallas_call(
        finish_kernel,
        out_shape=(
            jax.ShapeDtypeStruct((own, rank), F32),
            jax.ShapeDtypeStruct((rank, rank), F32),
            jax.ShapeDtypeStruct(v_basis.shape, F32),
        ),
        in_specs=[VM, VM, VM],
        out_specs=(HBM, HBM, HBM),
        scratch_shapes=[
            pltpu.VMEM((rank, 2 * rank), F32),
            pltpu.VMEM((rank, rank), F32),
            pltpu.VMEM(v_basis.shape, F32),
            pltpu.SemaphoreType.DMA((2 + chunks,)),
        ],
        compiler_params=pltpu.CompilerParams(vmem_limit_bytes=12 * 2**20),
    )(gram, lnew, basis_x)
    return basis_x.reshape(k_coeffs.shape), coupling, basis_v


def solution(mesh):
    return jax.shard_map(
        local,
        mesh=mesh,
        in_specs=(P("slab", "brick", None, None), P(("slab", "brick"), None)),
        out_specs=(P("slab", "brick", None, None), P(), P(("slab", "brick"), None)),
        check_vma=False,
    )
```

```python
import functools
import math

import jax
import jax.numpy as jnp
from jax import lax
from jax.experimental import pallas as pl
from jax.experimental.pallas import tpu as pltpu
from jax.sharding import PartitionSpec as P

NVX = 32

CFL = 0.9
VMAX = 6.0
COLLIDE = 0.3
RHO_MIN = 0.25
TEMP_MIN = 0.25
PRECISE = lax.Precision.HIGHEST
MESH = pl.DeviceIdType.MESH
VM = pl.BlockSpec(memory_space=pltpu.VMEM)
HBM = pl.BlockSpec(memory_space=pltpu.HBM)
F32 = jnp.float32
BF16 = jnp.bfloat16
BITS = NVX.bit_length() - 1


def halves(values):
    high = values.astype(BF16)
    return high, (values - high.astype(F32)).astype(BF16)


def dot(left, right):
    return jnp.dot(left, right, preferred_element_type=F32)


def dot_split(high, low, right):
    width = right.shape[1]
    right_high, right_low = halves(right)
    both = dot(high, jnp.concatenate([right_high, right_low], axis=1))
    return both[:, :width] + (both[:, width:] + dot(low, right_high))


def dot3(left, right):
    depth, width = right.shape
    high, low = halves(left)
    if depth != 128:
        return dot_split(high, low, right)
    right_high, right_low = halves(right)
    top = jnp.concatenate([right_high, right_low], axis=1)
    under = jnp.concatenate([right_high, jnp.zeros_like(right_low)], axis=1)
    both = dot(jnp.concatenate([high, low], axis=1), jnp.concatenate([top, under], axis=0))
    return both[:, :width] + both[:, width:]


def thirds(values):
    high = values.astype(BF16)
    rest = values - high.astype(F32)
    middle = rest.astype(BF16)
    return high, middle, (rest - middle.astype(F32)).astype(BF16)


def dot6(left, right):
    width = right.shape[1]
    high, middle, low = thirds(left)
    right_high, right_middle, right_low = thirds(right)
    top = jnp.concatenate([right_high, right_low], axis=1)
    under = jnp.concatenate([right_high, right_middle], axis=1)
    both = dot(jnp.concatenate([high, middle], axis=1), jnp.concatenate([top, under], axis=0))
    cross = dot(jnp.concatenate([high, low], axis=1), jnp.concatenate([right_middle, right_high], axis=0))
    return both[:, :width] + (cross + both[:, width:])


def node_velocity(indices):
    spacing = 2.0 * VMAX / NVX
    last = NVX - 1
    parts = (
        lax.shift_right_logical(indices, 2 * BITS),
        lax.shift_right_logical(indices, BITS) & last,
        indices & last,
    )
    return [-VMAX + (part.astype(F32) + 0.5) * spacing for part in parts]


class Sum:
    def __init__(self, send, pos, ref, name):
        self.send, self.pos = send, pos
        self.x, self.first, self.half, self.second, self.third, self.out = [
            ref[name + part] for part in ("x", "1", "h", "2", "3", "o")
        ]
        self.sems = [(ref[name + part + "s"], ref[name + part + "r"]) for part in ("c", "s", "l", "g")]

    def copy(self, source, target, stage, index, device):
        sent, received = self.sems[stage]
        return self.send(source, target, sent.at[index], received.at[index], device)

    def wait(self):
        for copy in self.copies:
            copy.wait_recv()

    def start(self):
        self.copies = [self.copy(self.x.at[1 - self.pos.core], self.first, 0, 0, self.pos.partner())]

    def scatter(self):
        self.wait()
        slab = self.pos.slab
        self.half[...] = self.x[self.pos.core] + self.first[...]
        self.second[slab] = self.half[slab]
        self.copies = []
        for k in range(1, self.pos.slabs):
            to, device = self.pos.slab_at(k)
            self.copies.append(self.copy(self.half.at[to], self.second.at[slab], 1, k - 1, device))

    def cross(self):
        self.wait()
        total = self.second[0]
        for k in range(1, self.pos.slabs):
            total = total + self.second[k]
        self.third[self.pos.layer] = total
        mine = self.third.at[self.pos.layer]
        self.copies = [self.copy(mine, mine, 2, k - 1, self.pos.across(k)) for k in range(1, self.pos.layers)]

    def collect(self):
        self.wait()
        total = self.third[0]
        for k in range(1, self.pos.layers):
            total = total + self.third[k]
        self.out[self.pos.core, self.pos.slab] = total
        mine = self.out.at[self.pos.core, self.pos.slab]
        self.copies = [self.copy(mine, mine, 3, k - 1, self.pos.slab_at(k)[1]) for k in range(1, self.pos.slabs)]

    def share(self):
        self.wait()
        mine = self.out.at[self.pos.core]
        self.copies = [self.copy(mine, mine, 0, 1, self.pos.partner())]

    def finish(self):
        self.wait()


class Position:
    def __init__(self, slabs, layers):
        self.slabs, self.layers, self.members = slabs, layers, 2 * slabs
        brick = lax.axis_index("brick")
        self.brick = brick
        self.core, self.layer = lax.rem(brick, 2), lax.div(brick, 2)
        self.slab = lax.axis_index("slab")
        self.me = 2 * self.slab + self.core

    def member(self, k):
        to = lax.rem(self.me + k, self.members)
        return to, (lax.div(to, 2), 2 * self.layer + lax.rem(to, 2))

    def mate(self, k):
        if self.layers != 4:
            return lax.rem(self.layer + k, self.layers)
        if k == 1:
            return self.layer + 1 - 2 * lax.rem(self.layer, 2)
        return lax.rem(self.layer + 2, self.layers) if k == 2 else self.layers - 1 - self.layer

    def source(self, k):
        if k == 0:
            return self.layer
        return self.mate(k) if self.layers == 4 else lax.rem(self.layer + self.layers - k, self.layers)

    def across(self, k):
        return (self.slab, 2 * lax.rem(self.layer + k, self.layers) + self.core)

    def others(self):
        bricks = 2 * self.layers
        count = self.slabs * bricks
        at = self.slab * bricks + self.brick
        for k in range(1, count):
            to = lax.rem(at + k, count)
            yield k - 1, (lax.div(to, bricks), lax.rem(to, bricks))

    def partner(self):
        return (self.slab, 2 * self.layer + 1 - self.core)

    def slab_at(self, k):
        to = lax.rem(self.slab + k, self.slabs)
        return to, (to, self.brick)

    def slab_mate(self, k):
        if self.slabs != 4 or k == 0:
            return lax.rem(self.slab + k, self.slabs)
        if k == 1:
            return self.slabs - 1 - self.slab
        return self.slab + 1 - 2 * lax.rem(self.slab, 2) if k == 2 else lax.rem(self.slab + 2, self.slabs)

    def slab_source(self, k):
        return self.slab_mate(k) if self.slabs == 4 else lax.rem(self.slab + self.slabs - k, self.slabs)

    def brick_at(self, k):
        bricks = 2 * self.layers
        return (self.slab, lax.rem(self.brick + k + bricks, bricks))


def factor_steps(work, matrix, fillers=()):
    size = matrix.shape[0]
    block, panel = 8, 16
    row = lax.broadcasted_iota(jnp.int32, (size, size), 0)
    column = lax.broadcasted_iota(jnp.int32, (size, size), 1)
    work[:, :size] = matrix
    work[:, size:] = jnp.where(row == column, 1.0, 0.0)
    sub = lax.broadcasted_iota(jnp.int32, (block, size), 0)
    narrow, wide = (block, size), (block, 2 * size)
    fillers = list(fillers)
    for start in range(0, size, panel):
        if fillers:
            fillers.pop(0)()
        rows = [work[start : start + block, :], work[start + block : start + panel, :]]
        for b in range(2):
            at = start + b * block
            columns = {
                (r, m): jnp.broadcast_to(rows[r][:, at + m : at + m + 1], narrow)
                for r in range(b, 2)
                for m in range(block)
            }
            entry = {
                (i, m): jnp.broadcast_to(columns[b, m][i : i + 1], narrow) for m in range(block) for i in range(m, block)
            }
            scales = entry[0, 0]
            for k in range(block):
                scale = lax.rsqrt(entry[k, k])
                invert = scale * scale
                scales = scale if k == 0 else jnp.where(sub == k, scale, scales)
                ratios = {r: columns[r, k] * invert for r in range(b, 2)}
                ratios[b] = jnp.where(sub > k, ratios[b], 0.0)
                for m in range(k + 1, block):
                    factor = entry[m, k] * invert
                    for i in range(m, block):
                        entry[i, m] = entry[i, m] - entry[i, k] * factor
                for r in range(b, 2):
                    for m in range(k + 1, block):
                        columns[r, m] = columns[r, m] - ratios[r] * entry[m, k]
                pivot = jnp.broadcast_to(rows[b][k : k + 1], wide)
                for r in range(b, 2):
                    rows[r] = rows[r] - jnp.concatenate([ratios[r], ratios[r]], axis=1) * pivot
            rows[b] = rows[b] * jnp.concatenate([scales, scales], axis=1)
        both = jnp.concatenate(rows, axis=0)
        work[start : start + panel, :] = both
        if start + panel < size:
            high = both.astype(BF16).astype(F32)
            low = (both - high).astype(BF16).astype(F32)
            rest = both - high - low
            left = jnp.concatenate([item[:, :size] for item in (high, high, low, high, rest, low)], axis=0)
            right = jnp.concatenate([item.astype(BF16) for item in (high, low, high, rest, high, low)], axis=0)
            tall = left.T[start + panel :, :].astype(BF16)
            work[start + panel :, :] = work[start + panel :, :] - dot(tall, right)
    for filler in fillers:
        filler()
    factor = jnp.where(column <= row, work[:, :size].T, 0.0)
    inverse = jnp.where(column <= row, work[:, size:], 0.0)
    return factor, inverse


def step_kernel(names, slabs, layers, *refs):
    ref = dict(zip(names, refs))
    pos = Position(slabs, layers)
    core, slab, layer, brick, me = pos.core, pos.slab, pos.layer, pos.brick, pos.me
    members, bricks = pos.members, 2 * layers
    k_ref, v_ref = ref["k_here"], ref["v_here"]
    inputs = [
        pltpu.make_async_copy(ref["k"], k_ref, ref["insem"].at[0]),
        pltpu.make_async_copy(ref["v"], v_ref, ref["insem"].at[1]),
    ]
    for copy in inputs:
        copy.start()
    cells_x, cells_y, cells_z, rank = k_ref.shape
    own = cells_x * cells_y * cells_z
    nodes = v_ref.shape[0]
    lengths = (cells_x * slabs, cells_y * bricks, cells_z)
    cells = lengths[0] * lengths[1] * lengths[2]
    time_step = CFL / (VMAX * (lengths[0] + lengths[1] + lengths[2]))
    weight_x = 1.0 / cells
    weight_v = (2.0 * VMAX / NVX) ** 3
    base = (slab * bricks + brick) * nodes
    started = []

    def send(source, target, send_sem, recv_sem, device):
        copy = pltpu.make_async_remote_copy(
            src_ref=source,
            dst_ref=target,
            send_sem=send_sem,
            recv_sem=recv_sem,
            device_id=device,
            device_id_type=MESH,
        )
        copy.start()
        started.append(copy)
        return copy

    barrier = pltpu.get_barrier_semaphore()
    peers = [pos.member(k)[1] for k in range(1, members)] + [pos.across(k) for k in range(1, layers)]
    for peer in peers:
        pl.semaphore_signal(barrier, inc=1, device_id=peer, device_id_type=MESH)

    lane = lax.broadcasted_iota(jnp.int32, (8, nodes), 1)
    sub = lax.broadcasted_iota(jnp.int32, (8, nodes), 0)
    velocity = node_velocity(base + lane)
    square = velocity[0] * velocity[0] + velocity[1] * velocity[1] + velocity[2] * velocity[2]
    weights = jnp.where(sub == 0, 1.0, jnp.where(sub == 4, square, 0.0))
    upward = jnp.zeros_like(weights)
    for d in range(3):
        weights = jnp.where(sub == d + 1, velocity[d], weights)
        upward = jnp.where(sub == d + 5, jnp.maximum(velocity[d], 0.0), upward)
    for copy in inputs:
        copy.wait()
    values = v_ref[...]
    v_high, v_low = halves(values)
    v_rest = (values - v_high.astype(F32) - v_low.astype(F32)).astype(BF16)
    sums = dot(jnp.concatenate(halves(weights), axis=0), jnp.concatenate([v_high, v_low, v_rest], axis=1))
    sums = sums[:8] + sums[8:]
    squares = dot(upward.astype(BF16), jnp.concatenate(halves(values * values), axis=1))
    partial = sums[:, :rank] + (sums[:, rank : 2 * rank] + sums[:, 2 * rank :])
    partial = (partial + (squares[:, :rank] + squares[:, rank:])) * weight_v
    vec_l, vec_m = ref["vec_l"], ref["vec_m"]
    vec_l[layer] = partial

    turned_v = values.T
    vt_high, vt_low = halves(turned_v)
    vt = ref["vt"]
    vt[:rank] = vt_high
    vt[rank:] = vt_low
    v_both = jnp.concatenate([v_high, v_low], axis=1)
    row = lax.broadcasted_iota(jnp.int32, (rank, rank), 0)
    column = lax.broadcasted_iota(jnp.int32, (rank, rank), 1)
    packed = []

    def pack(d):
        sides = []
        for side in (jnp.maximum(velocity[d][:1], 0.0), jnp.minimum(velocity[d][:1], 0.0)):
            high, low = halves(turned_v * (side * weight_v))
            both = dot(high, v_both)
            sides.append(both[:, :rank] + (both[:, rank:] + dot(low, v_high)))
        packed.append(jnp.where(row > column, sides[0], sides[1]))

    for d in range(3):
        pack(d)
    ref["tx"][...] = jnp.concatenate(packed, axis=0).reshape(ref["tx"].shape)
    transport_sum = Sum(send, pos, ref, "t")
    pl.semaphore_wait(barrier, len(peers))
    mine = vec_l.at[layer]
    copies = [
        send(mine, mine, ref["vls"].at[k - 1], ref["vlr"].at[k - 1], pos.across(k)) for k in range(1, layers)
    ]
    transport_sum.start()
    transport_sum.scatter()
    for copy in copies:
        copy.wait_recv()
    total = vec_l[0]
    for k in range(1, layers):
        total = total + vec_l[k]
    vec_m[me] = total
    mine = vec_m.at[me]
    copies = [
        send(mine, mine, ref["vms"].at[k - 1], ref["vmr"].at[k - 1], pos.member(k)[1]) for k in range(1, members)
    ]
    transport_sum.cross()
    for copy in copies:
        copy.wait_recv()
    vectors = vec_m[0]
    for k in range(1, members):
        vectors = vectors + vec_m[k]

    own_k = k_ref[...].reshape(own, rank)
    kpad = ref["kpad"]
    kpad[...] = jnp.zeros_like(kpad)
    kpad[pl.ds(pl.multiple_of(core * own, 8), own), :] = own_k
    moments = lax.dot_general(
        vectors, kpad[...], (((1,), (1,)), ((), ())), precision=PRECISE, preferred_element_type=F32
    )
    pair = 2 * own
    density = jnp.maximum(moments[0:1], RHO_MIN)
    drift = [moments[d : d + 1] / density for d in range(1, 4)]
    bulk = drift[0] * drift[0] + drift[1] * drift[1] + drift[2] * drift[2]
    temper = jnp.maximum((moments[4:5] / density - bulk) / 3.0, TEMP_MIN)
    wide = 2.0 * math.pi * temper
    amplitude = density / (wide * jnp.sqrt(wide))
    state = jnp.zeros((8, pair), F32)
    sub_pair = lax.broadcasted_iota(jnp.int32, (8, pair), 0)
    lane_pair = lax.broadcasted_iota(jnp.int32, (8, pair), 1)
    for i, item in enumerate(drift + [-0.5 / temper, amplitude]):
        state = jnp.where(sub_pair == i, item, state)
    inside = (lane_pair >= core * own) & (lane_pair < (core + 1) * own)
    par = ref["par"]
    par[me, layer] = jnp.where(inside, state, 0.0)
    mine = par.at[me, layer, pl.ds(0, 5)]
    copies = [send(mine, mine, ref["ps"].at[i], ref["pr"].at[i], device) for i, device in pos.others()]
    halo_a, halo_b = ref["halo_a"], ref["halo_b"]
    halos = [
        send(k_ref.at[cells_x - 1], halo_a.at[0], ref["hs"].at[0], ref["hr"].at[0], pos.slab_at(1)[1]),
        send(k_ref.at[0], halo_a.at[1], ref["hs"].at[1], ref["hr"].at[1], pos.slab_at(slabs - 1)[1]),
        send(k_ref.at[:, cells_y - 1], halo_b.at[0], ref["hs"].at[2], ref["hr"].at[2], pos.brick_at(1)),
        send(k_ref.at[:, 0], halo_b.at[1], ref["hs"].at[3], ref["hr"].at[3], pos.brick_at(-1)),
    ]
    transport_sum.collect()
    for copy in copies:
        copy.wait_recv()

    mt_high, mt_low = ref["mt_high"], ref["mt_low"]
    mp, first, half, second, third = ref["mp"], ref["first"], ref["half"], ref["second"], ref["third"]
    group = math.gcd(nodes, NVX)
    groups = nodes // group
    width = 2 * pair
    slots = layers // 2
    fast_v = node_velocity(base + lax.broadcasted_iota(jnp.int32, (group, width), 0))
    slow_v = node_velocity(base + group * lax.broadcasted_iota(jnp.int32, (groups, width), 0))

    def build(to, slot, stage):
        blocks = [par[2 * to, 2 * slot + i] + par[2 * to + 1, 2 * slot + i] for i in range(2)]
        state = jnp.concatenate(blocks, axis=1)
        u = [state[d : d + 1] for d in range(3)]
        rate, scale = state[3:4], state[4:5]
        fast = jnp.exp((fast_v[2] - u[2]) ** 2 * rate)
        slow = jnp.exp(((slow_v[0] - u[0]) ** 2 + (slow_v[1] - u[1]) ** 2) * rate) * scale
        places = [pl.ds(pl.multiple_of(((2 * slot + i) * slabs + to) * pair, pair), pair) for i in range(2)]
        for t in range(groups):
            high, low = halves(fast * slow[t : t + 1])
            span = slice(t * group, (t + 1) * group)
            stage[0][span, :] = high
            stage[1][span, :] = low
            for i, place in enumerate(places):
                mt_high[span, place] = high[:, i * pair : (i + 1) * pair]
                mt_low[span, place] = low[:, i * pair : (i + 1) * pair]

    def multiply(to, slot, stage):
        high = dot(vt[...], stage[0][...])
        low = dot(vt[:rank], stage[1][...])
        result = ((high[:rank] + (high[rank:] + low)) * weight_v).T
        for i in range(2):
            for c in range(2):
                at = (2 * i + c) * own
                mp[to, 2 * slot + i, c] = result[at : at + own]

    def hand_over(k, slot, to):
        at = pl.ds(2 * slot, 2)
        return send(
            mp.at[to, at, 1 - core], first.at[to, at], ref["cs"].at[k, slot], ref["cr"].at[k, slot], pos.partner()
        )

    over = []

    def hand_on(k, slot, to, copy):
        copy.wait_recv()
        at = pl.ds(2 * slot, 2)
        if k == 0:
            second[slab, at] = mp[slab, at, core] + first[slab, at]
            return
        half[to, at] = mp[to, at, core] + first[to, at]
        over.append(
            send(half.at[to, at], second.at[slab, at], ref["ss"].at[k - 1, slot], ref["sr"].at[k - 1, slot], (to, brick))
        )

    waiting = []
    steps = [(k, pos.slab_mate(k), slot) for k in list(range(1, slabs)) + [0] for slot in range(slots)]
    stages = [(ref["stage_h0"], ref["stage_l0"]), (ref["stage_h1"], ref["stage_l1"])]
    build(*steps[0][1:], stages[0])
    for i, (k, to, slot) in enumerate(steps):
        multiply(to, slot, stages[i % 2])
        if i + 1 < len(steps):
            build(*steps[i + 1][1:], stages[(i + 1) % 2])
        copy = hand_over(k, slot, to)
        if i == 0:
            transport_sum.share()
        if len(waiting) >= 2:
            hand_on(*waiting.pop(0))
        waiting.append((k, slot, to, copy))

    for copy in waiting:
        hand_on(*copy)

    transport_sum.finish()
    packed = ref["to"][...].reshape(3 * rank, rank)
    trans = ref["trans"]
    for d in range(3):
        block = packed[d * rank : (d + 1) * rank]
        flipped = block.T
        diagonal = jnp.where(row == column, vectors[d + 5 : d + 6], 0.0)
        trans[d * rank : (d + 1) * rank] = jnp.where(row <= column, block, flipped)
        trans[(d + 3) * rank : (d + 4) * rank] = jnp.where(
            row > column, block, jnp.where(row < column, flipped, diagonal)
        )
    for copy in halos:
        copy.wait_recv()
    field = k_ref[...]
    after_a = jnp.concatenate([field[1:], halo_a[1:2]], axis=0)
    before_a = jnp.concatenate([halo_a[0:1], field[:-1]], axis=0)
    after_b = jnp.concatenate([field[:, 1:], halo_b[1].reshape(cells_x, 1, cells_z, rank)], axis=1)
    before_b = jnp.concatenate([halo_b[0].reshape(cells_x, 1, cells_z, rank), field[:, :-1]], axis=1)

    def next_third(flat):
        count = flat.shape[0]
        index = lax.broadcasted_iota(jnp.int32, flat.shape, 0)
        return jnp.where(
            lax.rem(index, cells_z) == cells_z - 1,
            pltpu.roll(flat, cells_z - 1, 0),
            pltpu.roll(flat, count - 1, 0),
        )

    def last_third(flat):
        count = flat.shape[0]
        index = lax.broadcasted_iota(jnp.int32, flat.shape, 0)
        return jnp.where(
            lax.rem(index, cells_z) == 0,
            pltpu.roll(flat, count - cells_z + 1, 0),
            pltpu.roll(flat, 1, 0),
        )

    fields = [
        (after_a.reshape(own, rank) - own_k) * lengths[0],
        (after_b.reshape(own, rank) - own_k) * lengths[1],
        (next_third(own_k) - own_k) * lengths[2],
        (own_k - before_a.reshape(own, rank)) * lengths[0],
        (own_k - before_b.reshape(own, rank)) * lengths[1],
        (own_k - last_third(own_k)) * lengths[2],
    ]
    flux = dot3(jnp.concatenate(fields, axis=1), trans[...])
    kept = own_k - time_step * flux - COLLIDE * own_k

    for copy in over:
        copy.wait_recv()
    total = second[0]
    for k in range(1, slabs):
        total = total + second[k]
    quarter = ref["quarter"]
    quarter[...] = total
    copies = []
    for k in range(1, layers):
        to = lax.rem(layer + k, layers)
        copies.append(
            send(quarter.at[to], third.at[layer], ref["zs"].at[k - 1], ref["zr"].at[k - 1], pos.across(k))
        )
    third[layer] = quarter[layer]
    for copy in copies:
        copy.wait_recv()
    mproj = third[0]
    for k in range(1, layers):
        mproj = mproj + third[k]
    advanced = kept + COLLIDE * mproj

    adv = ref["adv"]
    adv[layer, slab, core] = advanced.reshape(cells_x, cells_y, cells_z, rank)
    here = adv.at[layer, slab, core]

    def to_slabs(block, j):
        return [
            send(block, block, ref["bs"].at[k - 1, j], ref["br"].at[k - 1, j], (pos.slab_mate(k), brick))
            for k in range(1, slabs)
        ]

    along = [
        send(here, here, ref["as"].at[k - 1], ref["ar"].at[k - 1], (slab, 2 * pos.mate(k) + core))
        for k in range(1, layers)
    ]
    crossing = [to_slabs(here, 0)]
    last = [[send(here, here, ref["ds"].at[0, 0], ref["dr"].at[0, 0], pos.partner())]]
    raw_sum = Sum(send, pos, ref, "r")
    ref["rx"][...] = dot3(advanced.T, mproj).reshape(ref["rx"].shape)
    raw_sum.start()
    raw_sum.scatter()
    for j in range(1, layers):
        along[j - 1].wait_recv()
        block = adv.at[pos.source(j), slab, core]
        crossing.append(to_slabs(block, j))
        last.append([send(block, block, ref["ds"].at[0, j], ref["dr"].at[0, j], pos.partner())])

    at, ahl, back = ref["at"], ref["ahl"], ref["back"]
    d_high, d_low, gram_l = ref["d_high"], ref["d_low"], ref["gram_l"]
    plane = cells // layers

    def relay(j):
        for k in range(1, slabs):
            crossing[j][k - 1].wait_recv()
            block = adv.at[pos.source(j), pos.slab_source(k), core]
            last[j].append(send(block, block, ref["ds"].at[k, j], ref["dr"].at[k, j], pos.partner()))

    def store_slopes(span, d, values):
        high, low = halves(values)
        d_high[span, d * rank : (d + 1) * rank] = high
        d_low[span, d * rank : (d + 1) * rank] = low

    def take(j):
        for copy in last[j]:
            copy.wait_recv()
        from_layer = pos.source(j)
        block = adv[from_layer]
        span = pl.ds(pl.multiple_of(from_layer * plane, plane), plane)
        flat = block.reshape(plane, rank)
        high, low = halves(flat)
        ahl[span, :rank] = high
        ahl[span, rank:] = low
        high_t, low_t = halves(flat.T)
        at[:rank, span] = high_t
        at[rank:, span] = low_t
        gram_l[from_layer] = dot(high_t, jnp.concatenate([high, low], axis=1))
        across = jnp.concatenate([block[1:, :, :1], block[:1, :, :1]], axis=0)
        after = jnp.concatenate([block[:, :, 1:], across], axis=2)
        store_slopes(span, 0, after.reshape(plane, rank) - flat)
        store_slopes(span, 2, next_third(flat) - flat)

    def project_back(j, rows):
        span = pl.ds(pl.multiple_of(pos.source(j) * plane, plane), plane)
        top = dot(mt_high[rows, span], ahl[span, :])
        part = top[:, :rank] + (top[:, rank:] + dot(mt_low[rows, span], ahl[span, :rank]))
        back[rows, :] = part if j == 0 else back[rows, :] + part

    quarters = [slice(i * (nodes // 4), (i + 1) * (nodes // 4)) for i in range(4)]
    for j in range(layers):
        relay(j)
        if j == 1:
            raw_sum.cross()
        if j > 0:
            take(j - 1)
            for rows in quarters:
                project_back(j - 1, rows)
    raw_sum.collect()
    take(layers - 1)
    total = gram_l[0]
    for k in range(1, layers):
        total = total + gram_l[k]
    mixed = total[:, rank:]
    gram = (total[:, :rank] + (mixed + mixed.T)) * weight_x
    for k in range(layers):
        block, following = adv[k], adv[(k + 1) % layers]
        ups = [
            jnp.concatenate([block[:, 0, :, 1:], block[:, 1, :, :1]], axis=2),
            jnp.concatenate([block[:, 1, :, 1:], following[:, 0, :, :1]], axis=2),
        ]
        for c in range(2):
            difference = (ups[c] - block[:, c]).reshape(slabs, own, rank)
            for i in range(slabs):
                first_row = k * plane + (2 * i + c) * own
                store_slopes(slice(first_row, first_row + own), 1, difference[i])
    slopes = [None] * 3

    def slope_product(d):
        columns = slice(d * rank, (d + 1) * rank)
        both = dot(at[...], d_high[:, columns])
        both = both[:rank] + (both[rank:] + dot(at[:rank], d_low[:, columns]))
        slopes[d] = both * (lengths[d] * weight_x)

    sources = []

    def drive():
        sources.append(
            time_step * dot6(jnp.concatenate(slopes + [-item.T for item in slopes], axis=1), trans[...])
        )

    back_last = [functools.partial(project_back, layers - 1, rows) for rows in quarters]
    fillers = [functools.partial(slope_product, d) for d in (0, 2, 1)] + [drive]
    fillers += [back_last[0], lambda: (raw_sum.share(), back_last[1]()), back_last[2]]
    fillers += [lambda: (raw_sum.finish(), back_last[3]())]
    factor, inverse = factor_steps(ref["work"], gram, fillers)
    source = sources[0] - COLLIDE * weight_x * ref["ro"][...].reshape(rank, rank)

    turned = inverse.T
    middle = (1.0 + COLLIDE) * factor + dot6(source.T, turned)
    moved = dot6(inverse, jnp.concatenate(slopes, axis=1))
    plus = dot6(jnp.concatenate([moved[:, d * rank : (d + 1) * rank] for d in range(3)], axis=0), turned)
    plus = [plus[d * rank : (d + 1) * rank] for d in range(3)]
    lnew = ref["lnew"]
    chunk = math.gcd(nodes, NVX * NVX // 4)
    gram_v = jnp.zeros((rank, rank), F32)
    mixed_v = jnp.zeros((rank, rank), F32)
    behind = [-item.T for item in plus]
    for at_row in range(0, nodes, chunk):
        span = slice(at_row, at_row + chunk)
        node = base + at_row
        lnow = dot3(v_ref[span, :], middle)
        ahead = [node // (NVX * NVX) >= NVX // 2, node // NVX % NVX >= NVX // 2]
        sides = [jnp.where(ahead[d], plus[d], behind[d]) for d in range(2)] + [plus[2], behind[2]]
        sliding = dot3(lnow, jnp.concatenate(sides, axis=1))
        part = node_velocity(node + lax.broadcasted_iota(jnp.int32, (chunk, rank), 0))
        slide = part[0] * sliding[:, :rank] + part[1] * sliding[:, rank : 2 * rank]
        slide = slide + part[2] * jnp.where(part[2] > 0, sliding[:, 2 * rank : 3 * rank], sliding[:, 3 * rank :])
        mback = dot3(back[span, :] * weight_x, turned)
        new = lnow + time_step * slide + COLLIDE * (mback - lnow)
        lnew[span, :] = new
        high, low = halves(new)
        rest = (new - high.astype(F32) - low.astype(F32)).astype(BF16)
        high_t, low_t = halves(new.T)
        both = dot(high_t, jnp.concatenate([high, low, rest], axis=1))
        gram_v = gram_v + both[:, :rank]
        mixed_v = mixed_v + (both[:, rank : 2 * rank] + (both[:, 2 * rank :] + 0.5 * dot(low_t, low)))
    gram_v = (gram_v + (mixed_v + mixed_v.T)) * weight_v

    half_rank = rank // 2
    lanes = lax.broadcasted_iota(jnp.int32, (half_rank // 2, rank), 1)
    corner = jnp.where(
        lanes < half_rank,
        pltpu.roll(gram_v[half_rank : half_rank + half_rank // 2], half_rank, 1),
        gram_v[half_rank + half_rank // 2 :],
    )
    gx, g1, g2, g3, go = ref["gx"], ref["g1"], ref["g2"], ref["g3"], ref["go"]
    gx[...] = jnp.concatenate([gram_v[:half_rank], corner], axis=0).reshape(gx.shape)
    copy = send(gx.at[1 - core], g1, ref["gcs"].at[0], ref["gcr"].at[0], pos.partner())
    copy.wait_recv()
    g2[slab] = gx[core] + g1[...]
    mine = g2.at[slab]
    copies = [
        send(mine, mine, ref["gss"].at[k - 1], ref["gsr"].at[k - 1], pos.slab_at(k)[1]) for k in range(1, slabs)
    ]
    ref["basis_x"][...] = dot3(advanced, turned)
    sent = len(started) - len(copies)
    for copy in started[:sent]:
        copy.wait_send()
    for copy in copies:
        copy.wait_recv()
    total = g2[0]
    for k in range(1, slabs):
        total = total + g2[k]
    g3[layer] = total
    mine = g3.at[layer]
    copies = [
        send(mine, mine, ref["gls"].at[k - 1], ref["glr"].at[k - 1], pos.across(k)) for k in range(1, layers)
    ]
    for copy in copies:
        copy.wait_recv()
    total = g3[0]
    for k in range(1, layers):
        total = total + g3[k]
    go[core] = total
    mine = go.at[core]
    send(mine, mine, ref["gcs"].at[1], ref["gcr"].at[1], pos.partner()).wait_recv()
    whole = go[...].reshape(half_rank + half_rank // 2, rank)
    corner = whole[half_rank:]
    gram_ref = ref["gram"]
    gram_ref[:half_rank] = whole[:half_rank]
    gram_ref[half_rank : half_rank + half_rank // 2] = pltpu.roll(corner, half_rank, 1)
    gram_ref[half_rank + half_rank // 2 :] = corner
    for copy in started[sent:]:
        copy.wait_send()


def finish_kernel(gram, lnew, field, basis_x, coupling, basis_v, work, factor_buffer, out, sems):
    give = pltpu.make_async_copy(field, basis_x, sems.at[0])
    give.start()
    factor, inverse = factor_steps(work, gram[...])
    factor_buffer[...] = factor
    copies = [give, pltpu.make_async_copy(factor_buffer, coupling, sems.at[1])]
    copies[1].start()
    turned = inverse.T
    nodes = lnew.shape[0]
    count = sems.shape[0] - 2
    chunk = nodes // count
    for i in range(count):
        span = pl.ds(i * chunk, chunk)
        out[span, :] = dot3(lnew[span, :], turned)
        copies.append(pltpu.make_async_copy(out.at[span], basis_v.at[span], sems.at[2 + i]))
        copies[-1].start()
    for copy in copies:
        copy.wait()


def local(k_coeffs, v_basis):
    cells_x, cells_y, cells_z, rank = k_coeffs.shape
    slabs = lax.axis_size("slab")
    layers = lax.axis_size("brick") // 2
    members = 2 * slabs
    own = cells_x * cells_y * cells_z
    nodes = v_basis.shape[0]
    cells = own * members * layers
    share = 3 * rank // members
    part = rank // members
    pair = 2 * own
    devices = members * layers
    names = ["k", "v", "basis_x", "gram", "lnew"]
    scratch = []

    used = [0]

    def buffer(name, shape, dtype=F32):
        names.append(name)
        used[0] += math.prod(shape) * jnp.dtype(dtype).itemsize
        scratch.append(pltpu.VMEM(shape, dtype))

    def semaphores(name, *shape):
        names.append(name)
        scratch.append(pltpu.SemaphoreType.DMA(shape))

    def reduction(name, rows):
        buffer(name + "x", (2, slabs, rows, rank))
        buffer(name + "1", (slabs, rows, rank))
        buffer(name + "h", (slabs, rows, rank))
        buffer(name + "2", (slabs, rows, rank))
        buffer(name + "3", (layers, rows, rank))
        buffer(name + "o", (2, slabs, rows, rank))
        for stage, count in (("c", 2), ("s", slabs - 1), ("l", layers - 1), ("g", slabs - 1)):
            semaphores(name + stage + "s", count)
            semaphores(name + stage + "r", count)

    buffer("k_here", k_coeffs.shape)
    buffer("v_here", v_basis.shape)
    semaphores("insem", 2)
    buffer("vec_l", (layers, 8, rank))
    buffer("vec_m", (members, 8, rank))
    buffer("halo_a", (2, cells_y, cells_z, rank))
    buffer("halo_b", (2, cells_x, cells_z, rank))
    buffer("vt", (2 * rank, nodes), BF16)
    buffer("kpad", (pair, rank))
    buffer("par", (members, layers, 8, pair))
    buffer("mt_high", (nodes, cells), BF16)
    buffer("mt_low", (nodes, cells), BF16)
    for name in ("stage_h0", "stage_l0", "stage_h1", "stage_l1"):
        buffer(name, (nodes, 2 * pair), BF16)
    buffer("mp", (slabs, layers, 2, own, rank))
    buffer("first", (slabs, layers, own, rank))
    buffer("half", (slabs, layers, own, rank))
    buffer("second", (slabs, layers, own, rank))
    buffer("quarter", (layers, own, rank))
    buffer("third", (layers, own, rank))
    buffer("trans", (6 * rank, rank))
    buffer("adv", (layers, slabs, 2, cells_x, cells_y, cells_z, rank))
    buffer("back", (nodes, rank))
    buffer("gram_l", (layers, rank, 2 * rank))
    buffer("at", (2 * rank, cells), BF16)
    buffer("ahl", (cells, 2 * rank), BF16)
    buffer("d_high", (cells, 3 * rank), BF16)
    buffer("d_low", (cells, 3 * rank), BF16)
    buffer("work", (rank, 2 * rank))
    reduction("t", share)
    reduction("r", part)
    packed = 3 * rank // 8
    buffer("gx", (2, packed, rank))
    buffer("g1", (packed, rank))
    buffer("g2", (slabs, packed, rank))
    buffer("g3", (layers, packed, rank))
    buffer("go", (2, packed, rank))
    for name, count in (("gc", 2), ("gs", slabs - 1), ("vl", layers - 1), ("vm", members - 1), ("p", devices - 1)):
        semaphores(name + "s", count)
        semaphores(name + "r", count)
    for name in ("gl", "z", "a"):
        semaphores(name + "s", layers - 1)
        semaphores(name + "r", layers - 1)
    semaphores("hs", 4)
    semaphores("hr", 4)
    for name, shape in (
        ("c", (slabs, layers // 2)),
        ("s", (slabs - 1, layers // 2)),
        ("b", (slabs - 1, layers)),
        ("d", (slabs, layers)),
    ):
        semaphores(name + "s", *shape)
        semaphores(name + "r", *shape)
    basis_x, gram, lnew = pl.pallas_call(
        functools.partial(step_kernel, tuple(names), slabs, layers),
        out_shape=(
            jax.ShapeDtypeStruct((own, rank), F32),
            jax.ShapeDtypeStruct((rank, rank), F32),
            jax.ShapeDtypeStruct(v_basis.shape, F32),
        ),
        in_specs=[HBM, HBM],
        out_specs=(VM, VM, VM),
        scratch_shapes=scratch,
        compiler_params=pltpu.CompilerParams(
            collective_id=1, has_side_effects=True, vmem_limit_bytes=min(62 * 2**20, used[0] + 14 * 2**20)
        ),
    )(pltpu.with_memory_space_constraint(k_coeffs, pltpu.HBM), pltpu.with_memory_space_constraint(v_basis, pltpu.HBM))
    chunks = 4
    basis_x, coupling, basis_v = pl.pallas_call(
        finish_kernel,
        out_shape=(
            jax.ShapeDtypeStruct((own, rank), F32),
            jax.ShapeDtypeStruct((rank, rank), F32),
            jax.ShapeDtypeStruct(v_basis.shape, F32),
        ),
        in_specs=[VM, VM, VM],
        out_specs=(HBM, HBM, HBM),
        scratch_shapes=[
            pltpu.VMEM((rank, 2 * rank), F32),
            pltpu.VMEM((rank, rank), F32),
            pltpu.VMEM(v_basis.shape, F32),
            pltpu.SemaphoreType.DMA((2 + chunks,)),
        ],
        compiler_params=pltpu.CompilerParams(vmem_limit_bytes=12 * 2**20),
    )(gram, lnew, basis_x)
    return basis_x.reshape(k_coeffs.shape), coupling, basis_v


def solution(mesh):
    return jax.shard_map(
        local,
        mesh=mesh,
        in_specs=(P("slab", "brick", None, None), P(("slab", "brick"), None)),
        out_specs=(P("slab", "brick", None, None), P(), P(("slab", "brick"), None)),
        check_vma=False,
    )
```

```python
import functools
import math

import jax
import jax.numpy as jnp
from jax import lax
from jax.experimental import pallas as pl
from jax.experimental.pallas import tpu as pltpu
from jax.sharding import PartitionSpec as P

NVX = 32

CFL = 0.9
VMAX = 6.0
COLLIDE = 0.3
RHO_MIN = 0.25
TEMP_MIN = 0.25
PRECISE = lax.Precision.HIGHEST
MESH = pl.DeviceIdType.MESH
VM = pl.BlockSpec(memory_space=pltpu.VMEM)
HBM = pl.BlockSpec(memory_space=pltpu.HBM)
F32 = jnp.float32
BF16 = jnp.bfloat16
BITS = NVX.bit_length() - 1


def halves(values):
    high = values.astype(BF16)
    return high, (values - high.astype(F32)).astype(BF16)


def dot(left, right):
    return jnp.dot(left, right, preferred_element_type=F32)


def dot_split(high, low, right):
    width = right.shape[1]
    right_high, right_low = halves(right)
    both = dot(high, jnp.concatenate([right_high, right_low], axis=1))
    return both[:, :width] + (both[:, width:] + dot(low, right_high))


def dot3(left, right):
    depth, width = right.shape
    high, low = halves(left)
    if depth != 128:
        return dot_split(high, low, right)
    right_high, right_low = halves(right)
    top = jnp.concatenate([right_high, right_low], axis=1)
    under = jnp.concatenate([right_high, jnp.zeros_like(right_low)], axis=1)
    both = dot(jnp.concatenate([high, low], axis=1), jnp.concatenate([top, under], axis=0))
    return both[:, :width] + both[:, width:]


def thirds(values):
    high = values.astype(BF16)
    rest = values - high.astype(F32)
    middle = rest.astype(BF16)
    return high, middle, (rest - middle.astype(F32)).astype(BF16)


def dot6(left, right):
    width = right.shape[1]
    high, middle, low = thirds(left)
    right_high, right_middle, right_low = thirds(right)
    top = jnp.concatenate([right_high, right_low], axis=1)
    under = jnp.concatenate([right_high, right_middle], axis=1)
    both = dot(jnp.concatenate([high, middle], axis=1), jnp.concatenate([top, under], axis=0))
    cross = dot(jnp.concatenate([high, low], axis=1), jnp.concatenate([right_middle, right_high], axis=0))
    return both[:, :width] + (cross + both[:, width:])


def node_velocity(indices):
    spacing = 2.0 * VMAX / NVX
    last = NVX - 1
    parts = (
        lax.shift_right_logical(indices, 2 * BITS),
        lax.shift_right_logical(indices, BITS) & last,
        indices & last,
    )
    return [-VMAX + (part.astype(F32) + 0.5) * spacing for part in parts]


class Sum:
    def __init__(self, send, pos, ref, name):
        self.send, self.pos = send, pos
        self.x, self.first, self.half, self.second, self.third, self.out = [
            ref[name + part] for part in ("x", "1", "h", "2", "3", "o")
        ]
        self.sems = [(ref[name + part + "s"], ref[name + part + "r"]) for part in ("c", "s", "l", "g")]

    def copy(self, source, target, stage, index, device):
        sent, received = self.sems[stage]
        return self.send(source, target, sent.at[index], received.at[index], device)

    def wait(self):
        for copy in self.copies:
            copy.wait_recv()

    def start(self):
        self.copies = [self.copy(self.x.at[1 - self.pos.core], self.first, 0, 0, self.pos.partner())]

    def scatter(self):
        self.wait()
        slab = self.pos.slab
        self.half[...] = self.x[self.pos.core] + self.first[...]
        self.second[slab] = self.half[slab]
        self.copies = []
        for k in range(1, self.pos.slabs):
            to, device = self.pos.slab_at(k)
            self.copies.append(self.copy(self.half.at[to], self.second.at[slab], 1, k - 1, device))

    def cross(self):
        self.wait()
        total = self.second[0]
        for k in range(1, self.pos.slabs):
            total = total + self.second[k]
        self.third[self.pos.layer] = total
        mine = self.third.at[self.pos.layer]
        self.copies = [self.copy(mine, mine, 2, k - 1, self.pos.across(k)) for k in range(1, self.pos.layers)]

    def collect(self):
        self.wait()
        total = self.third[0]
        for k in range(1, self.pos.layers):
            total = total + self.third[k]
        self.out[self.pos.core, self.pos.slab] = total
        mine = self.out.at[self.pos.core, self.pos.slab]
        self.copies = [self.copy(mine, mine, 3, k - 1, self.pos.slab_at(k)[1]) for k in range(1, self.pos.slabs)]

    def share(self):
        self.wait()
        mine = self.out.at[self.pos.core]
        self.copies = [self.copy(mine, mine, 0, 1, self.pos.partner())]

    def finish(self):
        self.wait()


class Position:
    def __init__(self, slabs, layers):
        self.slabs, self.layers, self.members = slabs, layers, 2 * slabs
        brick = lax.axis_index("brick")
        self.brick = brick
        self.core, self.layer = lax.rem(brick, 2), lax.div(brick, 2)
        self.slab = lax.axis_index("slab")
        self.me = 2 * self.slab + self.core

    def member(self, k):
        to = lax.rem(self.me + k, self.members)
        return to, (lax.div(to, 2), 2 * self.layer + lax.rem(to, 2))

    def mate(self, k):
        if self.layers != 4:
            return lax.rem(self.layer + k, self.layers)
        if k == 1:
            return self.layer + 1 - 2 * lax.rem(self.layer, 2)
        return lax.rem(self.layer + 2, self.layers) if k == 2 else self.layers - 1 - self.layer

    def source(self, k):
        if k == 0:
            return self.layer
        return self.mate(k) if self.layers == 4 else lax.rem(self.layer + self.layers - k, self.layers)

    def across(self, k):
        return (self.slab, 2 * lax.rem(self.layer + k, self.layers) + self.core)

    def others(self):
        bricks = 2 * self.layers
        count = self.slabs * bricks
        at = self.slab * bricks + self.brick
        for k in range(1, count):
            to = lax.rem(at + k, count)
            yield k - 1, (lax.div(to, bricks), lax.rem(to, bricks))

    def partner(self):
        return (self.slab, 2 * self.layer + 1 - self.core)

    def slab_at(self, k):
        to = lax.rem(self.slab + k, self.slabs)
        return to, (to, self.brick)

    def slab_mate(self, k):
        if self.slabs != 4 or k == 0:
            return lax.rem(self.slab + k, self.slabs)
        if k == 1:
            return self.slabs - 1 - self.slab
        return self.slab + 1 - 2 * lax.rem(self.slab, 2) if k == 3 else lax.rem(self.slab + 2, self.slabs)

    def slab_source(self, k):
        return self.slab_mate(k) if self.slabs == 4 else lax.rem(self.slab + self.slabs - k, self.slabs)

    def brick_at(self, k):
        bricks = 2 * self.layers
        return (self.slab, lax.rem(self.brick + k + bricks, bricks))


def factor_steps(work, matrix, fillers=()):
    size = matrix.shape[0]
    block, panel = 8, 16
    row = lax.broadcasted_iota(jnp.int32, (size, size), 0)
    column = lax.broadcasted_iota(jnp.int32, (size, size), 1)
    work[:, :size] = matrix
    work[:, size:] = jnp.where(row == column, 1.0, 0.0)
    sub = lax.broadcasted_iota(jnp.int32, (block, size), 0)
    narrow, wide = (block, size), (block, 2 * size)
    fillers = list(fillers)
    for start in range(0, size, panel):
        if fillers:
            fillers.pop(0)()
        rows = [work[start : start + block, :], work[start + block : start + panel, :]]
        for b in range(2):
            at = start + b * block
            columns = {
                (r, m): jnp.broadcast_to(rows[r][:, at + m : at + m + 1], narrow)
                for r in range(b, 2)
                for m in range(block)
            }
            entry = {
                (i, m): jnp.broadcast_to(columns[b, m][i : i + 1], narrow) for m in range(block) for i in range(m, block)
            }
            scales = entry[0, 0]
            for k in range(block):
                scale = lax.rsqrt(entry[k, k])
                invert = scale * scale
                scales = scale if k == 0 else jnp.where(sub == k, scale, scales)
                ratios = {r: columns[r, k] * invert for r in range(b, 2)}
                ratios[b] = jnp.where(sub > k, ratios[b], 0.0)
                for m in range(k + 1, block):
                    factor = entry[m, k] * invert
                    for i in range(m, block):
                        entry[i, m] = entry[i, m] - entry[i, k] * factor
                for r in range(b, 2):
                    for m in range(k + 1, block):
                        columns[r, m] = columns[r, m] - ratios[r] * entry[m, k]
                pivot = jnp.broadcast_to(rows[b][k : k + 1], wide)
                for r in range(b, 2):
                    rows[r] = rows[r] - jnp.concatenate([ratios[r], ratios[r]], axis=1) * pivot
            rows[b] = rows[b] * jnp.concatenate([scales, scales], axis=1)
        both = jnp.concatenate(rows, axis=0)
        work[start : start + panel, :] = both
        if start + panel < size:
            high = both.astype(BF16).astype(F32)
            low = (both - high).astype(BF16).astype(F32)
            rest = both - high - low
            left = jnp.concatenate([item[:, :size] for item in (high, high, low, high, rest, low)], axis=0)
            right = jnp.concatenate([item.astype(BF16) for item in (high, low, high, rest, high, low)], axis=0)
            tall = left.T[start + panel :, :].astype(BF16)
            work[start + panel :, :] = work[start + panel :, :] - dot(tall, right)
    for filler in fillers:
        filler()
    factor = jnp.where(column <= row, work[:, :size].T, 0.0)
    inverse = jnp.where(column <= row, work[:, size:], 0.0)
    return factor, inverse


def step_kernel(names, slabs, layers, *refs):
    ref = dict(zip(names, refs))
    pos = Position(slabs, layers)
    core, slab, layer, brick, me = pos.core, pos.slab, pos.layer, pos.brick, pos.me
    members, bricks = pos.members, 2 * layers
    k_ref, v_ref = ref["k_here"], ref["v_here"]
    inputs = [
        pltpu.make_async_copy(ref["k"], k_ref, ref["insem"].at[0]),
        pltpu.make_async_copy(ref["v"], v_ref, ref["insem"].at[1]),
    ]
    for copy in inputs:
        copy.start()
    cells_x, cells_y, cells_z, rank = k_ref.shape
    own = cells_x * cells_y * cells_z
    nodes = v_ref.shape[0]
    lengths = (cells_x * slabs, cells_y * bricks, cells_z)
    cells = lengths[0] * lengths[1] * lengths[2]
    time_step = CFL / (VMAX * (lengths[0] + lengths[1] + lengths[2]))
    weight_x = 1.0 / cells
    weight_v = (2.0 * VMAX / NVX) ** 3
    base = (slab * bricks + brick) * nodes
    started = []

    def send(source, target, send_sem, recv_sem, device):
        copy = pltpu.make_async_remote_copy(
            src_ref=source,
            dst_ref=target,
            send_sem=send_sem,
            recv_sem=recv_sem,
            device_id=device,
            device_id_type=MESH,
        )
        copy.start()
        started.append(copy)
        return copy

    barrier = pltpu.get_barrier_semaphore()
    peers = [pos.member(k)[1] for k in range(1, members)] + [pos.across(k) for k in range(1, layers)]
    for peer in peers:
        pl.semaphore_signal(barrier, inc=1, device_id=peer, device_id_type=MESH)

    lane = lax.broadcasted_iota(jnp.int32, (8, nodes), 1)
    sub = lax.broadcasted_iota(jnp.int32, (8, nodes), 0)
    velocity = node_velocity(base + lane)
    square = velocity[0] * velocity[0] + velocity[1] * velocity[1] + velocity[2] * velocity[2]
    weights = jnp.where(sub == 0, 1.0, jnp.where(sub == 4, square, 0.0))
    upward = jnp.zeros_like(weights)
    for d in range(3):
        weights = jnp.where(sub == d + 1, velocity[d], weights)
        upward = jnp.where(sub == d + 5, jnp.maximum(velocity[d], 0.0), upward)
    for copy in inputs:
        copy.wait()
    values = v_ref[...]
    v_high, v_low = halves(values)
    v_rest = (values - v_high.astype(F32) - v_low.astype(F32)).astype(BF16)
    sums = dot(jnp.concatenate(halves(weights), axis=0), jnp.concatenate([v_high, v_low, v_rest], axis=1))
    sums = sums[:8] + sums[8:]
    squares = dot(upward.astype(BF16), jnp.concatenate(halves(values * values), axis=1))
    partial = sums[:, :rank] + (sums[:, rank : 2 * rank] + sums[:, 2 * rank :])
    partial = (partial + (squares[:, :rank] + squares[:, rank:])) * weight_v
    vec_l, vec_m = ref["vec_l"], ref["vec_m"]
    vec_l[layer] = partial

    turned_v = values.T
    vt_high, vt_low = halves(turned_v)
    vt = ref["vt"]
    vt[:rank] = vt_high
    vt[rank:] = vt_low
    v_both = jnp.concatenate([v_high, v_low], axis=1)
    row = lax.broadcasted_iota(jnp.int32, (rank, rank), 0)
    column = lax.broadcasted_iota(jnp.int32, (rank, rank), 1)
    packed = []

    def pack(d):
        sides = []
        for side in (jnp.maximum(velocity[d][:1], 0.0), jnp.minimum(velocity[d][:1], 0.0)):
            high, low = halves(turned_v * (side * weight_v))
            both = dot(high, v_both)
            sides.append(both[:, :rank] + (both[:, rank:] + dot(low, v_high)))
        packed.append(jnp.where(row > column, sides[0], sides[1]))

    for d in range(3):
        pack(d)
    ref["tx"][...] = jnp.concatenate(packed, axis=0).reshape(ref["tx"].shape)
    transport_sum = Sum(send, pos, ref, "t")
    pl.semaphore_wait(barrier, len(peers))
    mine = vec_l.at[layer]
    copies = [
        send(mine, mine, ref["vls"].at[k - 1], ref["vlr"].at[k - 1], pos.across(k)) for k in range(1, layers)
    ]
    transport_sum.start()
    transport_sum.scatter()
    for copy in copies:
        copy.wait_recv()
    total = vec_l[0]
    for k in range(1, layers):
        total = total + vec_l[k]
    vec_m[me] = total
    mine = vec_m.at[me]
    copies = [
        send(mine, mine, ref["vms"].at[k - 1], ref["vmr"].at[k - 1], pos.member(k)[1]) for k in range(1, members)
    ]
    transport_sum.cross()
    for copy in copies:
        copy.wait_recv()
    vectors = vec_m[0]
    for k in range(1, members):
        vectors = vectors + vec_m[k]

    own_k = k_ref[...].reshape(own, rank)
    kpad = ref["kpad"]
    kpad[...] = jnp.zeros_like(kpad)
    kpad[pl.ds(pl.multiple_of(core * own, 8), own), :] = own_k
    moments = lax.dot_general(
        vectors, kpad[...], (((1,), (1,)), ((), ())), precision=PRECISE, preferred_element_type=F32
    )
    pair = 2 * own
    density = jnp.maximum(moments[0:1], RHO_MIN)
    drift = [moments[d : d + 1] / density for d in range(1, 4)]
    bulk = drift[0] * drift[0] + drift[1] * drift[1] + drift[2] * drift[2]
    temper = jnp.maximum((moments[4:5] / density - bulk) / 3.0, TEMP_MIN)
    wide = 2.0 * math.pi * temper
    amplitude = density / (wide * jnp.sqrt(wide))
    state = jnp.zeros((8, pair), F32)
    sub_pair = lax.broadcasted_iota(jnp.int32, (8, pair), 0)
    lane_pair = lax.broadcasted_iota(jnp.int32, (8, pair), 1)
    for i, item in enumerate(drift + [-0.5 / temper, amplitude]):
        state = jnp.where(sub_pair == i, item, state)
    inside = (lane_pair >= core * own) & (lane_pair < (core + 1) * own)
    par = ref["par"]
    par[me, layer] = jnp.where(inside, state, 0.0)
    mine = par.at[me, layer, pl.ds(0, 5)]
    copies = [send(mine, mine, ref["ps"].at[i], ref["pr"].at[i], device) for i, device in pos.others()]
    halo_a, halo_b = ref["halo_a"], ref["halo_b"]
    halos = [
        send(k_ref.at[cells_x - 1], halo_a.at[0], ref["hs"].at[0], ref["hr"].at[0], pos.slab_at(1)[1]),
        send(k_ref.at[0], halo_a.at[1], ref["hs"].at[1], ref["hr"].at[1], pos.slab_at(slabs - 1)[1]),
        send(k_ref.at[:, cells_y - 1], halo_b.at[0], ref["hs"].at[2], ref["hr"].at[2], pos.brick_at(1)),
        send(k_ref.at[:, 0], halo_b.at[1], ref["hs"].at[3], ref["hr"].at[3], pos.brick_at(-1)),
    ]
    transport_sum.collect()
    for copy in copies:
        copy.wait_recv()

    mt_high, mt_low = ref["mt_high"], ref["mt_low"]
    mp, first, half, second, third = ref["mp"], ref["first"], ref["half"], ref["second"], ref["third"]
    group = math.gcd(nodes, NVX)
    groups = nodes // group
    width = 2 * pair
    slots = layers // 2
    fast_v = node_velocity(base + lax.broadcasted_iota(jnp.int32, (group, width), 0))
    slow_v = node_velocity(base + group * lax.broadcasted_iota(jnp.int32, (groups, width), 0))

    def build(to, slot, stage):
        blocks = [par[2 * to, 2 * slot + i] + par[2 * to + 1, 2 * slot + i] for i in range(2)]
        state = jnp.concatenate(blocks, axis=1)
        u = [state[d : d + 1] for d in range(3)]
        rate, scale = state[3:4], state[4:5]
        fast = jnp.exp((fast_v[2] - u[2]) ** 2 * rate)
        slow = jnp.exp(((slow_v[0] - u[0]) ** 2 + (slow_v[1] - u[1]) ** 2) * rate) * scale
        places = [pl.ds(pl.multiple_of(((2 * slot + i) * slabs + to) * pair, pair), pair) for i in range(2)]
        for t in range(groups):
            high, low = halves(fast * slow[t : t + 1])
            span = slice(t * group, (t + 1) * group)
            stage[0][span, :] = high
            stage[1][span, :] = low
            for i, place in enumerate(places):
                mt_high[span, place] = high[:, i * pair : (i + 1) * pair]
                mt_low[span, place] = low[:, i * pair : (i + 1) * pair]

    def multiply(to, slot, stage):
        high = dot(vt[...], stage[0][...])
        low = dot(vt[:rank], stage[1][...])
        result = ((high[:rank] + (high[rank:] + low)) * weight_v).T
        for i in range(2):
            for c in range(2):
                at = (2 * i + c) * own
                mp[to, 2 * slot + i, c] = result[at : at + own]

    def hand_over(k, slot, to):
        at = pl.ds(2 * slot, 2)
        return send(
            mp.at[to, at, 1 - core], first.at[to, at], ref["cs"].at[k, slot], ref["cr"].at[k, slot], pos.partner()
        )

    over = []

    def hand_on(k, slot, to, copy):
        copy.wait_recv()
        at = pl.ds(2 * slot, 2)
        if k == 0:
            second[slab, at] = mp[slab, at, core] + first[slab, at]
            return
        half[to, at] = mp[to, at, core] + first[to, at]
        over.append(
            send(half.at[to, at], second.at[slab, at], ref["ss"].at[k - 1, slot], ref["sr"].at[k - 1, slot], (to, brick))
        )

    waiting = []
    steps = [(k, pos.slab_mate(k), slot) for k in list(range(1, slabs)) + [0] for slot in range(slots)]
    stages = [(ref["stage_h0"], ref["stage_l0"]), (ref["stage_h1"], ref["stage_l1"])]
    build(*steps[0][1:], stages[0])
    for i, (k, to, slot) in enumerate(steps):
        multiply(to, slot, stages[i % 2])
        if i + 1 < len(steps):
            build(*steps[i + 1][1:], stages[(i + 1) % 2])
        copy = hand_over(k, slot, to)
        if i == 0:
            transport_sum.share()
        if len(waiting) >= 2:
            hand_on(*waiting.pop(0))
        waiting.append((k, slot, to, copy))

    for copy in waiting:
        hand_on(*copy)

    transport_sum.finish()
    packed = ref["to"][...].reshape(3 * rank, rank)
    trans = ref["trans"]
    for d in range(3):
        block = packed[d * rank : (d + 1) * rank]
        flipped = block.T
        diagonal = jnp.where(row == column, vectors[d + 5 : d + 6], 0.0)
        trans[d * rank : (d + 1) * rank] = jnp.where(row <= column, block, flipped)
        trans[(d + 3) * rank : (d + 4) * rank] = jnp.where(
            row > column, block, jnp.where(row < column, flipped, diagonal)
        )
    for copy in halos:
        copy.wait_recv()
    field = k_ref[...]
    after_a = jnp.concatenate([field[1:], halo_a[1:2]], axis=0)
    before_a = jnp.concatenate([halo_a[0:1], field[:-1]], axis=0)
    after_b = jnp.concatenate([field[:, 1:], halo_b[1].reshape(cells_x, 1, cells_z, rank)], axis=1)
    before_b = jnp.concatenate([halo_b[0].reshape(cells_x, 1, cells_z, rank), field[:, :-1]], axis=1)

    def next_third(flat):
        count = flat.shape[0]
        index = lax.broadcasted_iota(jnp.int32, flat.shape, 0)
        return jnp.where(
            lax.rem(index, cells_z) == cells_z - 1,
            pltpu.roll(flat, cells_z - 1, 0),
            pltpu.roll(flat, count - 1, 0),
        )

    def last_third(flat):
        count = flat.shape[0]
        index = lax.broadcasted_iota(jnp.int32, flat.shape, 0)
        return jnp.where(
            lax.rem(index, cells_z) == 0,
            pltpu.roll(flat, count - cells_z + 1, 0),
            pltpu.roll(flat, 1, 0),
        )

    fields = [
        (after_a.reshape(own, rank) - own_k) * lengths[0],
        (after_b.reshape(own, rank) - own_k) * lengths[1],
        (next_third(own_k) - own_k) * lengths[2],
        (own_k - before_a.reshape(own, rank)) * lengths[0],
        (own_k - before_b.reshape(own, rank)) * lengths[1],
        (own_k - last_third(own_k)) * lengths[2],
    ]
    flux = dot3(jnp.concatenate(fields, axis=1), trans[...])
    kept = own_k - time_step * flux - COLLIDE * own_k

    for copy in over:
        copy.wait_recv()
    total = second[0]
    for k in range(1, slabs):
        total = total + second[k]
    quarter = ref["quarter"]
    quarter[...] = total
    copies = []
    for k in range(1, layers):
        to = lax.rem(layer + k, layers)
        copies.append(
            send(quarter.at[to], third.at[layer], ref["zs"].at[k - 1], ref["zr"].at[k - 1], pos.across(k))
        )
    third[layer] = quarter[layer]
    for copy in copies:
        copy.wait_recv()
    mproj = third[0]
    for k in range(1, layers):
        mproj = mproj + third[k]
    advanced = kept + COLLIDE * mproj

    adv = ref["adv"]
    adv[layer, slab, core] = advanced.reshape(cells_x, cells_y, cells_z, rank)
    here = adv.at[layer, slab, core]

    def to_slabs(block, j):
        return [
            send(block, block, ref["bs"].at[k - 1, j], ref["br"].at[k - 1, j], (pos.slab_mate(k), brick))
            for k in range(1, slabs)
        ]

    along = [
        send(here, here, ref["as"].at[k - 1], ref["ar"].at[k - 1], (slab, 2 * pos.mate(k) + core))
        for k in range(1, layers)
    ]
    crossing = [to_slabs(here, 0)]
    last = [[send(here, here, ref["ds"].at[0, 0], ref["dr"].at[0, 0], pos.partner())]]
    raw_sum = Sum(send, pos, ref, "r")
    ref["rx"][...] = dot3(advanced.T, mproj).reshape(ref["rx"].shape)
    raw_sum.start()
    raw_sum.scatter()
    for j in range(1, layers):
        along[j - 1].wait_recv()
        block = adv.at[pos.source(j), slab, core]
        crossing.append(to_slabs(block, j))
        last.append([send(block, block, ref["ds"].at[0, j], ref["dr"].at[0, j], pos.partner())])

    at, ahl, back = ref["at"], ref["ahl"], ref["back"]
    d_high, d_low, gram_l = ref["d_high"], ref["d_low"], ref["gram_l"]
    plane = cells // layers

    def relay(j):
        for k in range(1, slabs):
            crossing[j][k - 1].wait_recv()
            block = adv.at[pos.source(j), pos.slab_source(k), core]
            last[j].append(send(block, block, ref["ds"].at[k, j], ref["dr"].at[k, j], pos.partner()))

    def store_slopes(span, d, values):
        high, low = halves(values)
        d_high[span, d * rank : (d + 1) * rank] = high
        d_low[span, d * rank : (d + 1) * rank] = low

    def take(j):
        for copy in last[j]:
            copy.wait_recv()
        from_layer = pos.source(j)
        block = adv[from_layer]
        span = pl.ds(pl.multiple_of(from_layer * plane, plane), plane)
        flat = block.reshape(plane, rank)
        high, low = halves(flat)
        ahl[span, :rank] = high
        ahl[span, rank:] = low
        high_t, low_t = halves(flat.T)
        at[:rank, span] = high_t
        at[rank:, span] = low_t
        gram_l[from_layer] = dot(high_t, jnp.concatenate([high, low], axis=1))
        across = jnp.concatenate([block[1:, :, :1], block[:1, :, :1]], axis=0)
        after = jnp.concatenate([block[:, :, 1:], across], axis=2)
        store_slopes(span, 0, after.reshape(plane, rank) - flat)
        store_slopes(span, 2, next_third(flat) - flat)

    def project_back(j, rows):
        span = pl.ds(pl.multiple_of(pos.source(j) * plane, plane), plane)
        top = dot(mt_high[rows, span], ahl[span, :])
        part = top[:, :rank] + (top[:, rank:] + dot(mt_low[rows, span], ahl[span, :rank]))
        back[rows, :] = part if j == 0 else back[rows, :] + part

    quarters = [slice(i * (nodes // 4), (i + 1) * (nodes // 4)) for i in range(4)]
    for j in range(layers):
        relay(j)
        if j == 1:
            raw_sum.cross()
        if j > 0:
            take(j - 1)
            for rows in quarters if j < layers - 1 else ():
                project_back(j - 1, rows)
    raw_sum.collect()
    take(layers - 1)
    total = gram_l[0]
    for k in range(1, layers):
        total = total + gram_l[k]
    mixed = total[:, rank:]
    gram = (total[:, :rank] + (mixed + mixed.T)) * weight_x
    for k in range(layers):
        block, following = adv[k], adv[(k + 1) % layers]
        ups = [
            jnp.concatenate([block[:, 0, :, 1:], block[:, 1, :, :1]], axis=2),
            jnp.concatenate([block[:, 1, :, 1:], following[:, 0, :, :1]], axis=2),
        ]
        for c in range(2):
            difference = (ups[c] - block[:, c]).reshape(slabs, own, rank)
            for i in range(slabs):
                first_row = k * plane + (2 * i + c) * own
                store_slopes(slice(first_row, first_row + own), 1, difference[i])
    slopes = [None] * 3

    def slope_product(d):
        columns = slice(d * rank, (d + 1) * rank)
        both = dot(at[...], d_high[:, columns])
        both = both[:rank] + (both[rank:] + dot(at[:rank], d_low[:, columns]))
        slopes[d] = both * (lengths[d] * weight_x)

    sources = []

    def drive():
        sources.append(
            time_step * dot6(jnp.concatenate(slopes + [-item.T for item in slopes], axis=1), trans[...])
        )

    def finish_back(rows):
        project_back(layers - 2, rows)
        project_back(layers - 1, rows)

    back_last = [functools.partial(finish_back, rows) for rows in quarters]
    fillers = [functools.partial(slope_product, d) for d in (0, 2, 1)] + [drive]
    fillers += [back_last[0], lambda: (raw_sum.share(), back_last[1]()), back_last[2]]
    fillers += [lambda: (raw_sum.finish(), back_last[3]())]
    factor, inverse = factor_steps(ref["work"], gram, fillers)
    source = sources[0] - COLLIDE * weight_x * ref["ro"][...].reshape(rank, rank)

    turned = inverse.T
    middle = (1.0 + COLLIDE) * factor + dot6(source.T, turned)
    moved = dot6(inverse, jnp.concatenate(slopes, axis=1))
    plus = dot6(jnp.concatenate([moved[:, d * rank : (d + 1) * rank] for d in range(3)], axis=0), turned)
    plus = [plus[d * rank : (d + 1) * rank] for d in range(3)]
    lnew = ref["lnew"]
    chunk = math.gcd(nodes, NVX * NVX // 4)
    gram_v = jnp.zeros((rank, rank), F32)
    mixed_v = jnp.zeros((rank, rank), F32)
    behind = [-item.T for item in plus]
    for at_row in range(0, nodes, chunk):
        span = slice(at_row, at_row + chunk)
        node = base + at_row
        lnow = dot3(v_ref[span, :], middle)
        ahead = [node // (NVX * NVX) >= NVX // 2, node // NVX % NVX >= NVX // 2]
        sides = [jnp.where(ahead[d], plus[d], behind[d]) for d in range(2)] + [plus[2], behind[2]]
        sliding = dot3(lnow, jnp.concatenate(sides, axis=1))
        part = node_velocity(node + lax.broadcasted_iota(jnp.int32, (chunk, rank), 0))
        slide = part[0] * sliding[:, :rank] + part[1] * sliding[:, rank : 2 * rank]
        slide = slide + part[2] * jnp.where(part[2] > 0, sliding[:, 2 * rank : 3 * rank], sliding[:, 3 * rank :])
        mback = dot3(back[span, :] * weight_x, turned)
        new = lnow + time_step * slide + COLLIDE * (mback - lnow)
        lnew[span, :] = new
        high, low = halves(new)
        rest = (new - high.astype(F32) - low.astype(F32)).astype(BF16)
        high_t, low_t = halves(new.T)
        both = dot(high_t, jnp.concatenate([high, low, rest], axis=1))
        gram_v = gram_v + both[:, :rank]
        mixed_v = mixed_v + (both[:, rank : 2 * rank] + (both[:, 2 * rank :] + 0.5 * dot(low_t, low)))
    gram_v = (gram_v + (mixed_v + mixed_v.T)) * weight_v

    half_rank = rank // 2
    lanes = lax.broadcasted_iota(jnp.int32, (half_rank // 2, rank), 1)
    corner = jnp.where(
        lanes < half_rank,
        pltpu.roll(gram_v[half_rank : half_rank + half_rank // 2], half_rank, 1),
        gram_v[half_rank + half_rank // 2 :],
    )
    gx, g1, g2, g3, go = ref["gx"], ref["g1"], ref["g2"], ref["g3"], ref["go"]
    gx[...] = jnp.concatenate([gram_v[:half_rank], corner], axis=0).reshape(gx.shape)
    copy = send(gx.at[1 - core], g1, ref["gcs"].at[0], ref["gcr"].at[0], pos.partner())
    copy.wait_recv()
    g2[slab] = gx[core] + g1[...]
    mine = g2.at[slab]
    copies = [
        send(mine, mine, ref["gss"].at[k - 1], ref["gsr"].at[k - 1], (pos.slab_mate(k), brick)) for k in range(1, slabs)
    ]
    ref["basis_x"][...] = dot3(advanced, turned)
    sent = len(started) - len(copies)
    for copy in started[:sent]:
        copy.wait_send()
    for copy in copies:
        copy.wait_recv()
    total = g2[0]
    for k in range(1, slabs):
        total = total + g2[k]
    g3[layer] = total
    mine = g3.at[layer]
    copies = [
        send(mine, mine, ref["gls"].at[k - 1], ref["glr"].at[k - 1], pos.across(k)) for k in range(1, layers)
    ]
    for copy in copies:
        copy.wait_recv()
    total = g3[0]
    for k in range(1, layers):
        total = total + g3[k]
    go[core] = total
    mine = go.at[core]
    send(mine, mine, ref["gcs"].at[1], ref["gcr"].at[1], pos.partner()).wait_recv()
    whole = go[...].reshape(half_rank + half_rank // 2, rank)
    corner = whole[half_rank:]
    gram_ref = ref["gram"]
    gram_ref[:half_rank] = whole[:half_rank]
    gram_ref[half_rank : half_rank + half_rank // 2] = pltpu.roll(corner, half_rank, 1)
    gram_ref[half_rank + half_rank // 2 :] = corner
    for copy in started[sent:]:
        copy.wait_send()


def finish_kernel(gram, lnew, field, basis_x, coupling, basis_v, work, factor_buffer, out, sems):
    give = pltpu.make_async_copy(field, basis_x, sems.at[0])
    give.start()
    factor, inverse = factor_steps(work, gram[...])
    factor_buffer[...] = factor
    copies = [give, pltpu.make_async_copy(factor_buffer, coupling, sems.at[1])]
    copies[1].start()
    turned = inverse.T
    nodes = lnew.shape[0]
    count = sems.shape[0] - 2
    chunk = nodes // count
    for i in range(count):
        span = pl.ds(i * chunk, chunk)
        out[span, :] = dot3(lnew[span, :], turned)
        copies.append(pltpu.make_async_copy(out.at[span], basis_v.at[span], sems.at[2 + i]))
        copies[-1].start()
    for copy in copies:
        copy.wait()


def local(k_coeffs, v_basis):
    cells_x, cells_y, cells_z, rank = k_coeffs.shape
    slabs = lax.axis_size("slab")
    layers = lax.axis_size("brick") // 2
    members = 2 * slabs
    own = cells_x * cells_y * cells_z
    nodes = v_basis.shape[0]
    cells = own * members * layers
    share = 3 * rank // members
    part = rank // members
    pair = 2 * own
    devices = members * layers
    names = ["k", "v", "basis_x", "gram", "lnew"]
    scratch = []

    used = [0]

    def buffer(name, shape, dtype=F32):
        names.append(name)
        used[0] += math.prod(shape) * jnp.dtype(dtype).itemsize
        scratch.append(pltpu.VMEM(shape, dtype))

    def semaphores(name, *shape):
        names.append(name)
        scratch.append(pltpu.SemaphoreType.DMA(shape))

    def reduction(name, rows):
        buffer(name + "x", (2, slabs, rows, rank))
        buffer(name + "1", (slabs, rows, rank))
        buffer(name + "h", (slabs, rows, rank))
        buffer(name + "2", (slabs, rows, rank))
        buffer(name + "3", (layers, rows, rank))
        buffer(name + "o", (2, slabs, rows, rank))
        for stage, count in (("c", 2), ("s", slabs - 1), ("l", layers - 1), ("g", slabs - 1)):
            semaphores(name + stage + "s", count)
            semaphores(name + stage + "r", count)

    buffer("k_here", k_coeffs.shape)
    buffer("v_here", v_basis.shape)
    semaphores("insem", 2)
    buffer("vec_l", (layers, 8, rank))
    buffer("vec_m", (members, 8, rank))
    buffer("halo_a", (2, cells_y, cells_z, rank))
    buffer("halo_b", (2, cells_x, cells_z, rank))
    buffer("vt", (2 * rank, nodes), BF16)
    buffer("kpad", (pair, rank))
    buffer("par", (members, layers, 8, pair))
    buffer("mt_high", (nodes, cells), BF16)
    buffer("mt_low", (nodes, cells), BF16)
    for name in ("stage_h0", "stage_l0", "stage_h1", "stage_l1"):
        buffer(name, (nodes, 2 * pair), BF16)
    buffer("mp", (slabs, layers, 2, own, rank))
    buffer("first", (slabs, layers, own, rank))
    buffer("half", (slabs, layers, own, rank))
    buffer("second", (slabs, layers, own, rank))
    buffer("quarter", (layers, own, rank))
    buffer("third", (layers, own, rank))
    buffer("trans", (6 * rank, rank))
    buffer("adv", (layers, slabs, 2, cells_x, cells_y, cells_z, rank))
    buffer("back", (nodes, rank))
    buffer("gram_l", (layers, rank, 2 * rank))
    buffer("at", (2 * rank, cells), BF16)
    buffer("ahl", (cells, 2 * rank), BF16)
    buffer("d_high", (cells, 3 * rank), BF16)
    buffer("d_low", (cells, 3 * rank), BF16)
    buffer("work", (rank, 2 * rank))
    reduction("t", share)
    reduction("r", part)
    packed = 3 * rank // 8
    buffer("gx", (2, packed, rank))
    buffer("g1", (packed, rank))
    buffer("g2", (slabs, packed, rank))
    buffer("g3", (layers, packed, rank))
    buffer("go", (2, packed, rank))
    for name, count in (("gc", 2), ("gs", slabs - 1), ("vl", layers - 1), ("vm", members - 1), ("p", devices - 1)):
        semaphores(name + "s", count)
        semaphores(name + "r", count)
    for name in ("gl", "z", "a"):
        semaphores(name + "s", layers - 1)
        semaphores(name + "r", layers - 1)
    semaphores("hs", 4)
    semaphores("hr", 4)
    for name, shape in (
        ("c", (slabs, layers // 2)),
        ("s", (slabs - 1, layers // 2)),
        ("b", (slabs - 1, layers)),
        ("d", (slabs, layers)),
    ):
        semaphores(name + "s", *shape)
        semaphores(name + "r", *shape)
    basis_x, gram, lnew = pl.pallas_call(
        functools.partial(step_kernel, tuple(names), slabs, layers),
        out_shape=(
            jax.ShapeDtypeStruct((own, rank), F32),
            jax.ShapeDtypeStruct((rank, rank), F32),
            jax.ShapeDtypeStruct(v_basis.shape, F32),
        ),
        in_specs=[HBM, HBM],
        out_specs=(VM, VM, VM),
        scratch_shapes=scratch,
        compiler_params=pltpu.CompilerParams(
            collective_id=1, has_side_effects=True, vmem_limit_bytes=min(62 * 2**20, used[0] + 14 * 2**20)
        ),
    )(pltpu.with_memory_space_constraint(k_coeffs, pltpu.HBM), pltpu.with_memory_space_constraint(v_basis, pltpu.HBM))
    chunks = 4
    basis_x, coupling, basis_v = pl.pallas_call(
        finish_kernel,
        out_shape=(
            jax.ShapeDtypeStruct((own, rank), F32),
            jax.ShapeDtypeStruct((rank, rank), F32),
            jax.ShapeDtypeStruct(v_basis.shape, F32),
        ),
        in_specs=[VM, VM, VM],
        out_specs=(HBM, HBM, HBM),
        scratch_shapes=[
            pltpu.VMEM((rank, 2 * rank), F32),
            pltpu.VMEM((rank, rank), F32),
            pltpu.VMEM(v_basis.shape, F32),
            pltpu.SemaphoreType.DMA((2 + chunks,)),
        ],
        compiler_params=pltpu.CompilerParams(vmem_limit_bytes=12 * 2**20),
    )(gram, lnew, basis_x)
    return basis_x.reshape(k_coeffs.shape), coupling, basis_v


def solution(mesh):
    return jax.shard_map(
        local,
        mesh=mesh,
        in_specs=(P("slab", "brick", None, None), P(("slab", "brick"), None)),
        out_specs=(P("slab", "brick", None, None), P(), P(("slab", "brick"), None)),
        check_vma=False,
    )
```
